256 devices in a mesh: grp: 2 (over core), seq: 32 (over z, x), head: 4 (over y).
Axes of the slice: x: 4, y: 4, z: 8, core: 2. Of those that a mesh axis runs over, the one named last changes fastest.
Arguments:
- queries: bfloat16 [6144, 64, 128], P('seq', ('grp', 'head')), may hold values from -6 to 6
- keys: bfloat16 [6144, 64, 128], P('seq', ('grp', 'head')), may hold values from -6 to 6
- values: bfloat16 [6144, 64, 128], P('seq', ('grp', 'head')), may hold values from -6 to 6
- documents: int32 [6144], P('seq'), may hold values from 0 to 3, never falling along the last dimension, each value on 1 to 4608 neighbouring positions
- feature_map: float32 [64, 128, 128], P(('grp', 'head')), may hold values from -8 to 8
Outputs:
- teacher_out: bfloat16 [6144, 64, 128], P('seq', ('grp', 'head'))
- student_out: bfloat16 [6144, 64, 128], P('seq', ('grp', 'head'))
- loss: float32 [], replicated
- feature_grad: float32 [64, 128, 128], P(('grp', 'head'))
The draws below stay inside these ranges and needn't reach their ends.
All inputs are finite; a program needn't handle non-finite values.
Results may differ from the reference program's by a relative error of at most 0.006.
Values may be sent and summed in bfloat16 or wider, within the bound.
A program may use at most 192 MiB of HBM per device.

```python
import math
import jax
import jax.numpy as jnp
import numpy as np
from jax import lax

HEADS = 64
HEAD_DIM = 128
FEAT = 128
WINDOW = 64
DOCS = 4
TOKENS = 6144
DOC_MOST = 4608


def paired_draw(key):
    base_key = jax.random.fold_in(key, 17)
    first_key, second_key = jax.random.split(base_key)
    shape = (TOKENS, HEADS, HEAD_DIM)
    query_base = jnp.clip(jax.random.normal(first_key, shape, jnp.float32), -4.0, 4.0)
    key_base = jnp.clip(jax.random.normal(second_key, shape, jnp.float32), -4.0, 4.0)
    return (query_base, key_base)


def draw_queries(key, part):
    query_base, key_base = paired_draw(key)
    return query_base.astype(jnp.bfloat16)


def draw_keys(key, part):
    query_base, key_base = paired_draw(key)
    return key_base.astype(jnp.bfloat16)


def draw_values(key, part):
    base_key = jax.random.fold_in(key, 29)
    noise_key, amp_key, freq_key, phase_key = jax.random.split(base_key, 4)
    shape = (TOKENS, HEADS, HEAD_DIM)
    amplitude = jnp.exp(jax.random.uniform(amp_key, (HEADS, HEAD_DIM), jnp.float32, math.log(0.5), math.log(1.5)))
    frequency = jax.random.uniform(freq_key, (HEADS, HEAD_DIM), jnp.float32, 0.5, 3.0)
    phase = jax.random.uniform(phase_key, (HEADS, HEAD_DIM), jnp.float32, 0.0, 2.0 * math.pi)
    position = jnp.arange(TOKENS).astype(jnp.float32)[:, None, None] / TOKENS
    wave = jnp.cos(2.0 * math.pi * frequency[None] * position + phase[None])
    noise = jnp.clip(jax.random.normal(noise_key, shape, jnp.float32), -4.0, 4.0)
    drawn = noise + amplitude[None] * wave
    return drawn.astype(jnp.bfloat16)


def draw_feature_map(key, part):
    base_key = jax.random.fold_in(key, 41)
    main_key = jax.random.fold_in(base_key, 0)
    shape = (HEADS, HEAD_DIM, FEAT)
    normal_part = jnp.clip(jax.random.normal(main_key, shape, jnp.float32), -4.0, 4.0)
    drawn = normal_part * HEAD_DIM ** (-0.5)
    return drawn


def profile(amount, total, bound, lean):
    loads = [(1 << 20) // math.isqrt(standing ** lean) + 1 for standing in range(2, amount + 1)]
    surplus, counts = total - bound - (amount - 1), [1] * (amount - 1)
    while surplus > 0:
        free = [i for i in range(amount - 1) if counts[i] < bound]
        whole, remaining = sum([loads[i] for i in free]), surplus
        for i in free:
            more = min(bound - counts[i], max(1, remaining * loads[i] // whole), surplus)
            counts[i] = counts[i] + more
            surplus = surplus - more
    return np.array([bound] + counts)


def ragged_sizes(own_key, number_of, total, limit, skew):
    if number_of == 2:
        one = jax.random.randint(own_key, (), max(1, total - limit), min(limit, total - 1) + 1)
        return jnp.stack([one, total - one])
    tallies = jnp.asarray(profile(number_of, total, limit, skew), jnp.int32)
    pairs = (number_of - 1) // 2
    donor, receiver = tallies[1:1 + 2 * pairs:2], tallies[2:2 + 2 * pairs:2]
    room = jnp.minimum(donor - 1, limit - receiver)
    moved = jax.random.randint(jax.random.fold_in(own_key, 1), (pairs,), 0, 1 << 20) % (room + 1)
    tallies = tallies.at[1:1 + 2 * pairs:2].set(donor - moved).at[2:2 + 2 * pairs:2].set(receiver + moved)
    return tallies[jax.random.permutation(jax.random.fold_in(own_key, 2), number_of)]


def setup_inputs(seed: int = 0) -> dict:
    key_of = jax.random.split(jax.random.key(seed), 6)
    return {
        "queries": draw_queries(jax.random.fold_in(key_of[5], 71), 0),
        "keys": draw_keys(jax.random.fold_in(key_of[5], 71), 0),
        "values": draw_values(jax.random.fold_in(key_of[5], 71), 0),
        "documents": jnp.searchsorted(jnp.cumsum(ragged_sizes(key_of[3], DOCS, TOKENS, DOC_MOST, 1)), jnp.arange(TOKENS), side="right").astype(jnp.int32),
        "feature_map": draw_feature_map(jax.random.fold_in(key_of[5], 71), 0),
    }


exact_mode = lax.Precision.HIGHEST
masked_value = -1e+30

def features(inputs, weights):
    logits = jnp.einsum('rhd,hdf->rhf', inputs, weights, precision=exact_mode)
    return jnp.concatenate([jax.nn.softmax(logits, axis=-1), jax.nn.softmax(-logits, axis=-1)], axis=-1)

def join_up(earlier, later):
    merged_tag = jnp.maximum(earlier[0], later[0])
    early_keep = (earlier[0] == merged_tag).astype(earlier[1].dtype)
    late_keep = (later[0] == merged_tag).astype(later[1].dtype)
    return (merged_tag, early_keep * earlier[1] + late_keep * later[1], early_keep * earlier[2] + late_keep * later[2])

def teacher(queries, keys, values, documents):
    position = jnp.arange(TOKENS)
    allowed = (position[None, :] <= position[:, None]) & (documents[None, :] == documents[:, None])
    score_scale = HEAD_DIM ** (-0.5)

    def one_head(operands):
        head_query, head_key, head_value = operands
        scores = jnp.dot(head_query.astype(jnp.float32), head_key.astype(jnp.float32).T, precision=exact_mode) * score_scale
        scores = jnp.where(allowed, scores, masked_value)
        row_max = lax.optimization_barrier(jnp.max(scores, axis=1, keepdims=True))
        probabilities = jnp.where(allowed, jnp.exp(scores - row_max), 0.0)
        totals = lax.optimization_barrier(jnp.sum(probabilities, axis=1, keepdims=True))
        rounded = lax.optimization_barrier(probabilities.astype(jnp.bfloat16)).astype(jnp.float32)
        numerator = jnp.dot(rounded, head_value.astype(jnp.float32), precision=exact_mode)
        return (numerator / totals).astype(jnp.bfloat16)
    per_head = lax.map(one_head, (jnp.swapaxes(queries, 0, 1), jnp.swapaxes(keys, 0, 1), jnp.swapaxes(values, 0, 1)))
    return jnp.swapaxes(per_head, 0, 1)

def student(queries, keys, values, documents, weights):
    half_feat = FEAT // 2
    score_scale = HEAD_DIM ** (-0.5)
    query_float = queries.astype(jnp.float32)
    key_float = keys.astype(jnp.float32)
    value_float = values.astype(jnp.float32)
    query_feat = features(query_float, weights[:, :, :half_feat])
    key_feat = features(key_float, weights[:, :, half_feat:])
    block_count = TOKENS // WINDOW
    doc_float = documents.astype(jnp.float32)

    def padded(array, filler):
        front = jnp.full((WINDOW,) + array.shape[1:], filler, array.dtype)
        return jnp.concatenate([front, array], axis=0).reshape((block_count + 1, WINDOW) + array.shape[1:])

    def paired(blocks):
        return jnp.concatenate([blocks[:-1], blocks[1:]], axis=1)
    key_blocks = padded(key_float, 0.0)
    value_blocks = padded(value_float, 0.0)
    feat_blocks = padded(key_feat, 0.0)
    doc_blocks = padded(doc_float, -1.0)
    inputs_all = (query_float.reshape(block_count, WINDOW, HEADS, HEAD_DIM), query_feat.reshape(block_count, WINDOW, HEADS, FEAT), doc_float.reshape(block_count, WINDOW), paired(key_blocks), paired(value_blocks), paired(feat_blocks), paired(doc_blocks), value_blocks[:-1], feat_blocks[:-1], doc_blocks[:-1])
    distance = jnp.arange(WINDOW)[:, None] + WINDOW - jnp.arange(2 * WINDOW)[None, :]
    in_window = (distance >= 0) & (distance < WINDOW)
    beyond = distance >= WINDOW

    def block_step(carried, block_inputs):
        tag_in, state_in, norm_in = carried
        block_query, block_qfeat, block_docs, near_keys, near_values, near_feat, near_docs, elem_values, elem_feat, elem_docs = block_inputs
        same_doc = block_docs[:, None] == near_docs[None, :]
        scores = jnp.einsum('ihd,jhd->hij', block_query, near_keys, precision=exact_mode) * score_scale
        window_mask = (in_window & same_doc)[None]
        row_max = lax.optimization_barrier(jnp.max(jnp.where(window_mask, scores, masked_value), axis=-1, keepdims=True))
        window_weight = jnp.where(window_mask, jnp.exp(scores - row_max), 0.0)
        linear_weight = jnp.where((beyond & same_doc)[None], jnp.einsum('ihf,jhf->hij', block_qfeat, near_feat, precision=exact_mode), 0.0)
        weight = window_weight + linear_weight
        uses_state = (block_docs == tag_in).astype(jnp.float32)[:, None]
        numer_sum = jnp.einsum('hij,jhd->ihd', weight, near_values, precision=exact_mode)
        numer_sum = numer_sum + uses_state[:, :, None] * jnp.einsum('ihf,hfd->ihd', block_qfeat, state_in, precision=exact_mode)
        denominator = lax.optimization_barrier(jnp.sum(weight, axis=-1)).T + uses_state * jnp.einsum('ihf,hf->ih', block_qfeat, norm_in, precision=exact_mode)
        output = numer_sum / denominator[:, :, None]
        elem_tag = elem_docs[-1]
        in_tail = (elem_docs == elem_tag).astype(jnp.float32)
        masked_feat = elem_feat * in_tail[:, None, None]
        elem_state = jnp.einsum('jhf,jhd->hfd', masked_feat, elem_values, precision=exact_mode)
        elem_norm = lax.optimization_barrier(jnp.sum(masked_feat, axis=0))
        return (join_up(carried, (elem_tag, elem_state, elem_norm)), output)
    start_carry = (jnp.float32(-2.0), jnp.zeros((HEADS, FEAT, HEAD_DIM), jnp.float32), jnp.zeros((HEADS, FEAT), jnp.float32))
    final_carry, outputs = lax.scan(block_step, start_carry, inputs_all)
    return outputs.reshape(TOKENS, HEADS, HEAD_DIM)

def reference(queries, keys, values, documents, feature_map):
    teacher_out = teacher(queries, keys, values, documents)
    target = teacher_out.astype(jnp.float32)

    def objective(weights):
        output = student(queries, keys, values, documents, weights)
        loss_total = jnp.sum(jnp.square(output - target)) / (TOKENS * HEADS)
        return (loss_total, output)
    (loss_total, output), feature_grad = jax.value_and_grad(objective, has_aux=True)(feature_map)
    return (teacher_out, output.astype(jnp.bfloat16), loss_total, feature_grad)
```

```python
import functools
import math

import jax
import jax.numpy as jnp
from jax import lax
from jax.experimental import pallas as pl
from jax.experimental.pallas import tpu as pltpu
from jax.sharding import Mesh
from jax.sharding import PartitionSpec as P

SEQ = ("seq_0", "seq_1")
MESH = pl.DeviceIdType.MESH

TOKENS=6144; BLK=192; NB=8; WINDOW=64; LOC=384; GRP=768; TK=512
F32=jnp.float32; BF=jnp.bfloat16
NEG=-1e30

def mm(a,b,ca=1,cb=0):
    return lax.dot_general(a,b,(((ca,),(cb,)),((),())),preferred_element_type=F32)

def hilo(a):
    hi=a.astype(BF)
    return hi,(a-hi.astype(F32)).astype(BF)

def local_start(b):
    s=((192*b-64)//128)*128
    return jnp.clip(s,0,TOKENS-LOC)

def compute_kernel(norm, st_ref, q_ref, k_ref, v_ref, w_ref, t_ref, y_ref, dw_ref, loss_ref,
                   vx, pkT, dpT, st_s, ds_s, pq_s, dwq_s):
    st1,st2,st3,xi = st_ref[0],st_ref[1],st_ref[2],st_ref[3]
    def dstart(i):
        return jnp.where(i>=st3,st3,jnp.where(i>=st2,st2,jnp.where(i>=st1,st1,0)))
    scale=128**-0.5
    c2=scale*math.log2(math.e)
    w=w_ref[...]
    half=64
    wq=jnp.concatenate([w[:,:half],-w[:,:half]],axis=1)
    wk=jnp.concatenate([w[:,half:],-w[:,half:]],axis=1)
    wqh,wql=hilo(wq)
    wq2=jnp.concatenate([wqh,wql],axis=1)
    wkh,wkl=hilo(wk.T)

    def kfeat(c,_):
        o=pl.multiple_of(c*GRP,GRP)
        kk=k_ref[pl.ds(o,GRP),:]
        vx[pl.ds(o,GRP),:128]=v_ref[pl.ds(o,GRP),:]
        vx[pl.ds(o,GRP),128:]=jnp.ones((GRP,128),BF)
        l=mm(wkh,kk,1,1)+mm(wkl,kk,1,1)
        for h in (0,half):
            lh=l[h:h+half]
            e=jnp.exp(lh-jnp.max(lh,axis=0,keepdims=True))
            pkT[h:h+half,pl.ds(o,GRP)]=e/jnp.sum(e,axis=0,keepdims=True)
        dpT[:,pl.ds(o,GRP)]=jnp.zeros((128,GRP),F32)
        return 0
    lax.fori_loop(0,TOKENS//GRP,kfeat,0)

    dwq_s[...]=jnp.zeros_like(dwq_s)
    loss_ref[...]=jnp.zeros_like(loss_ref)
    st_s[...]=jnp.zeros_like(st_s)

    def block(z,_):
        b=4*z+xi
        i0=192*b
        ls=pl.multiple_of(local_start(b),128)
        prev=jnp.where(z>0,local_start(b-4),0)
        q=q_ref[z]
        kl=k_ref[pl.ds(ls,LOC),:]
        vl=vx[pl.ds(ls,LOC),:]
        icol=i0+lax.broadcasted_iota(jnp.int32,(BLK,1),0)
        dcol=dstart(icol)
        jrow=ls+lax.broadcasted_iota(jnp.int32,(1,LOC),1)
        same=jrow>=dcol
        s=mm(q,kl,1,1)
        vis=same&(jrow<=icol)
        sm=jnp.where(vis,s,NEG)
        m=jnp.max(sm,axis=1,keepdims=True)
        p=jnp.exp2((sm-m)*c2)
        acc=mm(p.astype(BF),vl)
        lo=dstart(i0)
        def tile(n,carry):
            m,acc=carry
            hi_=ls-n*TK
            ts=pl.multiple_of(jnp.maximum(hi_-TK,0),128)
            kt=k_ref[pl.ds(ts,TK),:]
            vt=vx[pl.ds(ts,TK),:]
            jr=ts+lax.broadcasted_iota(jnp.int32,(1,TK),1)
            sc=mm(q,kt,1,1)
            jr=jnp.where(jr<hi_,jr,-1)
            sc=jnp.where(jr>=dcol,sc,NEG)
            mn=jnp.maximum(m,jnp.max(sc,axis=1,keepdims=True))
            al=jnp.exp2((m-mn)*c2)
            pp=jnp.exp2((sc-mn)*c2)
            acc=acc*al+mm(pp.astype(BF),vt)
            return mn,acc
        ntile=jnp.maximum((ls-lo+TK-1)//TK,0)
        m,acc=lax.fori_loop(0,ntile,tile,(m,acc))
        t=(acc[:,:128]/acc[:,128:]).astype(BF)
        t_ref[z]=t
        lq=mm(q,wq2)
        lq=lq[:,:128]+lq[:,128:]
        ph=[]
        for h in (0,half):
            lh=lq[:,h:h+half]
            e=jnp.exp(lh-jnp.max(lh,axis=1,keepdims=True))
            ph.append(e/jnp.sum(e,axis=1,keepdims=True))
        pq=jnp.concatenate(ph,axis=1)
        pq_h,pq_l=hilo(pq)
        gs=pl.multiple_of(jnp.maximum(ls-GRP,0),128)
        dtag=dstart(ls-1)
        jg=gs+lax.broadcasted_iota(jnp.int32,(1,GRP),1)
        gm=(jg>=jnp.maximum(dtag,prev))&(jg<ls)
        pg=jnp.where(gm,pkT[:,pl.ds(gs,GRP)],0.0).astype(BF)
        keep=jnp.where(dtag<prev,1.0,0.0)
        st=st_s[...]*keep+mm(pg,vx[pl.ds(gs,GRP),:])
        st_s[...]=st
        uses=jnp.where((dcol==dtag)&(ls>0),1.0,0.0)
        sh,sl=hilo(st)
        sth=mm(pq_h,sh)+mm(pq_l,sh)+mm(pq_h,sl)
        inw=same&(jrow<=icol)&(jrow>icol-WINDOW)
        swm=jnp.where(inw,s,NEG)
        mw=jnp.max(swm,axis=1,keepdims=True)
        a=jnp.exp2((swm-mw)*c2)
        bey=same&(jrow<=icol-WINDOW)
        pl_T=pkT[:,pl.ds(ls,LOC)].astype(BF)
        bb=jnp.where(bey,mm(pq_h,pl_T),0.0)
        nd=mm((a+bb).astype(BF),vl)+uses*sth
        rden=1.0/nd[:,128:]
        y=nd[:,:128]*rden
        y_ref[z]=y.astype(BF)
        e=y-t.astype(F32)
        loss_ref[...]+=jnp.sum((e*e).reshape(BLK//8,8,128),axis=0)
        g=e*rden*(2.0*norm)
        gx=jnp.concatenate([g,-g*y],axis=1)
        gh,gl=hilo(gx)
        db=jnp.where(bey,mm(gh,vl,1,1),0.0).astype(BF)
        gu=gx*uses
        guh,gul=hilo(gu)
        dpq=mm(db,pl_T,1,1)+mm(guh,sh,1,1)+mm(gul,sh,1,1)+mm(guh,sl,1,1)
        dpT[:,pl.ds(ls,LOC)]+=mm(pq_h,db,0,0)
        ds_s[z]=mm(pq_h,guh,0,0)
        out=[]
        for h in (0,half):
            pp=pq[:,h:h+half]; dd=dpq[:,h:h+half]
            out.append(pp*(dd-jnp.sum(pp*dd,axis=1,keepdims=True)))
        dl=jnp.concatenate(out,axis=1)
        dh,dlo=hilo(dl)
        dwq_s[...]+=mm(q,jnp.concatenate([dh,dlo],axis=1),0,0)
        return 0
    lax.fori_loop(0,NB,block,0)

    st_s[...]=jnp.zeros_like(st_s)
    def back(n,_):
        z=NB-1-n
        b=4*z+xi
        ls=pl.multiple_of(local_start(b),128)
        prev=jnp.where(z>0,local_start(b-4),0)
        nxt=jnp.where(z<NB-1,local_start(b+4),ls)
        dtag=dstart(ls-1)
        keep=jnp.where(dstart(nxt-1)==dtag,1.0,0.0)
        r=st_s[...]*keep+ds_s[z]
        st_s[...]=r
        gs=pl.multiple_of(jnp.maximum(ls-GRP,0),128)
        jg=gs+lax.broadcasted_iota(jnp.int32,(1,GRP),1)
        gm=(jg>=jnp.maximum(dtag,prev))&(jg<ls)
        d=mm(r.astype(BF),vx[pl.ds(gs,GRP),:],1,1)
        dpT[:,pl.ds(gs,GRP)]+=jnp.where(gm,d,0.0)
        return 0
    lax.fori_loop(0,NB,back,0)

    def fin(c,acc):
        o=pl.multiple_of(c*GRP,GRP)
        out=[]
        for h in (0,half):
            pp=pkT[h:h+half,pl.ds(o,GRP)]; dd=dpT[h:h+half,pl.ds(o,GRP)]
            out.append(pp*(dd-jnp.sum(pp*dd,axis=0,keepdims=True)))
        dl=jnp.concatenate(out,axis=0)
        dh,dlo=hilo(dl)
        kk=k_ref[pl.ds(o,GRP),:]
        return acc+mm(dh,kk)+mm(dlo,kk)
    dk=lax.fori_loop(0,TOKENS//GRP,fin,jnp.zeros((128,128),F32))
    dkt=dk.T
    dq=dwq_s[:,:128]+dwq_s[:,128:]
    dw_ref[...]=jnp.concatenate([dq[:,:half]-dq[:,half:],dkt[:,:half]-dkt[:,half:]],axis=1)

def compute(norm, st, q, k, v, w):
    V=pl.BlockSpec(memory_space=pltpu.VMEM)
    return pl.pallas_call(
        functools.partial(compute_kernel,norm),
        out_shape=(jax.ShapeDtypeStruct((NB,BLK,128),BF),jax.ShapeDtypeStruct((NB,BLK,128),BF),
                   jax.ShapeDtypeStruct((128,128),F32),jax.ShapeDtypeStruct((8,128),F32)),
        in_specs=[pl.BlockSpec(memory_space=pltpu.SMEM)]+[V]*4,
        out_specs=(V,)*4,
        scratch_shapes=[pltpu.VMEM((TOKENS,256),BF),pltpu.VMEM((128,TOKENS),F32),pltpu.VMEM((128,TOKENS),F32),
                        pltpu.VMEM((128,256),F32),pltpu.VMEM((NB,128,256),F32),pltpu.VMEM((BLK,128),F32),pltpu.VMEM((128,256),F32)],
        compiler_params=pltpu.CompilerParams(vmem_limit_bytes=60<<20),
    )(st,q,k,v,w)


NZ, NX = 8, 4
ORDER = (0, 1, 7, 2, 6, 3, 5, 4)


def rcopy(src, dst, ssem, rsem, **where):
    return pltpu.make_async_remote_copy(
        src_ref=src, dst_ref=dst, send_sem=ssem, recv_sem=rsem,
        device_id=where, device_id_type=MESH)


def greet(peers):
    barrier = pltpu.get_barrier_semaphore()
    for peer in peers:
        pl.semaphore_signal(barrier, inc=1, device_id=peer, device_id_type=MESH)
    pl.semaphore_wait(barrier, len(peers))


def gather_kernel(q_ref, k_ref, v_ref, c_ref, qa, ka, va, ca,
                  zs, zr, rs, rr, ls, lr, ys, yr, cs, cr, own):
    z, x = lax.axis_index("seq_0"), lax.axis_index("seq_1")
    right, left = lax.rem(x + 1, NX), lax.rem(x + 3, NX)
    greet([{"seq_0": lax.rem(z + d, NZ)} for d in range(1, NZ)]
          + [{"seq_1": lax.rem(x + d, NX)} for d in range(1, NX)])
    me = NX * z + x
    local = [pltpu.make_async_copy(k_ref.at[z], ka.at[me], own.at[0]),
             pltpu.make_async_copy(v_ref.at[z], va.at[me], own.at[1]),
             pltpu.make_async_copy(q_ref.at[z], qa.at[z], own.at[2]),
             pltpu.make_async_copy(c_ref, ca.at[x, z], own.at[3])]
    for c in local:
        c.start()
    sent = []
    for ref, dst, i in ((k_ref, ka, 0), (v_ref, va, 1), (q_ref, qa, 2)):
        for d in ORDER[1:]:
            t = lax.rem(z + d, NZ)
            c = rcopy(ref.at[t], dst.at[z if i == 2 else me], zs.at[i, t], zr.at[i, z], seq_0=t)
            c.start()
            sent.append(c)
        if i == 0:
            for d in ORDER[1:]:
                t = lax.rem(z + d, NZ)
                c = rcopy(c_ref, ca.at[x, z], zs.at[3, t], zr.at[3, z], seq_0=t)
                c.start()
                sent.append(c)

    def arrived(i, s, dst):
        rcopy(dst, dst, zs.at[i, s], zr.at[i, s], seq_0=s).wait_recv()

    for c in local:
        c.wait()
    relayed = []

    def relay(s):
        slot = NX * s + left
        c = rcopy(ka.at[slot], ka.at[slot], rs.at[0, s], rr.at[0, s], seq_1=right)
        c.wait_recv()
        c = rcopy(ka.at[slot], ka.at[slot], ys.at[0, s], yr.at[0, s], seq_1=right)
        c.start()
        relayed.append(c)
        slot = NX * s + right
        c = rcopy(va.at[slot], va.at[slot], ls.at[1, s], lr.at[1, s], seq_1=left)
        c.wait_recv()
        c = rcopy(va.at[slot], va.at[slot], ys.at[1, s], yr.at[1, s], seq_1=left)
        c.start()
        relayed.append(c)

    last = None
    for d in ORDER:
        s = lax.rem(z + d, NZ)
        slot = NX * s + x
        for i, arr in ((0, ka), (1, va)):
            if d:
                arrived(i, s, arr.at[slot])
            for sems, semr, to in ((rs, rr, right), (ls, lr, left)):
                c = rcopy(arr.at[slot], arr.at[slot], sems.at[i, s], semr.at[i, s], seq_1=to)
                c.start()
                sent.append(c)
        if last is not None:
            relay(last)
        last = s
    for d in ORDER[1:]:
        s = lax.rem(z + d, NZ)
        arrived(3, s, ca.at[x, s])
    for d in range(1, NX):
        t = lax.rem(x + d, NX)
        c = rcopy(ca.at[x], ca.at[x], cs.at[t], cr.at[x], seq_1=t)
        c.start()
        sent.append(c)
    relay(last)
    for d in ORDER[1:]:
        s = lax.rem(z + d, NZ)
        arrived(2, s, qa.at[s])
    for d in range(1, NX):
        s = lax.rem(x + d, NX)
        rcopy(ca.at[s], ca.at[s], cs.at[s], cr.at[s], seq_1=s).wait_recv()
    far = lax.rem(x + 2, NX)
    for d in ORDER:
        s = lax.rem(z + d, NZ)
        slot = NX * s + left
        rcopy(va.at[slot], va.at[slot], rs.at[1, s], rr.at[1, s], seq_1=right).wait_recv()
        slot = NX * s + right
        rcopy(ka.at[slot], ka.at[slot], ls.at[0, s], lr.at[0, s], seq_1=left).wait_recv()
        slot = NX * s + far
        rcopy(ka.at[slot], ka.at[slot], ys.at[0, s], yr.at[0, s], seq_1=right).wait_recv()
        rcopy(va.at[slot], va.at[slot], ys.at[1, s], yr.at[1, s], seq_1=left).wait_recv()
    for c in sent + relayed:
        c.wait_send()


def gather(q, k, v, counts):
    A = pl.BlockSpec(memory_space=pl.ANY)
    D = pltpu.SemaphoreType.DMA
    return pl.pallas_call(
        gather_kernel,
        out_shape=(jax.ShapeDtypeStruct((NZ, BLK, 128), BF),
                   jax.ShapeDtypeStruct((NZ * NX, BLK, 128), BF),
                   jax.ShapeDtypeStruct((NZ * NX, BLK, 128), BF),
                   jax.ShapeDtypeStruct((NX, NZ, 8, 128), F32)),
        in_specs=[A] * 4, out_specs=(A,) * 4,
        scratch_shapes=[D((4, NZ)), D((4, NZ)), D((2, NZ)), D((2, NZ)), D((2, NZ)), D((2, NZ)),
                        D((2, NZ)), D((2, NZ)), D((NX,)), D((NX,)), D((4,))],
        compiler_params=pltpu.CompilerParams(collective_id=0, has_side_effects=True),
    )(q, k, v, counts)


def spread_kernel(t_ref, y_ref, dw_ref, l_ref, ta, ya, wa, la,
                  wx, wsum, lx, lz, lc, fin,
                  zs, zr, xs, xr, gs, gr, own):
    z, x = lax.axis_index("seq_0"), lax.axis_index("seq_1")
    h, g = lax.axis_index("head"), lax.axis_index("grp")
    cols = [{"grp": lax.rem(g + (d // NX), 2), "head": lax.rem(h + d % NX, NX)} for d in range(1, 8)]
    greet([{"seq_0": lax.rem(z + d, NZ)} for d in range(1, NZ)]
          + [{"seq_1": lax.rem(x + d, NX)} for d in range(1, NX)] + cols)
    local = [pltpu.make_async_copy(t_ref.at[z], ta.at[z], own.at[0]),
             pltpu.make_async_copy(y_ref.at[z], ya.at[z], own.at[1]),
             pltpu.make_async_copy(dw_ref, wx.at[x], own.at[2]),
             pltpu.make_async_copy(l_ref, lx.at[x], own.at[3])]
    for c in local:
        c.start()
    sent = []
    for i, (src, dst) in enumerate(((dw_ref, wx), (l_ref, lx))):
        for d in range(1, NX):
            t = lax.rem(x + d, NX)
            c = rcopy(src, dst.at[x], xs.at[i, t], xr.at[i, x], seq_1=t)
            c.start()
            sent.append(c)
    for i, (src, dst) in enumerate(((t_ref, ta), (y_ref, ya))):
        for d in ORDER[1:]:
            t = lax.rem(z + d, NZ)
            c = rcopy(src.at[t], dst.at[z], zs.at[i, t], zr.at[i, z], seq_0=t)
            c.start()
            sent.append(c)
    for c in local:
        c.wait()
    for i, dst in enumerate((wx, lx)):
        for d in range(1, NX):
            s = lax.rem(x + d, NX)
            rcopy(dst.at[s], dst.at[s], xs.at[i, s], xr.at[i, s], seq_1=s).wait_recv()
    wsum[...] = (wx[0] + wx[1]) + (wx[2] + wx[3])
    lz[z] = (lx[0] + lx[1]) + (lx[2] + lx[3])
    keep = pltpu.make_async_copy(wsum, wa.at[z], own.at[2])
    keep.start()
    for d in ORDER[1:]:
        t = lax.rem(z + d, NZ)
        c = rcopy(lz.at[z], lz.at[z], zs.at[3, t], zr.at[3, z], seq_0=t)
        c.start()
        sent.append(c)
        c = rcopy(wsum, wa.at[z], zs.at[2, t], zr.at[2, z], seq_0=t)
        c.start()
        sent.append(c)
    for d in ORDER[1:]:
        s = lax.rem(z + d, NZ)
        rcopy(lz.at[s], lz.at[s], zs.at[3, s], zr.at[3, s], seq_0=s).wait_recv()
    part = lz[0]
    for i in range(1, NZ):
        part = part + lz[i]
    mine = NX * g + h
    lc[mine] = part
    for d, peer in zip(range(1, 8), cols):
        there = NX * peer["grp"] + peer["head"]
        c = rcopy(lc.at[mine], lc.at[mine], gs.at[there], gr.at[mine], **peer)
        c.start()
        sent.append(c)
    for peer in cols:
        there = NX * peer["grp"] + peer["head"]
        rcopy(lc.at[there], lc.at[there], gs.at[there], gr.at[there], **peer).wait_recv()
    part = lc[0]
    for i in range(1, 8):
        part = part + lc[i]
    total = jnp.sum(jnp.sum(part, axis=0, keepdims=True), axis=1, keepdims=True)
    fin[...] = jnp.broadcast_to(total, (8, 128))
    done = pltpu.make_async_copy(fin, la, own.at[3])
    done.start()
    for d in ORDER[1:]:
        s = lax.rem(z + d, NZ)
        for i, dst in enumerate((ta, ya, wa)):
            rcopy(dst.at[s], dst.at[s], zs.at[i, s], zr.at[i, s], seq_0=s).wait_recv()
    for c in sent:
        c.wait_send()
    keep.wait()
    done.wait()


def spread(t, y, dw, l):
    A = pl.BlockSpec(memory_space=pl.ANY)
    D = pltpu.SemaphoreType.DMA
    V = pltpu.VMEM
    return pl.pallas_call(
        spread_kernel,
        out_shape=(jax.ShapeDtypeStruct((NZ, BLK, 128), BF),
                   jax.ShapeDtypeStruct((NZ, BLK, 128), BF),
                   jax.ShapeDtypeStruct((NZ, 128, 128), F32),
                   jax.ShapeDtypeStruct((8, 128), F32)),
        in_specs=[A] * 4, out_specs=(A,) * 4,
        scratch_shapes=[V((NX, 128, 128), F32), V((128, 128), F32), V((NX, 8, 128), F32),
                        V((NZ, 8, 128), F32), V((8, 8, 128), F32), V((8, 128), F32),
                        D((4, NZ)), D((4, NZ)), D((2, NX)), D((2, NX)), D((8,)), D((8,)), D((4,))],
        compiler_params=pltpu.CompilerParams(collective_id=1, has_side_effects=True),
    )(t, y, dw, l)


def body(queries, keys, values, documents, feature_map):
    z, x = lax.axis_index("seq_0"), lax.axis_index("seq_1")
    norm = 1.0 / (TOKENS * 64)
    below = [jnp.sum((documents < d).astype(F32)) for d in (1, 2, 3)]
    row = jnp.stack(below + [jnp.float32(0)] * 5)
    counts = jnp.broadcast_to(row[:, None], (8, 128))
    turned = [jnp.swapaxes(a, 0, 1) for a in (queries, keys, values)]
    qa, ka, va, ca = gather(*turned, counts)
    starts = jnp.sum(ca[:, :, :, 0], axis=(0, 1)).astype(jnp.int32)
    scalars = jnp.concatenate([starts[:3], jnp.stack([x, z]).astype(jnp.int32)])
    w = lax.dynamic_index_in_dim(feature_map, z, 0, keepdims=False)
    t, y, dw, loss = compute(norm, scalars, qa, ka.reshape(TOKENS, 128), va.reshape(TOKENS, 128), w)
    ta, ya, wa, la = spread(t, y, dw, loss * norm)
    return (jnp.swapaxes(ta, 0, 1), jnp.swapaxes(ya, 0, 1), la[0, 0], wa)


def solution(mesh):
    split = Mesh(
        mesh.devices.reshape(mesh.shape["grp"], 8, 4, mesh.shape["head"]),
        ("grp", "seq_0", "seq_1", "head"),
    )
    return jax.shard_map(
        body,
        mesh=split,
        in_specs=(
            P(SEQ, ("grp", "head"), None),
            P(SEQ, ("grp", "head"), None),
            P(SEQ, ("grp", "head"), None),
            P(SEQ),
            P(("grp", "head"), None, None),
        ),
        out_specs=(
            P(SEQ, ("grp", "head"), None),
            P(SEQ, ("grp", "head"), None),
            P(),
            P(("grp", "head"), None, None),
        ),
        check_vma=False,
    )
```

```python
import functools
import math

import jax
import jax.numpy as jnp
from jax import lax
from jax.experimental import pallas as pl
from jax.experimental.pallas import tpu as pltpu
from jax.sharding import Mesh
from jax.sharding import PartitionSpec as P

SEQ = ("seq_0", "seq_1")
MESH = pl.DeviceIdType.MESH

TOKENS, BLK, WINDOW, LOC, GRP, HALF = 6144, 192, 64, 384, 768, 64
NZ, NX = 8, 4
FRONT = 896
ROWS = FRONT + TOKENS + 128
F32, BF = jnp.float32, jnp.bfloat16
NEG = -1e30
SCALE = 128**-0.5
C2 = SCALE * math.log2(math.e)


def mm(a, b, ca=1, cb=0):
    return lax.dot_general(a, b, (((ca,), (cb,)), ((), ())), preferred_element_type=F32)


def hilo(a):
    hi = a.astype(BF)
    return hi, (a - hi.astype(F32)).astype(BF)


def rcopy(src, dst, ssem, rsem, **where):
    return pltpu.make_async_remote_copy(
        src_ref=src, dst_ref=dst, send_sem=ssem, recv_sem=rsem,
        device_id=where, device_id_type=MESH)


def greet(peers):
    barrier = pltpu.get_barrier_semaphore()
    for peer in peers:
        pl.semaphore_signal(barrier, inc=1, device_id=peer, device_id_type=MESH)
    pl.semaphore_wait(barrier, len(peers))


def nth(j):
    odd = lax.rem(j, 2)
    return lax.rem(odd * ((j + 1) // 2) + (1 - odd) * (NZ - j // 2), NZ)


def with_ones(v):
    return jnp.concatenate([v, jnp.ones_like(v)], axis=1)


def iota(shape, dim):
    return lax.broadcasted_iota(jnp.int32, shape, dim).astype(F32)


def kernel(norm, q_ref, k_ref, v_ref, doc_ref, fm_ref, ta, ya, wout, lout,
           qa, ka, va, ca, qe, ke, wq2, wk2, pkT, dpT, ms, accs, tb, yb, sts, dss, run, dwq, pls,
           dwb, wx, wg, lx, lz, lc,
           own, zs, zr, rs, rr, ls_, lr, ys, yr, cs, cr, xs, xr, gs, gr, os, orr):
    z, x = lax.axis_index("seq_0"), lax.axis_index("seq_1")
    h, g = lax.axis_index("head"), lax.axis_index("grp")
    right, left, far = lax.rem(x + 1, NX), lax.rem(x + 3, NX), lax.rem(x + 2, NX)
    cols = [{"grp": lax.rem(g + (d // NX), 2), "head": lax.rem(h + d % NX, NX)} for d in range(1, 8)]

    docs = doc_ref[...]
    row = lax.broadcasted_iota(jnp.int32, (8, 128), 0)
    tile = jnp.zeros((8, 128), F32)
    for d in (1, 2, 3):
        n = jnp.sum((docs < d).astype(F32), axis=1, keepdims=True)
        tile = tile + jnp.where(row == d, jnp.broadcast_to(n, (8, 128)), 0.0)
    ca[x, z] = tile
    zero = jnp.zeros((FRONT, 128), BF)
    ka[:FRONT] = zero
    va[:FRONT] = zero
    ka[FRONT + TOKENS:] = zero[:128]
    va[FRONT + TOKENS:] = zero[:128]
    pkT[:, :FRONT] = jnp.zeros((128, FRONT), F32)
    pkT[:, FRONT + TOKENS:] = jnp.zeros((128, 128), F32)
    w = fm_ref[z]
    wqh, wql = hilo(jnp.concatenate([w[:, :HALF], -w[:, :HALF]], axis=1))
    wq2[...] = jnp.concatenate([wqh, wql], axis=1)
    wkh, wkl = hilo(jnp.concatenate([w[:, HALF:], -w[:, HALF:]], axis=1).T)
    wk2[0] = wkh
    wk2[1] = wkl

    greet([{"seq_0": lax.rem(z + d, NZ)} for d in range(1, NZ)]
          + [{"seq_1": lax.rem(x + d, NX)} for d in range(1, NX)] + cols)

    def krows(arr, s, col):
        return arr.at[pl.ds(pl.multiple_of(FRONT + GRP * s + BLK * col, 64), BLK)]

    def zcopy(i, t):
        src = (k_ref, v_ref, q_ref)[i].at[t]
        dst = qa.at[z] if i == 2 else krows((ka, va)[i], z, x)
        return rcopy(src, dst, zs.at[i, t], zr.at[i, z], seq_0=t)

    def zarrive(i, s):
        dst = qa.at[s] if i == 2 else krows((ka, va)[i], s, x)
        rcopy(dst, dst, zs.at[i, s], zr.at[i, s], seq_0=s).wait_recv()

    def count_copy(t):
        return rcopy(ca.at[x, z], ca.at[x, z], zs.at[3, t], zr.at[3, z], seq_0=t)

    def xcopy(i, s, col, to, sems, semr):
        ref = krows((ka, va)[i], s, col)
        return rcopy(ref, ref, sems.at[i, s], semr.at[i, s], seq_1=to)

    local = [pltpu.make_async_copy(k_ref.at[z], krows(ka, z, x), own.at[0]),
             pltpu.make_async_copy(v_ref.at[z], krows(va, z, x), own.at[1]),
             pltpu.make_async_copy(q_ref.at[z], qa.at[z], own.at[2])]
    for c in local:
        c.start()
    for j in range(1, NZ):
        count_copy(lax.rem(z + nth(j), NZ)).start()

    def send_all(j, _):
        t = lax.rem(z + NZ - nth(j), NZ)
        for i in range(3):
            zcopy(i, t).start()
        return 0
    lax.fori_loop(1, NZ, send_all, 0)
    for c in local:
        c.wait()

    def forward(s):
        for i in range(2):
            xcopy(i, s, x, right, rs, rr).start()
            xcopy(i, s, x, left, ls_, lr).start()

    def relay(s):
        xcopy(0, s, left, right, rs, rr).wait_recv()
        xcopy(0, s, left, right, ys, yr).start()
        xcopy(1, s, right, left, ls_, lr).wait_recv()
        xcopy(1, s, right, left, ys, yr).start()

    def complete(s):
        xcopy(1, s, left, right, rs, rr).wait_recv()
        xcopy(0, s, right, left, ls_, lr).wait_recv()
        xcopy(0, s, far, right, ys, yr).wait_recv()
        xcopy(1, s, far, left, ys, yr).wait_recv()

    forward(z)
    for j in range(1, NZ):
        s = lax.rem(z + j, NZ)
        rcopy(ca.at[x, s], ca.at[x, s], zs.at[3, s], zr.at[3, s], seq_0=s).wait_recv()
    for d in range(1, NX):
        t = lax.rem(x + d, NX)
        rcopy(ca.at[x], ca.at[x], cs.at[t], cr.at[x], seq_1=t).start()
    relay(z)
    for d in range(1, NX):
        s = lax.rem(x + d, NX)
        rcopy(ca.at[s], ca.at[s], cs.at[s], cr.at[s], seq_1=s).wait_recv()
    for d in range(1, NX):
        t = lax.rem(x + d, NX)
        rcopy(ca.at[x], ca.at[x], cs.at[t], cr.at[x], seq_1=t).wait_send()
    tally = jnp.zeros((8, 128), F32)
    for i in range(NX):
        for j in range(NZ):
            tally = tally + ca[i, j]
    st1, st2, st3 = tally[1:2, :1], tally[2:3, :1], tally[3:4, :1]
    lane = lax.broadcasted_iota(jnp.int32, (1, 128), 1)
    full = lambda d: tally[d:d + 1, :]
    low = jnp.where(lane == 0, 0.0, jnp.where(lane == 1, full(1), jnp.where(
        lane == 2, full(2), jnp.where(lane == 3, full(3), 1e9))))
    high = jnp.where(lane == 0, full(1), jnp.where(lane == 1, full(2), jnp.where(
        lane == 2, full(3), 1e9)))

    def dstart(i):
        return jnp.where(i >= st3, st3, jnp.where(i >= st2, st2, jnp.where(i >= st1, st1, 0.0)))

    def qpos(s):
        return (GRP * s + BLK * x).astype(F32) + iota((BLK, 1), 0)

    def absorb(n):
        a = lax.rem(z + nth(n), NZ)
        o = pl.multiple_of(FRONT + GRP * a, 128)
        kk = ka[pl.ds(o, GRP), :]
        l = mm(wk2[0], kk, 1, 1) + mm(wk2[1], kk, 1, 1)
        for f in (0, HALF):
            lh = l[f:f + HALF]
            e = jnp.exp(lh - jnp.max(lh, axis=0, keepdims=True))
            pkT[f:f + HALF, pl.ds(o, GRP)] = e * (1.0 / jnp.sum(e, axis=0, keepdims=True))
        kpos = (GRP * a).astype(F32) + iota((GRP, 1), 0)
        ke[pl.ds(o, GRP), :] = jnp.where((kpos >= low) & (kpos < high), 1.0, 0.0).astype(BF)
        icol = qpos(a)
        miss = jnp.logical_not((icol >= low) & (icol < high)) & (lane < 4)
        qe[a] = jnp.where(miss, NEG, 0.0).astype(BF)
        jrow = (GRP * a).astype(F32) + iota((1, GRP), 1)
        s = mm(qa[a], kk, 1, 1)
        s = jnp.where((jrow <= icol) & (jrow >= dstart(icol)), s, NEG)
        m = jnp.max(s, axis=1, keepdims=True)
        p = jnp.exp2((s - m) * C2)
        ms[a] = m
        accs[a] = mm(p.astype(BF), with_ones(va[pl.ds(o, GRP), :]))

        def pair(j, _):
            b = lax.rem(z + nth(j), NZ)
            ge = (a - b + NZ) // NZ
            zq, zk = ge * a + (1 - ge) * b, ge * b + (1 - ge) * a
            r = pl.multiple_of(FRONT + GRP * zk, 128)
            sc = mm(jnp.concatenate([qa[zq], qe[zq]], axis=1),
                    jnp.concatenate([ka[pl.ds(r, GRP), :], ke[pl.ds(r, GRP), :]], axis=1), 1, 1)
            mo = ms[zq]
            mn = jnp.maximum(mo, jnp.max(sc, axis=1, keepdims=True))
            pp = jnp.exp2((sc - mn) * C2)
            ms[zq] = mn
            accs[zq] = accs[zq] * jnp.exp2((mo - mn) * C2) + mm(
                pp.astype(BF), with_ones(va[pl.ds(r, GRP), :]))
            return 0
        lax.fori_loop(0, n, pair, 0)

    def step(n, _):
        s = lax.rem(z + nth(n), NZ)
        zarrive(0, s)
        zarrive(1, s)
        forward(s)
        prior = lax.rem(z + nth(n - 1), NZ)
        complete(prior)
        absorb(n - 1)
        relay(s)
        zarrive(2, s)
        return 0
    lax.fori_loop(1, NZ, step, 0)
    complete(lax.rem(z + nth(NZ - 1), NZ))
    absorb(jnp.int32(NZ - 1))

    off = BLK * x + 64 * lax.rem(x, 2)
    run[...] = jnp.zeros_like(run)

    def local_row(s):
        return pl.multiple_of(GRP * s + off + GRP, 128)

    def group_mask(s):
        end = (GRP * s + off + GRP - FRONT).astype(F32)
        jg = end - GRP + iota((1, GRP), 1)
        tag = dstart(jnp.zeros((1, 1), F32) + (end - 1.0))
        return (jg >= tag) & (jg < end) & (jg >= 0.0), tag, end

    def states(s, _):
        r = local_row(s)
        mask, tag, end = group_mask(s)
        o = pl.multiple_of(r - GRP, 128)
        pg = jnp.where(mask, pkT[:, pl.ds(o, GRP)], 0.0).astype(BF)
        keep = jnp.where(tag < end - GRP, 1.0, 0.0)
        st = run[...] * keep + mm(pg, with_ones(va[pl.ds(o, GRP), :]))
        run[...] = st
        hi, lo = hilo(st)
        sts[s, 0] = hi
        sts[s, 1] = lo
        tb[s] = (accs[s][:, :128] / accs[s][:, 128:]).astype(BF)
        return 0
    lax.fori_loop(0, NZ, states, 0)

    dwq[...] = jnp.zeros_like(dwq)
    pls[...] = jnp.zeros_like(pls)
    dpT[...] = jnp.zeros_like(dpT)

    def send_out(i, t):
        src, dst = ((tb, ta), (yb, ya))[i]
        return rcopy(src.at[t], dst.at[z], os.at[i, t], orr.at[i, z], seq_0=t)

    def block(n, _):
        s = lax.rem(z + nth(NZ - 1 - n), NZ)

        @pl.when(n < NZ - 1)
        def _():
            send_out(0, s).start()

        @pl.when(n > 0)
        def _():
            send_out(1, lax.rem(z + nth(NZ - n), NZ)).start()
        r = local_row(s)
        q = qa[s]
        kl = ka[pl.ds(r, LOC), :]
        vl = with_ones(va[pl.ds(r, LOC), :])
        icol = qpos(s)
        dcol = dstart(icol)
        jrow = (GRP * s + off + GRP - FRONT).astype(F32) + iota((1, LOC), 1)
        same = jrow >= dcol
        sc = mm(q, kl, 1, 1)
        lq = mm(q, wq2[...])
        lq = lq[:, :128] + lq[:, 128:]
        ph = []
        for f in (0, HALF):
            lh = lq[:, f:f + HALF]
            e = jnp.exp(lh - jnp.max(lh, axis=1, keepdims=True))
            ph.append(e * (1.0 / jnp.sum(e, axis=1, keepdims=True)))
        pq = jnp.concatenate(ph, axis=1)
        pq_h, pq_l = hilo(pq)
        _, tag, end = group_mask(s)
        uses = jnp.where((dcol == tag) & (end > 0.0), 1.0, 0.0)
        sh, sl = sts[s, 0], sts[s, 1]
        sth = mm(pq_h, sh) + mm(pq_l, sh) + mm(pq_h, sl)
        swm = jnp.where(same & (jrow <= icol) & (jrow > icol - WINDOW), sc, NEG)
        a = jnp.exp2((swm - jnp.max(swm, axis=1, keepdims=True)) * C2)
        bey = same & (jrow <= icol - WINDOW)
        pl_T = pkT[:, pl.ds(r, LOC)].astype(BF)
        bb = jnp.where(bey, mm(pq_h, pl_T), 0.0)
        nd = mm((a + bb).astype(BF), vl) + uses * sth
        rden = 1.0 / nd[:, 128:]
        y = nd[:, :128] * rden
        yb[s] = y.astype(BF)
        e = y - tb[s].astype(F32)
        pls[...] += jnp.sum((e * e).reshape(BLK // 8, 8, 128), axis=0)
        gr_ = e * rden * (2.0 * norm)
        gx = jnp.concatenate([gr_, -gr_ * y], axis=1)
        gh, _ = hilo(gx)
        db = jnp.where(bey, mm(gh, vl, 1, 1), 0.0).astype(BF)
        guh, gul = hilo(gx * uses)
        dpq = mm(db, pl_T, 1, 1) + mm(guh, sh, 1, 1) + mm(gul, sh, 1, 1) + mm(guh, sl, 1, 1)
        dpT[:, pl.ds(r, LOC)] += mm(pq_h, db, 0, 0)
        dss[s] = mm(pq_h, guh, 0, 0)
        out = []
        for f in (0, HALF):
            pp, dd = pq[:, f:f + HALF], dpq[:, f:f + HALF]
            out.append(pp * (dd - jnp.sum(pp * dd, axis=1, keepdims=True)))
        dh, dlo = hilo(jnp.concatenate(out, axis=1))
        dwq[...] += mm(q, jnp.concatenate([dh, dlo], axis=1), 0, 0)
        return 0
    lax.fori_loop(0, NZ, block, 0)

    run[...] = jnp.zeros_like(run)

    def back(n, _):
        s = NZ - 1 - n
        o = pl.multiple_of(local_row(s) - GRP, 128)
        mask, tag, end = group_mask(s)
        keep = jnp.where(dstart(jnp.zeros((1, 1), F32) + (end + GRP - 1.0)) == tag, 1.0, 0.0)
        rr_ = run[...] * keep + dss[s]
        run[...] = rr_
        d = mm(rr_.astype(BF), with_ones(va[pl.ds(o, GRP), :]), 1, 1)
        dpT[:, pl.ds(o, GRP)] += jnp.where(mask, d, 0.0)
        return 0
    lax.fori_loop(0, NZ, back, 0)

    def fin(s, acc):
        o = pl.multiple_of(FRONT + GRP * s, 128)
        out = []
        for f in (0, HALF):
            pp, dd = pkT[f:f + HALF, pl.ds(o, GRP)], dpT[f:f + HALF, pl.ds(o, GRP)]
            out.append(pp * (dd - jnp.sum(pp * dd, axis=0, keepdims=True)))
        dh, dlo = hilo(jnp.concatenate(out, axis=0))
        kk = ka[pl.ds(o, GRP), :]
        return acc + mm(dh, kk) + mm(dlo, kk)
    dk = lax.fori_loop(0, NZ, fin, jnp.zeros((128, 128), F32)).T
    dq = dwq[:, :128] + dwq[:, 128:]
    dw = jnp.concatenate([dq[:, :HALF] - dq[:, HALF:], dk[:, :HALF] - dk[:, HALF:]], axis=1)
    dwb[...] = dw.reshape(NX, 32, 128)
    lx[x] = pls[...] * norm

    def scatter(i, t):
        if i:
            return rcopy(lx.at[x], lx.at[x], xs.at[1, t], xr.at[1, x], seq_1=t)
        return rcopy(dwb.at[t], wx.at[x], xs.at[0, t], xr.at[0, x], seq_1=t)
    for d in range(1, NX):
        for i in range(2):
            scatter(i, lax.rem(x + d, NX)).start()
    wx[x] = dwb[x]
    for d in range(1, NX):
        s = lax.rem(x + d, NX)
        rcopy(wx.at[s], wx.at[s], xs.at[0, s], xr.at[0, s], seq_1=s).wait_recv()
        rcopy(lx.at[s], lx.at[s], xs.at[1, s], xr.at[1, s], seq_1=s).wait_recv()
    wg[x, z] = ((wx[0] + wx[1]) + (wx[2] + wx[3])).astype(BF)
    lz[z] = (lx[0] + lx[1]) + (lx[2] + lx[3])

    def zspread(i, s, t):
        ref = (wg.at[x, s], lz.at[s])[i]
        return rcopy(ref, ref, zs.at[4 + i, t], zr.at[4 + i, s], seq_0=t)
    for j in range(1, NZ):
        for i in range(2):
            zspread(i, z, lax.rem(z + nth(j), NZ)).start()
    for j in range(1, NZ):
        s = lax.rem(z + j, NZ)
        zspread(1, s, s).wait_recv()
    part = lz[0]
    for i in range(1, NZ):
        part = part + lz[i]
    mine = NX * g + h
    lc[mine] = part
    for peer in cols:
        there = NX * peer["grp"] + peer["head"]
        rcopy(lc.at[mine], lc.at[mine], gs.at[there], gr.at[mine], **peer).start()
    for j in range(1, NZ):
        s = lax.rem(z + j, NZ)
        zspread(0, s, s).wait_recv()
    for d in range(1, NX):
        t = lax.rem(x + d, NX)
        rcopy(wg.at[x], wg.at[x], xs.at[2, t], xr.at[2, x], seq_1=t).start()
    for peer in cols:
        there = NX * peer["grp"] + peer["head"]
        rcopy(lc.at[there], lc.at[there], gs.at[there], gr.at[there], **peer).wait_recv()
    part = lc[0]
    for i in range(1, 8):
        part = part + lc[i]
    total = jnp.sum(jnp.sum(part, axis=0, keepdims=True), axis=1, keepdims=True)
    lout[...] = jnp.broadcast_to(total, (8, 128))
    keep = [pltpu.make_async_copy(tb.at[z], ta.at[z], own.at[0]),
            pltpu.make_async_copy(yb.at[z], ya.at[z], own.at[1])]
    for c in keep:
        c.start()
    for d in range(1, NX):
        s = lax.rem(x + d, NX)
        rcopy(wg.at[s], wg.at[s], xs.at[2, s], xr.at[2, s], seq_1=s).wait_recv()
    for i in range(NX):
        wout[:, i] = wg[i].astype(F32)

    def drain(j, _):
        s = lax.rem(z + j, NZ)
        for i, dst in enumerate((ta, ya)):
            rcopy(dst.at[s], dst.at[s], os.at[i, s], orr.at[i, s], seq_0=s).wait_recv()
            send_out(i, s).wait_send()
        for i in range(3):
            zcopy(i, s).wait_send()
        count_copy(s).wait_send()
        for i in range(2):
            zspread(i, z, s).wait_send()
        return 0
    lax.fori_loop(1, NZ, drain, 0)

    def drain_x(s, _):
        for i in range(2):
            xcopy(i, s, x, right, rs, rr).wait_send()
            xcopy(i, s, x, left, ls_, lr).wait_send()
        xcopy(0, s, left, right, ys, yr).wait_send()
        xcopy(1, s, right, left, ys, yr).wait_send()
        return 0
    lax.fori_loop(0, NZ, drain_x, 0)
    for d in range(1, NX):
        t = lax.rem(x + d, NX)
        scatter(0, t).wait_send()
        scatter(1, t).wait_send()
        rcopy(wg.at[x], wg.at[x], xs.at[2, t], xr.at[2, x], seq_1=t).wait_send()
    for peer in cols:
        there = NX * peer["grp"] + peer["head"]
        rcopy(lc.at[mine], lc.at[mine], gs.at[there], gr.at[mine], **peer).wait_send()
    for c in keep:
        c.wait()


def whole(norm, q, k, v, docs, fm):
    A = pl.BlockSpec(memory_space=pl.ANY)
    M = pl.BlockSpec(memory_space=pltpu.VMEM)
    D, V = pltpu.SemaphoreType.DMA, pltpu.VMEM
    return pl.pallas_call(
        functools.partial(kernel, norm),
        out_shape=(jax.ShapeDtypeStruct((NZ, BLK, 128), BF),
                   jax.ShapeDtypeStruct((NZ, BLK, 128), BF),
                   jax.ShapeDtypeStruct((NZ, NX, 32, 128), F32),
                   jax.ShapeDtypeStruct((8, 128), F32)),
        in_specs=[A, A, A, M, M], out_specs=(A, A, M, M),
        scratch_shapes=[
            V((NZ, BLK, 128), BF), V((ROWS, 128), BF), V((ROWS, 128), BF), V((NX, NZ, 8, 128), F32),
            V((NZ, BLK, 128), BF), V((ROWS, 128), BF), V((128, 256), BF), V((2, 128, 128), BF),
            V((128, ROWS), F32), V((128, ROWS), F32),
            V((NZ, BLK, 1), F32), V((NZ, BLK, 256), F32), V((NZ, BLK, 128), BF), V((NZ, BLK, 128), BF),
            V((NZ, 2, 128, 256), BF), V((NZ, 128, 256), F32), V((128, 256), F32), V((128, 256), F32),
            V((8, 128), F32),
            V((NX, 32, 128), F32), V((NX, 32, 128), F32), V((NX, NZ, 32, 128), BF),
            V((NX, 8, 128), F32), V((NZ, 8, 128), F32), V((8, 8, 128), F32),
            D((3,)), D((6, NZ)), D((6, NZ)), D((2, NZ)), D((2, NZ)), D((2, NZ)), D((2, NZ)),
            D((2, NZ)), D((2, NZ)), D((NX,)), D((NX,)), D((3, NX)), D((3, NX)), D((8,)), D((8,)),
            D((2, NZ)), D((2, NZ))],
        compiler_params=pltpu.CompilerParams(
            collective_id=0, has_side_effects=True, vmem_limit_bytes=60 << 20),
    )(q, k, v, docs, fm)


def body(queries, keys, values, documents, feature_map):
    norm = 1.0 / (TOKENS * 64)
    turned = [jnp.swapaxes(a, 0, 1) for a in (queries, keys, values)]
    ta, ya, wa, la = whole(norm, *turned, documents.reshape(1, BLK), feature_map)
    return (jnp.swapaxes(ta, 0, 1), jnp.swapaxes(ya, 0, 1), la[0, 0], wa.reshape(NZ, 128, 128))


def solution(mesh):
    split = Mesh(
        mesh.devices.reshape(mesh.shape["grp"], 8, 4, mesh.shape["head"]),
        ("grp", "seq_0", "seq_1", "head"),
    )
    return jax.shard_map(
        body,
        mesh=split,
        in_specs=(
            P(SEQ, ("grp", "head"), None),
            P(SEQ, ("grp", "head"), None),
            P(SEQ, ("grp", "head"), None),
            P(SEQ),
            P(("grp", "head"), None, None),
        ),
        out_specs=(
            P(SEQ, ("grp", "head"), None),
            P(SEQ, ("grp", "head"), None),
            P(),
            P(("grp", "head"), None, None),
        ),
        check_vma=False,
    )
```

```python
import functools
import math

import jax
import jax.numpy as jnp
from jax import lax
from jax.experimental import pallas as pl
from jax.experimental.pallas import tpu as pltpu
from jax.sharding import Mesh
from jax.sharding import PartitionSpec as P

SEQ = ("seq_0", "seq_1")
MESH = pl.DeviceIdType.MESH

TOKENS, BLK, WINDOW, LOC, GRP, HALF = 6144, 192, 64, 384, 768, 64
NZ, NX = 8, 4
FRONT = 896
ROWS = FRONT + TOKENS + 128
F32, BF = jnp.float32, jnp.bfloat16
NEG = -1e30
SCALE = 128**-0.5
C2 = SCALE * math.log2(math.e)


def mm(a, b, ca=1, cb=0):
    return lax.dot_general(a, b, (((ca,), (cb,)), ((), ())), preferred_element_type=F32)


def hilo(a):
    hi = a.astype(BF)
    return hi, (a - hi.astype(F32)).astype(BF)


def rcopy(src, dst, ssem, rsem, **where):
    return pltpu.make_async_remote_copy(
        src_ref=src, dst_ref=dst, send_sem=ssem, recv_sem=rsem,
        device_id=where, device_id_type=MESH)


def nth(j):
    odd = lax.rem(j, 2)
    return lax.rem(odd * ((j + 1) // 2) + (1 - odd) * (NZ - j // 2), NZ)


def with_ones(v):
    return jnp.concatenate([v, jnp.ones_like(v)], axis=1)


def iota(shape, dim):
    return lax.broadcasted_iota(jnp.int32, shape, dim).astype(F32)


def kernel(norm, q_ref, k_ref, v_ref, doc_ref, fm_ref, ta, ya, wout, lout,
           flat, out3, tr, qa, ka, va, ca, qe, ke, wq2, wk2, pkT, dpT, ms, accs, tb, yb, sts, dss, run, dwq, pls,
           dwb, wx, wg, lx, lz, lc,
           own, zs, zr, rs, rr, ls_, lr, ys, yr, cs, cr, xs, xr, gs, gr, os, orr):
    z, x = lax.axis_index("seq_0"), lax.axis_index("seq_1")
    h, g = lax.axis_index("head"), lax.axis_index("grp")
    right, left, far = lax.rem(x + 1, NX), lax.rem(x + 3, NX), lax.rem(x + 2, NX)
    cols = [{"grp": lax.rem(g + (d // NX), 2), "head": lax.rem(h + d % NX, NX)} for d in range(1, 8)]

    everyone = ([{"seq_0": lax.rem(z + d, NZ)} for d in range(1, NZ)]
                + [{"seq_1": lax.rem(x + d, NX)} for d in range(1, NX)] + cols)
    barrier = pltpu.get_barrier_semaphore()
    for peer in everyone:
        pl.semaphore_signal(barrier, inc=1, device_id=peer, device_id_type=MESH)

    for i, ref in enumerate((k_ref, v_ref, q_ref)):
        flat[...] = ref[...].astype(F32).reshape(BLK * NZ, 128)
        for d in range(NZ):
            out3[i, d] = flat[pl.ds(d, BLK, stride=NZ), :].astype(BF)

    docs = doc_ref[...]
    row = lax.broadcasted_iota(jnp.int32, (8, 128), 0)
    tile = jnp.zeros((8, 128), F32)
    for d in (1, 2, 3):
        n = jnp.sum((docs < d).astype(F32), axis=1, keepdims=True)
        tile = tile + jnp.where(row == d, jnp.broadcast_to(n, (8, 128)), 0.0)
    ca[x, z] = tile
    zero = jnp.zeros((FRONT, 128), BF)
    ka[:FRONT] = zero
    va[:FRONT] = zero
    ka[FRONT + TOKENS:] = zero[:128]
    va[FRONT + TOKENS:] = zero[:128]
    pkT[:, :FRONT] = jnp.zeros((128, FRONT), F32)
    pkT[:, FRONT + TOKENS:] = jnp.zeros((128, 128), F32)
    w = fm_ref[z]
    wqh, wql = hilo(jnp.concatenate([w[:, :HALF], -w[:, :HALF]], axis=1))
    wq2[...] = jnp.concatenate([wqh, wql], axis=1)
    wkh, wkl = hilo(jnp.concatenate([w[:, HALF:], -w[:, HALF:]], axis=1).T)
    wk2[0] = wkh
    wk2[1] = wkl

    pl.semaphore_wait(barrier, len(everyone))

    def krows(arr, s, col):
        return arr.at[pl.ds(pl.multiple_of(FRONT + GRP * s + BLK * col, 64), BLK)]

    def zcopy(i, t):
        src = out3.at[i, t]
        dst = qa.at[z] if i == 2 else krows((ka, va)[i], z, x)
        return rcopy(src, dst, zs.at[i, t], zr.at[i, z], seq_0=t)

    def zarrive(i, s):
        dst = qa.at[s] if i == 2 else krows((ka, va)[i], s, x)
        rcopy(dst, dst, zs.at[i, s], zr.at[i, s], seq_0=s).wait_recv()

    def count_copy(t):
        return rcopy(ca.at[x, z], ca.at[x, z], zs.at[3, t], zr.at[3, z], seq_0=t)

    def xcopy(i, s, col, to, sems, semr):
        ref = krows((ka, va)[i], s, col)
        return rcopy(ref, ref, sems.at[i, s], semr.at[i, s], seq_1=to)

    local = [pltpu.make_async_copy(out3.at[0, z], krows(ka, z, x), own.at[0]),
             pltpu.make_async_copy(out3.at[1, z], krows(va, z, x), own.at[1]),
             pltpu.make_async_copy(out3.at[2, z], qa.at[z], own.at[2])]
    for c in local:
        c.start()
    for j in range(1, NZ):
        count_copy(lax.rem(z + nth(j), NZ)).start()

    def send_all(j, _):
        t = lax.rem(z + NZ - nth(j), NZ)
        for i in range(3):
            zcopy(i, t).start()
        return 0
    lax.fori_loop(1, NZ, send_all, 0)
    for c in local:
        c.wait()

    def forward(s):
        for i in range(2):
            xcopy(i, s, x, right, rs, rr).start()
            xcopy(i, s, x, left, ls_, lr).start()

    def relay(s):
        xcopy(0, s, left, right, rs, rr).wait_recv()
        xcopy(0, s, left, right, ys, yr).start()
        xcopy(1, s, right, left, ls_, lr).wait_recv()
        xcopy(1, s, right, left, ys, yr).start()

    def complete(s):
        xcopy(1, s, left, right, rs, rr).wait_recv()
        xcopy(0, s, right, left, ls_, lr).wait_recv()
        xcopy(0, s, far, right, ys, yr).wait_recv()
        xcopy(1, s, far, left, ys, yr).wait_recv()

    def nearby(n):
        return lax.rem(z + nth(n), NZ)

    forward(z)
    for j in range(1, NZ):
        s = lax.rem(z + j, NZ)
        rcopy(ca.at[x, s], ca.at[x, s], zs.at[3, s], zr.at[3, s], seq_0=s).wait_recv()
    for d in range(1, NX):
        t = lax.rem(x + d, NX)
        rcopy(ca.at[x], ca.at[x], cs.at[t], cr.at[x], seq_1=t).start()
    relay(z)
    first = nearby(1)
    zarrive(0, first)
    zarrive(1, first)
    forward(first)
    for d in range(1, NX):
        s = lax.rem(x + d, NX)
        rcopy(ca.at[s], ca.at[s], cs.at[s], cr.at[s], seq_1=s).wait_recv()
    for d in range(1, NX):
        t = lax.rem(x + d, NX)
        rcopy(ca.at[x], ca.at[x], cs.at[t], cr.at[x], seq_1=t).wait_send()
    tally = jnp.zeros((8, 128), F32)
    for i in range(NX):
        for j in range(NZ):
            tally = tally + ca[i, j]
    st1, st2, st3 = tally[1:2, :1], tally[2:3, :1], tally[3:4, :1]
    lane = lax.broadcasted_iota(jnp.int32, (1, 128), 1)
    full = lambda d: tally[d:d + 1, :]
    low = jnp.where(lane == 0, 0.0, jnp.where(lane == 1, full(1), jnp.where(
        lane == 2, full(2), jnp.where(lane == 3, full(3), 1e9))))
    high = jnp.where(lane == 0, full(1), jnp.where(lane == 1, full(2), jnp.where(
        lane == 2, full(3), 1e9)))

    def dstart(i):
        return jnp.where(i >= st3, st3, jnp.where(i >= st2, st2, jnp.where(i >= st1, st1, 0.0)))

    def qpos(s):
        return (GRP * s + BLK * x).astype(F32) + iota((BLK, 1), 0)

    def absorb(n):
        a = nearby(n)
        o = pl.multiple_of(FRONT + GRP * a, 128)
        kk = ka[pl.ds(o, GRP), :]
        l = mm(wk2[0], kk, 1, 1) + mm(wk2[1], kk, 1, 1)
        for f in (0, HALF):
            lh = l[f:f + HALF]
            e = jnp.exp(lh - jnp.max(lh, axis=0, keepdims=True))
            pkT[f:f + HALF, pl.ds(o, GRP)] = e * (1.0 / jnp.sum(e, axis=0, keepdims=True))
        kpos = (GRP * a).astype(F32) + iota((GRP, 1), 0)
        ke[pl.ds(o, GRP), :] = jnp.where((kpos >= low) & (kpos < high), 1.0, 0.0).astype(BF)
        icol = qpos(a)
        miss = jnp.logical_not((icol >= low) & (icol < high)) & (lane < 4)
        qe[a] = jnp.where(miss, NEG, 0.0).astype(BF)
        jrow = (GRP * a).astype(F32) + iota((1, GRP), 1)
        s = mm(qa[a], kk, 1, 1)
        s = jnp.where((jrow <= icol) & (jrow >= dstart(icol)), s, NEG)
        m = jnp.max(s, axis=1, keepdims=True)
        p = jnp.exp2((s - m) * C2)
        ms[a] = m
        accs[a] = mm(p.astype(BF), with_ones(va[pl.ds(o, GRP), :]))

        def place(j):
            b = nearby(j)
            ge = (a - b + NZ) // NZ
            zq, zk = ge * a + (1 - ge) * b, ge * b + (1 - ge) * a
            return zq, pl.ds(pl.multiple_of(FRONT + GRP * zk, 128), GRP)

        def pairs(spots):
            scs = [mm(jnp.concatenate([qa[zq], qe[zq]], axis=1),
                      jnp.concatenate([ka[r, :], ke[r, :]], axis=1), 1, 1) for zq, r in spots]
            tops = [jnp.max(sc, axis=1, keepdims=True) for sc in scs]
            olds, news = [], []
            for (zq, _), top in zip(spots, tops):
                olds.append(ms[zq])
                news.append(jnp.maximum(olds[-1], top))
                ms[zq] = news[-1]
            sums = [mm(jnp.exp2((sc - mn) * C2).astype(BF), with_ones(va[r, :]))
                    for sc, mn, (_, r) in zip(scs, news, spots)]
            for (zq, _), mo, mn, add in zip(spots, olds, news, sums):
                accs[zq] = accs[zq] * jnp.exp2((mo - mn) * C2) + add

        @pl.when(lax.rem(n, 2) == 1)
        def _():
            pairs([place(n - 1)])

        def two(j, _):
            pairs([place(2 * j), place(2 * j + 1)])
            return 0
        lax.fori_loop(0, n // 2, two, 0)

    def step(n, _):
        s = nearby(n)
        zarrive(0, s)
        zarrive(1, s)
        forward(s)
        relay(nearby(n - 1))
        complete(nearby(n - 2))
        absorb(n - 2)
        zarrive(2, nearby(n - 1))
        return 0
    lax.fori_loop(2, NZ, step, 0)
    relay(nearby(NZ - 1))
    zarrive(2, nearby(NZ - 1))

    def late(n, _):
        complete(nearby(n))
        absorb(n)
        return 0
    lax.fori_loop(NZ - 2, NZ, late, 0)

    off = BLK * x + 64 * lax.rem(x, 2)
    run[...] = jnp.zeros_like(run)

    def local_row(s):
        return pl.multiple_of(GRP * s + off + GRP, 128)

    def group_mask(s):
        end = (GRP * s + off + GRP - FRONT).astype(F32)
        jg = end - GRP + iota((1, GRP), 1)
        tag = dstart(jnp.zeros((1, 1), F32) + (end - 1.0))
        return (jg >= tag) & (jg < end) & (jg >= 0.0), tag, end

    def states(s, _):
        r = local_row(s)
        mask, tag, end = group_mask(s)
        o = pl.multiple_of(r - GRP, 128)
        pg = jnp.where(mask, pkT[:, pl.ds(o, GRP)], 0.0).astype(BF)
        keep = jnp.where(tag < end - GRP, 1.0, 0.0)
        st = run[...] * keep + mm(pg, with_ones(va[pl.ds(o, GRP), :]))
        run[...] = st
        hi, lo = hilo(st)
        sts[s, 0] = hi
        sts[s, 1] = lo
        tb[s] = (accs[s][:, :128] / accs[s][:, 128:]).astype(BF)
        return 0
    lax.fori_loop(0, NZ, states, 0)

    dwq[...] = jnp.zeros_like(dwq)
    pls[...] = jnp.zeros_like(pls)
    dpT[...] = jnp.zeros_like(dpT)

    def send_out(i, t):
        return rcopy((tb, yb)[i].at[t], tr.at[i, z], os.at[i, t], orr.at[i, z], seq_0=t)

    def block(n, _):
        s = lax.rem(z + nth(NZ - 1 - n), NZ)

        @pl.when(n < NZ - 1)
        def _():
            send_out(0, s).start()

        @pl.when(n > 0)
        def _():
            send_out(1, lax.rem(z + nth(NZ - n), NZ)).start()
        r = local_row(s)
        q = qa[s]
        kl = ka[pl.ds(r, LOC), :]
        vl = with_ones(va[pl.ds(r, LOC), :])
        icol = qpos(s)
        dcol = dstart(icol)
        jrow = (GRP * s + off + GRP - FRONT).astype(F32) + iota((1, LOC), 1)
        same = jrow >= dcol
        sc = mm(q, kl, 1, 1)
        lq = mm(q, wq2[...])
        lq = lq[:, :128] + lq[:, 128:]
        ph = []
        for f in (0, HALF):
            lh = lq[:, f:f + HALF]
            e = jnp.exp(lh - jnp.max(lh, axis=1, keepdims=True))
            ph.append(e * (1.0 / jnp.sum(e, axis=1, keepdims=True)))
        pq = jnp.concatenate(ph, axis=1)
        pq_h, pq_l = hilo(pq)
        _, tag, end = group_mask(s)
        uses = jnp.where((dcol == tag) & (end > 0.0), 1.0, 0.0)
        sh, sl = sts[s, 0], sts[s, 1]
        sth = mm(pq_h, sh) + mm(pq_l, sh) + mm(pq_h, sl)
        swm = jnp.where(same & (jrow <= icol) & (jrow > icol - WINDOW), sc, NEG)
        a = jnp.exp2((swm - jnp.max(swm, axis=1, keepdims=True)) * C2)
        bey = same & (jrow <= icol - WINDOW)
        pl_T = pkT[:, pl.ds(r, LOC)].astype(BF)
        bb = jnp.where(bey, mm(pq_h, pl_T), 0.0)
        nd = mm((a + bb).astype(BF), vl) + uses * sth
        rden = 1.0 / nd[:, 128:]
        y = nd[:, :128] * rden
        yb[s] = y.astype(BF)
        e = y - tb[s].astype(F32)
        pls[...] += jnp.sum((e * e).reshape(BLK // 8, 8, 128), axis=0)
        gr_ = e * rden * (2.0 * norm)
        gx = jnp.concatenate([gr_, -gr_ * y], axis=1)
        gh, _ = hilo(gx)
        db = jnp.where(bey, mm(gh, vl, 1, 1), 0.0).astype(BF)
        guh, gul = hilo(gx * uses)
        dpq = mm(db, pl_T, 1, 1) + mm(guh, sh, 1, 1) + mm(gul, sh, 1, 1) + mm(guh, sl, 1, 1)
        dpT[:, pl.ds(r, LOC)] += mm(pq_h, db, 0, 0)
        dss[s] = mm(pq_h, guh, 0, 0)
        out = []
        for f in (0, HALF):
            pp, dd = pq[:, f:f + HALF], dpq[:, f:f + HALF]
            out.append(pp * (dd - jnp.sum(pp * dd, axis=1, keepdims=True)))
        dh, dlo = hilo(jnp.concatenate(out, axis=1))
        dwq[...] += mm(q, jnp.concatenate([dh, dlo], axis=1), 0, 0)
        return 0
    lax.fori_loop(0, NZ, block, 0)

    def lscatter(t):
        return rcopy(lx.at[x], lx.at[x], xs.at[1, t], xr.at[1, x], seq_1=t)

    def lspread(s, t):
        return rcopy(lz.at[s], lz.at[s], zs.at[5, t], zr.at[5, s], seq_0=t)
    lx[x] = pls[...] * norm
    for d in range(1, NX):
        lscatter(lax.rem(x + d, NX)).start()

    run[...] = jnp.zeros_like(run)

    def back(n, _):
        s = NZ - 1 - n
        o = pl.multiple_of(local_row(s) - GRP, 128)
        mask, tag, end = group_mask(s)
        keep = jnp.where(dstart(jnp.zeros((1, 1), F32) + (end + GRP - 1.0)) == tag, 1.0, 0.0)
        rr_ = run[...] * keep + dss[s]
        run[...] = rr_
        d = mm(rr_.astype(BF), with_ones(va[pl.ds(o, GRP), :]), 1, 1)
        dpT[:, pl.ds(o, GRP)] += jnp.where(mask, d, 0.0)
        return 0
    lax.fori_loop(0, NZ, back, 0)
    for d in range(1, NX):
        s = lax.rem(x + d, NX)
        rcopy(lx.at[s], lx.at[s], xs.at[1, s], xr.at[1, s], seq_1=s).wait_recv()
    lz[z] = (lx[0] + lx[1]) + (lx[2] + lx[3])
    for j in range(1, NZ):
        lspread(z, lax.rem(z + nth(j), NZ)).start()

    def fin(s, acc):
        o = pl.multiple_of(FRONT + GRP * s, 128)
        out = []
        for f in (0, HALF):
            pp, dd = pkT[f:f + HALF, pl.ds(o, GRP)], dpT[f:f + HALF, pl.ds(o, GRP)]
            out.append(pp * (dd - jnp.sum(pp * dd, axis=0, keepdims=True)))
        dh, dlo = hilo(jnp.concatenate(out, axis=0))
        kk = ka[pl.ds(o, GRP), :]
        return acc + mm(dh, kk) + mm(dlo, kk)
    dk = lax.fori_loop(0, NZ, fin, jnp.zeros((128, 128), F32)).T
    dq = dwq[:, :128] + dwq[:, 128:]
    dw = jnp.concatenate([dq[:, :HALF] - dq[:, HALF:], dk[:, :HALF] - dk[:, HALF:]], axis=1)
    dwb[...] = dw.reshape(NX, 32, 128)

    def scatter(t):
        return rcopy(dwb.at[t], wx.at[x], xs.at[0, t], xr.at[0, x], seq_1=t)

    def zspread(s, t):
        return rcopy(wg.at[x, s], wg.at[x, s], zs.at[4, t], zr.at[4, s], seq_0=t)
    for d in range(1, NX):
        scatter(lax.rem(x + d, NX)).start()
    wx[x] = dwb[x]
    for j in range(1, NZ):
        s = lax.rem(z + j, NZ)
        lspread(s, s).wait_recv()
    part = lz[0]
    for i in range(1, NZ):
        part = part + lz[i]
    mine = NX * g + h
    lc[mine] = part
    for peer in cols:
        there = NX * peer["grp"] + peer["head"]
        rcopy(lc.at[mine], lc.at[mine], gs.at[there], gr.at[mine], **peer).start()
    for d in range(1, NX):
        s = lax.rem(x + d, NX)
        rcopy(wx.at[s], wx.at[s], xs.at[0, s], xr.at[0, s], seq_1=s).wait_recv()
    wg[x, z] = ((wx[0] + wx[1]) + (wx[2] + wx[3])).astype(BF)
    for j in range(1, NZ):
        zspread(z, lax.rem(z + nth(j), NZ)).start()

    def land(i, src, dst):
        for j in range(1, NZ):
            s = lax.rem(z + j, NZ)
            rcopy(tr.at[i, s], tr.at[i, s], os.at[i, s], orr.at[i, s], seq_0=s).wait_recv()
        tr[i, z] = src[z]
        for d in range(NZ):
            flat[pl.ds(d, BLK, stride=NZ), :] = tr[i, d].astype(F32)
        dst[...] = flat[...].reshape(BLK, NZ, 128).astype(BF)
    land(0, tb, ta)
    for j in range(1, NZ):
        s = lax.rem(z + j, NZ)
        zspread(s, s).wait_recv()
    for d in range(1, NX):
        t = lax.rem(x + d, NX)
        rcopy(wg.at[x], wg.at[x], xs.at[2, t], xr.at[2, x], seq_1=t).start()
    land(1, yb, ya)
    for peer in cols:
        there = NX * peer["grp"] + peer["head"]
        rcopy(lc.at[there], lc.at[there], gs.at[there], gr.at[there], **peer).wait_recv()
    part = lc[0]
    for i in range(1, 8):
        part = part + lc[i]
    lout[...] = jnp.sum(jnp.sum(part, axis=0, keepdims=True), axis=1, keepdims=True)
    for d in range(1, NX):
        s = lax.rem(x + d, NX)
        rcopy(wg.at[s], wg.at[s], xs.at[2, s], xr.at[2, s], seq_1=s).wait_recv()
    for i in range(NX):
        wout[:, i] = wg[i].astype(F32)

    def drain(j, _):
        s = lax.rem(z + j, NZ)
        for i in range(2):
            send_out(i, s).wait_send()
        for i in range(3):
            zcopy(i, s).wait_send()
        count_copy(s).wait_send()
        zspread(z, s).wait_send()
        lspread(z, s).wait_send()
        return 0
    lax.fori_loop(1, NZ, drain, 0)

    def drain_x(s, _):
        for i in range(2):
            xcopy(i, s, x, right, rs, rr).wait_send()
            xcopy(i, s, x, left, ls_, lr).wait_send()
        xcopy(0, s, left, right, ys, yr).wait_send()
        xcopy(1, s, right, left, ys, yr).wait_send()
        return 0
    lax.fori_loop(0, NZ, drain_x, 0)
    for d in range(1, NX):
        t = lax.rem(x + d, NX)
        scatter(t).wait_send()
        lscatter(t).wait_send()
        rcopy(wg.at[x], wg.at[x], xs.at[2, t], xr.at[2, x], seq_1=t).wait_send()
    for peer in cols:
        there = NX * peer["grp"] + peer["head"]
        rcopy(lc.at[mine], lc.at[mine], gs.at[there], gr.at[mine], **peer).wait_send()


def whole(norm, q, k, v, docs, fm):
    M = pl.BlockSpec(memory_space=pltpu.VMEM)
    D, V = pltpu.SemaphoreType.DMA, pltpu.VMEM
    return pl.pallas_call(
        functools.partial(kernel, norm),
        out_shape=(jax.ShapeDtypeStruct((BLK, NZ, 128), BF),
                   jax.ShapeDtypeStruct((BLK, NZ, 128), BF),
                   jax.ShapeDtypeStruct((NZ, NX, 32, 128), F32),
                   jax.ShapeDtypeStruct((1, 1), F32)),
        in_specs=[M] * 5, out_specs=(M,) * 4,
        scratch_shapes=[
            V((BLK * NZ, 128), F32), V((3, NZ, BLK, 128), BF), V((2, NZ, BLK, 128), BF),
            V((NZ, BLK, 128), BF), V((ROWS, 128), BF), V((ROWS, 128), BF), V((NX, NZ, 8, 128), F32),
            V((NZ, BLK, 128), BF), V((ROWS, 128), BF), V((128, 256), BF), V((2, 128, 128), BF),
            V((128, ROWS), F32), V((128, ROWS), F32),
            V((NZ, BLK, 1), F32), V((NZ, BLK, 256), F32), V((NZ, BLK, 128), BF), V((NZ, BLK, 128), BF),
            V((NZ, 2, 128, 256), BF), V((NZ, 128, 256), F32), V((128, 256), F32), V((128, 256), F32),
            V((8, 128), F32),
            V((NX, 32, 128), F32), V((NX, 32, 128), F32), V((NX, NZ, 32, 128), BF),
            V((NX, 8, 128), F32), V((NZ, 8, 128), F32), V((8, 8, 128), F32),
            D((3,)), D((6, NZ)), D((6, NZ)), D((2, NZ)), D((2, NZ)), D((2, NZ)), D((2, NZ)),
            D((2, NZ)), D((2, NZ)), D((NX,)), D((NX,)), D((3, NX)), D((3, NX)), D((8,)), D((8,)),
            D((2, NZ)), D((2, NZ))],
        compiler_params=pltpu.CompilerParams(
            collective_id=0, has_side_effects=True, vmem_limit_bytes=60 << 20),
    )(q, k, v, docs, fm)


def body(queries, keys, values, documents, feature_map):
    norm = 1.0 / (TOKENS * 64)
    ta, ya, wa, la = whole(norm, queries, keys, values, documents.reshape(1, BLK), feature_map)
    return (ta, ya, la.reshape(()), wa.reshape(NZ, 128, 128))


def solution(mesh):
    split = Mesh(
        mesh.devices.reshape(mesh.shape["grp"], 8, 4, mesh.shape["head"]),
        ("grp", "seq_0", "seq_1", "head"),
    )
    return jax.shard_map(
        body,
        mesh=split,
        in_specs=(
            P(SEQ, ("grp", "head"), None),
            P(SEQ, ("grp", "head"), None),
            P(SEQ, ("grp", "head"), None),
            P(SEQ),
            P(("grp", "head"), None, None),
        ),
        out_specs=(
            P(SEQ, ("grp", "head"), None),
            P(SEQ, ("grp", "head"), None),
            P(),
            P(("grp", "head"), None, None),
        ),
        check_vma=False,
    )
```

```python
import functools
import math

import jax
import jax.numpy as jnp
from jax import lax
from jax.experimental import pallas as pl
from jax.experimental.pallas import tpu as pltpu
from jax.sharding import Mesh
from jax.sharding import PartitionSpec as P

SEQ = ("seq_0", "seq_1")
MESH = pl.DeviceIdType.MESH

TOKENS, BLK, WINDOW, LOC, GRP, HALF = 6144, 192, 64, 384, 768, 64
NZ, NX = 8, 4
FRONT = 896
ROWS = FRONT + TOKENS + 128
F32, BF = jnp.float32, jnp.bfloat16
NEG = -1e30
SCALE = 128**-0.5
C2 = SCALE * math.log2(math.e)


def mm(a, b, ca=1, cb=0):
    return lax.dot_general(a, b, (((ca,), (cb,)), ((), ())), preferred_element_type=F32)


def hilo(a):
    hi = a.astype(BF)
    return hi, (a - hi.astype(F32)).astype(BF)


def rcopy(src, dst, ssem, rsem, **where):
    return pltpu.make_async_remote_copy(
        src_ref=src, dst_ref=dst, send_sem=ssem, recv_sem=rsem,
        device_id=where, device_id_type=MESH)


def nth(j):
    odd = lax.rem(j, 2)
    return lax.rem(odd * ((j + 1) // 2) + (1 - odd) * (NZ - j // 2), NZ)


def with_ones(v):
    return jnp.concatenate([v, jnp.ones_like(v)], axis=1)


def iota(shape, dim):
    return lax.broadcasted_iota(jnp.int32, shape, dim).astype(F32)


def kernel(norm, q_ref, k_ref, v_ref, doc_ref, fm_ref, ta, ya, wout, lout,
           flat, out3, tr, qa, ka, va, ca, qe, kT, vT, wq2, wk2, pkT, dpT, ms, accs, tb, yb, sts, dss, run, dwq, pls,
           dwb, wx, wg, lx, lz, lc,
           own, zs, zr, rs, rr, ls_, lr, ys, yr, cs, cr, xs, xr, gs, gr, os, orr):
    z, x = lax.axis_index("seq_0"), lax.axis_index("seq_1")
    h, g = lax.axis_index("head"), lax.axis_index("grp")
    right, left, far = lax.rem(x + 1, NX), lax.rem(x + 3, NX), lax.rem(x + 2, NX)
    cols = [{"grp": lax.rem(g + (d // NX), 2), "head": lax.rem(h + d % NX, NX)} for d in range(1, 8)]

    everyone = ([{"seq_0": lax.rem(z + d, NZ)} for d in range(1, NZ)]
                + [{"seq_1": lax.rem(x + d, NX)} for d in range(1, NX)] + cols)
    barrier = pltpu.get_barrier_semaphore()
    for peer in everyone:
        pl.semaphore_signal(barrier, inc=1, device_id=peer, device_id_type=MESH)

    for i, ref in enumerate((k_ref, v_ref, q_ref)):
        flat[...] = ref[...].astype(F32).reshape(BLK * NZ, 128)
        for d in range(NZ):
            out3[i, d] = flat[pl.ds(d, BLK, stride=NZ), :].astype(BF)

    docs = doc_ref[...]
    row = lax.broadcasted_iota(jnp.int32, (8, 128), 0)
    tile = jnp.zeros((8, 128), F32)
    for d in (1, 2, 3):
        n = jnp.sum((docs < d).astype(F32), axis=1, keepdims=True)
        tile = tile + jnp.where(row == d, jnp.broadcast_to(n, (8, 128)), 0.0)
    ca[x, z] = tile
    zero = jnp.zeros((FRONT, 128), BF)
    for ref in (ka, va):
        ref[:FRONT] = zero
        ref[FRONT + TOKENS:] = zero[:128]
    vT[:, :FRONT] = jnp.zeros((128, FRONT), BF)
    vT[:, FRONT + TOKENS:] = jnp.zeros((128, 128), BF)
    dpT[...] = jnp.zeros_like(dpT)
    pkT[:, :FRONT] = jnp.zeros((128, FRONT), F32)
    pkT[:, FRONT + TOKENS:] = jnp.zeros((128, 128), F32)
    w = fm_ref[z]
    wqh, wql = hilo(jnp.concatenate([w[:, :HALF], -w[:, :HALF]], axis=1))
    wq2[...] = jnp.concatenate([wqh, wql], axis=1)
    wkh, wkl = hilo(jnp.concatenate([w[:, HALF:], -w[:, HALF:]], axis=1).T)
    wk2[0] = wkh
    wk2[1] = wkl

    pl.semaphore_wait(barrier, len(everyone))

    def krows(arr, s, col):
        return arr.at[pl.ds(pl.multiple_of(FRONT + GRP * s + BLK * col, 64), BLK)]

    def zcopy(i, t):
        src = out3.at[i, t]
        dst = qa.at[z] if i == 2 else krows((ka, va)[i], z, x)
        return rcopy(src, dst, zs.at[i, t], zr.at[i, z], seq_0=t)

    def zarrive(i, s):
        dst = qa.at[s] if i == 2 else krows((ka, va)[i], s, x)
        rcopy(dst, dst, zs.at[i, s], zr.at[i, s], seq_0=s).wait_recv()

    def count_copy(t):
        return rcopy(ca.at[x, z], ca.at[x, z], zs.at[3, t], zr.at[3, z], seq_0=t)

    def xcopy(i, s, col, to, sems, semr):
        ref = krows((ka, va)[i], s, col)
        return rcopy(ref, ref, sems.at[i, s], semr.at[i, s], seq_1=to)

    local = [pltpu.make_async_copy(out3.at[0, z], krows(ka, z, x), own.at[0]),
             pltpu.make_async_copy(out3.at[1, z], krows(va, z, x), own.at[1]),
             pltpu.make_async_copy(out3.at[2, z], qa.at[z], own.at[2])]
    for c in local:
        c.start()
    for j in range(1, NZ):
        count_copy(lax.rem(z + nth(j), NZ)).start()

    def target(j):
        return lax.rem(z + NZ - nth(j), NZ)

    def send_all(j, _):
        zcopy(0, target(j)).start()
        zcopy(1, target(j)).start()

        @pl.when(j > 1)
        def _():
            zcopy(2, target(j - 1)).start()
        return 0
    lax.fori_loop(1, NZ, send_all, 0)
    zcopy(2, target(NZ - 1)).start()
    for c in local:
        c.wait()

    def forward(s):
        for i in range(2):
            xcopy(i, s, x, right, rs, rr).start()
            xcopy(i, s, x, left, ls_, lr).start()

    def relay(s):
        xcopy(0, s, left, right, rs, rr).wait_recv()
        xcopy(0, s, left, right, ys, yr).start()
        xcopy(1, s, right, left, ls_, lr).wait_recv()
        xcopy(1, s, right, left, ys, yr).start()

    def complete(s):
        xcopy(1, s, left, right, rs, rr).wait_recv()
        xcopy(0, s, right, left, ls_, lr).wait_recv()
        xcopy(0, s, far, right, ys, yr).wait_recv()
        xcopy(1, s, far, left, ys, yr).wait_recv()

    def nearby(n):
        return lax.rem(z + nth(n), NZ)

    forward(z)
    for n in (1, 2):
        zarrive(0, nearby(n))
        zarrive(1, nearby(n))
        forward(nearby(n))
        relay(nearby(n - 1))
        if n == 1:
            for j in range(1, NZ):
                s = lax.rem(z + j, NZ)
                rcopy(ca.at[x, s], ca.at[x, s], zs.at[3, s], zr.at[3, s], seq_0=s).wait_recv()
            for d in range(1, NX):
                t = lax.rem(x + d, NX)
                rcopy(ca.at[x], ca.at[x], cs.at[t], cr.at[x], seq_1=t).start()
    for d in range(1, NX):
        s = lax.rem(x + d, NX)
        rcopy(ca.at[s], ca.at[s], cs.at[s], cr.at[s], seq_1=s).wait_recv()
    for d in range(1, NX):
        t = lax.rem(x + d, NX)
        rcopy(ca.at[x], ca.at[x], cs.at[t], cr.at[x], seq_1=t).wait_send()
    tally = jnp.zeros((8, 128), F32)
    for i in range(NX):
        for j in range(NZ):
            tally = tally + ca[i, j]
    st1, st2, st3 = tally[1:2, :1], tally[2:3, :1], tally[3:4, :1]
    lane = lax.broadcasted_iota(jnp.int32, (1, 128), 1)
    full = lambda d: tally[d:d + 1, :]
    low = jnp.where(lane == 0, 0.0, jnp.where(lane == 1, full(1), jnp.where(
        lane == 2, full(2), jnp.where(lane == 3, full(3), 1e9))))
    high = jnp.where(lane == 0, full(1), jnp.where(lane == 1, full(2), jnp.where(
        lane == 2, full(3), 1e9)))

    sub = lax.broadcasted_iota(jnp.int32, (128, 1), 0)
    low_col = jnp.where(sub == 0, 0.0, jnp.where(sub == 1, st1, jnp.where(
        sub == 2, st2, jnp.where(sub == 3, st3, 1e9))))
    high_col = jnp.where(sub == 0, st1, jnp.where(sub == 1, st2, jnp.where(sub == 2, st3, 1e9)))

    def dstart(i):
        return jnp.where(i >= st3, st3, jnp.where(i >= st2, st2, jnp.where(i >= st1, st1, 0.0)))

    def qpos(s):
        return (GRP * s + BLK * x).astype(F32) + iota((BLK, 1), 0)

    def absorb(n):
        a = nearby(n)
        o = pl.multiple_of(FRONT + GRP * a, 128)
        kk = ka[pl.ds(o, GRP), :].T
        kT[:128, pl.ds(o, GRP)] = kk
        vT[:, pl.ds(o, GRP)] = va[pl.ds(o, GRP), :].T
        l = mm(wk2[0], kk) + mm(wk2[1], kk)
        for f in (0, HALF):
            lh = l[f:f + HALF]
            e = jnp.exp(lh - jnp.max(lh, axis=0, keepdims=True))
            pkT[f:f + HALF, pl.ds(o, GRP)] = e * (1.0 / jnp.sum(e, axis=0, keepdims=True))
        kpos = (GRP * a).astype(F32) + iota((1, GRP), 1)
        kT[128:, pl.ds(o, GRP)] = jnp.where((kpos >= low_col) & (kpos < high_col), 1.0, 0.0).astype(BF)
        icol = qpos(a)
        miss = jnp.logical_not((icol >= low) & (icol < high)) & (lane < 4)
        qe[a] = jnp.where(miss, NEG, 0.0).astype(BF)
        jrow = (GRP * a).astype(F32) + iota((1, GRP), 1)
        s = mm(qa[a], kk)
        s = jnp.where((jrow <= icol) & (jrow >= dstart(icol)), s, NEG)
        m = jnp.max(s, axis=1, keepdims=True)
        p = jnp.exp2((s - m) * C2)
        ms[a] = m
        accs[a] = mm(p.astype(BF), with_ones(va[pl.ds(o, GRP), :]))

        def place(j):
            b = nearby(j)
            ge = (a - b + NZ) // NZ
            zq, zk = ge * a + (1 - ge) * b, ge * b + (1 - ge) * a
            return zq, pl.ds(pl.multiple_of(FRONT + GRP * zk, 128), GRP)

        def pairs(spots):
            scs = [mm(jnp.concatenate([qa[zq], qe[zq]], axis=1),
                      kT[:, r]) for zq, r in spots]
            tops = [jnp.max(sc, axis=1, keepdims=True) for sc in scs]
            olds, news = [], []
            for (zq, _), top in zip(spots, tops):
                olds.append(ms[zq])
                news.append(jnp.maximum(olds[-1], top))
                ms[zq] = news[-1]
            sums = [mm(jnp.exp2((sc - mn) * C2).astype(BF), with_ones(va[r, :]))
                    for sc, mn, (_, r) in zip(scs, news, spots)]
            for (zq, _), mo, mn, add in zip(spots, olds, news, sums):
                accs[zq] = accs[zq] * jnp.exp2((mo - mn) * C2) + add

        @pl.when(lax.rem(n, 2) == 1)
        def _():
            pairs([place(n - 1)])

        def two(j, _):
            pairs([place(2 * j), place(2 * j + 1)])
            return 0
        lax.fori_loop(0, n // 2, two, 0)

    def step(n, _):
        complete(nearby(n - 2))
        absorb(n - 2)
        s = nearby(n + 1)
        zarrive(0, s)
        zarrive(1, s)
        forward(s)
        relay(nearby(n))
        zarrive(2, nearby(n - 1))
        return 0
    lax.fori_loop(2, NZ - 1, step, 0)

    def late(n, _):
        @pl.when(n > NZ - 3)
        def _():
            zarrive(2, nearby(n))
        complete(nearby(n))
        absorb(n)

        @pl.when(n == NZ - 3)
        def _():
            relay(nearby(NZ - 1))
        return 0
    lax.fori_loop(NZ - 3, NZ, late, 0)

    off = BLK * x + 64 * lax.rem(x, 2)
    run[...] = jnp.zeros_like(run)

    def local_row(s):
        return pl.multiple_of(GRP * s + off + GRP, 128)

    def group_mask(s):
        end = (GRP * s + off + GRP - FRONT).astype(F32)
        jg = end - GRP + iota((1, GRP), 1)
        tag = dstart(jnp.zeros((1, 1), F32) + (end - 1.0))
        return (jg >= tag) & (jg < end) & (jg >= 0.0), tag, end

    def states(s, _):
        r = local_row(s)
        mask, tag, end = group_mask(s)
        o = pl.multiple_of(r - GRP, 128)
        pg = jnp.where(mask, pkT[:, pl.ds(o, GRP)], 0.0).astype(BF)
        keep = jnp.where(tag < end - GRP, 1.0, 0.0)
        st = run[...] * keep + mm(pg, with_ones(va[pl.ds(o, GRP), :]))
        run[...] = st
        hi, lo = hilo(st)
        sts[s, 0] = hi
        sts[s, 1] = lo
        tb[s] = (accs[s][:, :128] / accs[s][:, 128:]).astype(BF)
        return 0
    lax.fori_loop(0, NZ, states, 0)

    dwq[...] = jnp.zeros_like(dwq)
    pls[...] = jnp.zeros_like(pls)

    def send_out(i, t):
        return rcopy((tb, yb)[i].at[t], tr.at[i, z], os.at[i, t], orr.at[i, z], seq_0=t)

    def block(n, _):
        s = lax.rem(z + nth(NZ - 1 - n), NZ)

        @pl.when(n < NZ - 1)
        def _():
            send_out(0, s).start()

        @pl.when(n > 0)
        def _():
            send_out(1, lax.rem(z + nth(NZ - n), NZ)).start()
        r = local_row(s)
        q = qa[s]
        kl = ka[pl.ds(r, LOC), :]
        vl = with_ones(va[pl.ds(r, LOC), :])
        icol = qpos(s)
        dcol = dstart(icol)
        jrow = (GRP * s + off + GRP - FRONT).astype(F32) + iota((1, LOC), 1)
        same = jrow >= dcol
        sc = mm(q, kl, 1, 1)
        lq = mm(q, wq2[...])
        lq = lq[:, :128] + lq[:, 128:]
        ph = []
        for f in (0, HALF):
            lh = lq[:, f:f + HALF]
            e = jnp.exp(lh - jnp.max(lh, axis=1, keepdims=True))
            ph.append(e * (1.0 / jnp.sum(e, axis=1, keepdims=True)))
        pq = jnp.concatenate(ph, axis=1)
        pq_h, pq_l = hilo(pq)
        _, tag, end = group_mask(s)
        uses = jnp.where((dcol == tag) & (end > 0.0), 1.0, 0.0)
        sh, sl = sts[s, 0], sts[s, 1]
        sth = mm(pq_h, sh) + mm(pq_l, sh) + mm(pq_h, sl)
        swm = jnp.where(same & (jrow <= icol) & (jrow > icol - WINDOW), sc, NEG)
        a = jnp.exp2((swm - jnp.max(swm, axis=1, keepdims=True)) * C2)
        bey = same & (jrow <= icol - WINDOW)
        pl_T = pkT[:, pl.ds(r, LOC)].astype(BF)
        bb = jnp.where(bey, mm(pq_h, pl_T), 0.0)
        nd = mm((a + bb).astype(BF), vl) + uses * sth
        rden = 1.0 / nd[:, 128:]
        y = nd[:, :128] * rden
        yb[s] = y.astype(BF)
        e = y - tb[s].astype(F32)
        pls[...] += jnp.sum((e * e).reshape(BLK // 8, 8, 128), axis=0)
        gr_ = e * rden * (2.0 * norm)
        gx = jnp.concatenate([gr_, -gr_ * y], axis=1)
        gh, _ = hilo(gx)
        db = jnp.where(bey, mm(gh, vl, 1, 1), 0.0).astype(BF)
        guh, gul = hilo(gx * uses)
        dpq = mm(db, pl_T, 1, 1) + mm(guh, sh, 1, 1) + mm(gul, sh, 1, 1) + mm(guh, sl, 1, 1)
        dpT[:, pl.ds(r, LOC)] += mm(pq_h, db, 0, 0)
        dss[s] = mm(pq_h, guh, 0, 0)
        out = []
        for f in (0, HALF):
            pp, dd = pq[:, f:f + HALF], dpq[:, f:f + HALF]
            out.append(pp * (dd - jnp.sum(pp * dd, axis=1, keepdims=True)))
        dh, dlo = hilo(jnp.concatenate(out, axis=1))
        dwq[...] += mm(q, jnp.concatenate([dh, dlo], axis=1), 0, 0)
        return 0
    lax.fori_loop(0, NZ, block, 0)

    def lscatter(t):
        return rcopy(lx.at[x], lx.at[x], xs.at[1, t], xr.at[1, x], seq_1=t)

    def lspread(s, t):
        return rcopy(lz.at[s], lz.at[s], zs.at[5, t], zr.at[5, s], seq_0=t)
    lx[x] = pls[...] * norm
    for d in range(1, NX):
        lscatter(lax.rem(x + d, NX)).start()

    run[...] = jnp.zeros_like(run)

    def back(n, _):
        s = NZ - 1 - n
        o = pl.multiple_of(local_row(s) - GRP, 128)
        mask, tag, end = group_mask(s)
        keep = jnp.where(dstart(jnp.zeros((1, 1), F32) + (end + GRP - 1.0)) == tag, 1.0, 0.0)
        rr_ = run[...] * keep + dss[s]
        run[...] = rr_
        d = mm(rr_.astype(BF), jnp.concatenate([vT[:, pl.ds(o, GRP)], jnp.ones((128, GRP), BF)], axis=0))
        dpT[:, pl.ds(o, GRP)] += jnp.where(mask, d, 0.0)
        return 0
    lax.fori_loop(0, NZ, back, 0)
    for d in range(1, NX):
        s = lax.rem(x + d, NX)
        rcopy(lx.at[s], lx.at[s], xs.at[1, s], xr.at[1, s], seq_1=s).wait_recv()
    lz[z] = (lx[0] + lx[1]) + (lx[2] + lx[3])
    for j in range(1, NZ):
        lspread(z, lax.rem(z + nth(j), NZ)).start()

    def fin(s, acc):
        o = pl.multiple_of(FRONT + GRP * s, 128)
        out = []
        for f in (0, HALF):
            pp, dd = pkT[f:f + HALF, pl.ds(o, GRP)], dpT[f:f + HALF, pl.ds(o, GRP)]
            out.append(pp * (dd - jnp.sum(pp * dd, axis=0, keepdims=True)))
        dh, dlo = hilo(jnp.concatenate(out, axis=0))
        kk = ka[pl.ds(o, GRP), :]
        return acc + mm(dh, kk) + mm(dlo, kk)
    dk = lax.fori_loop(0, NZ, fin, jnp.zeros((128, 128), F32)).T
    dq = dwq[:, :128] + dwq[:, 128:]
    dw = jnp.concatenate([dq[:, :HALF] - dq[:, HALF:], dk[:, :HALF] - dk[:, HALF:]], axis=1)
    dwb[...] = dw.reshape(NX, 32, 128)

    def scatter(t):
        return rcopy(dwb.at[t], wx.at[x], xs.at[0, t], xr.at[0, x], seq_1=t)

    def zspread(s, t):
        return rcopy(wg.at[x, s], wg.at[x, s], zs.at[4, t], zr.at[4, s], seq_0=t)
    for d in range(1, NX):
        scatter(lax.rem(x + d, NX)).start()
    wx[x] = dwb[x]
    for j in range(1, NZ):
        s = lax.rem(z + j, NZ)
        lspread(s, s).wait_recv()
    part = lz[0]
    for i in range(1, NZ):
        part = part + lz[i]
    mine = NX * g + h
    lc[mine] = part
    for peer in cols:
        there = NX * peer["grp"] + peer["head"]
        rcopy(lc.at[mine], lc.at[mine], gs.at[there], gr.at[mine], **peer).start()
    for d in range(1, NX):
        s = lax.rem(x + d, NX)
        rcopy(wx.at[s], wx.at[s], xs.at[0, s], xr.at[0, s], seq_1=s).wait_recv()
    wg[x, z] = ((wx[0] + wx[1]) + (wx[2] + wx[3])).astype(BF)
    for j in range(1, NZ):
        zspread(z, lax.rem(z + nth(j), NZ)).start()

    def land(i, src, dst):
        for j in range(1, NZ):
            s = lax.rem(z + j, NZ)
            rcopy(tr.at[i, s], tr.at[i, s], os.at[i, s], orr.at[i, s], seq_0=s).wait_recv()
        tr[i, z] = src[z]
        for d in range(NZ):
            flat[pl.ds(d, BLK, stride=NZ), :] = tr[i, d].astype(F32)
        dst[...] = flat[...].reshape(BLK, NZ, 128).astype(BF)
    land(0, tb, ta)
    for j in range(1, NZ):
        s = lax.rem(z + j, NZ)
        zspread(s, s).wait_recv()
    for d in range(1, NX):
        t = lax.rem(x + d, NX)
        rcopy(wg.at[x], wg.at[x], xs.at[2, t], xr.at[2, x], seq_1=t).start()
    land(1, yb, ya)
    for peer in cols:
        there = NX * peer["grp"] + peer["head"]
        rcopy(lc.at[there], lc.at[there], gs.at[there], gr.at[there], **peer).wait_recv()
    part = lc[0]
    for i in range(1, 8):
        part = part + lc[i]
    lout[...] = jnp.sum(jnp.sum(part, axis=0, keepdims=True), axis=1, keepdims=True)
    for d in range(1, NX):
        s = lax.rem(x + d, NX)
        rcopy(wg.at[s], wg.at[s], xs.at[2, s], xr.at[2, s], seq_1=s).wait_recv()
    for i in range(NX):
        wout[:, i] = wg[i].astype(F32)

    def drain(j, _):
        s = lax.rem(z + j, NZ)
        for i in range(2):
            send_out(i, s).wait_send()
        for i in range(3):
            zcopy(i, s).wait_send()
        count_copy(s).wait_send()
        zspread(z, s).wait_send()
        lspread(z, s).wait_send()
        return 0
    lax.fori_loop(1, NZ, drain, 0)

    def drain_x(s, _):
        for i in range(2):
            xcopy(i, s, x, right, rs, rr).wait_send()
            xcopy(i, s, x, left, ls_, lr).wait_send()
        xcopy(0, s, left, right, ys, yr).wait_send()
        xcopy(1, s, right, left, ys, yr).wait_send()
        return 0
    lax.fori_loop(0, NZ, drain_x, 0)
    for d in range(1, NX):
        t = lax.rem(x + d, NX)
        scatter(t).wait_send()
        lscatter(t).wait_send()
        rcopy(wg.at[x], wg.at[x], xs.at[2, t], xr.at[2, x], seq_1=t).wait_send()
    for peer in cols:
        there = NX * peer["grp"] + peer["head"]
        rcopy(lc.at[mine], lc.at[mine], gs.at[there], gr.at[mine], **peer).wait_send()


def whole(norm, q, k, v, docs, fm):
    M = pl.BlockSpec(memory_space=pltpu.VMEM)
    D, V = pltpu.SemaphoreType.DMA, pltpu.VMEM
    return pl.pallas_call(
        functools.partial(kernel, norm),
        out_shape=(jax.ShapeDtypeStruct((BLK, NZ, 128), BF),
                   jax.ShapeDtypeStruct((BLK, NZ, 128), BF),
                   jax.ShapeDtypeStruct((NZ, NX, 32, 128), F32),
                   jax.ShapeDtypeStruct((1, 1), F32)),
        in_specs=[M] * 5, out_specs=(M,) * 4,
        scratch_shapes=[
            V((BLK * NZ, 128), F32), V((3, NZ, BLK, 128), BF), V((2, NZ, BLK, 128), BF),
            V((NZ, BLK, 128), BF), V((ROWS, 128), BF), V((ROWS, 128), BF), V((NX, NZ, 8, 128), F32),
            V((NZ, BLK, 128), BF), V((256, ROWS), BF), V((128, ROWS), BF), V((128, 256), BF), V((2, 128, 128), BF),
            V((128, ROWS), F32), V((128, ROWS), F32),
            V((NZ, BLK, 1), F32), V((NZ, BLK, 256), F32), V((NZ, BLK, 128), BF), V((NZ, BLK, 128), BF),
            V((NZ, 2, 128, 256), BF), V((NZ, 128, 256), F32), V((128, 256), F32), V((128, 256), F32),
            V((8, 128), F32),
            V((NX, 32, 128), F32), V((NX, 32, 128), F32), V((NX, NZ, 32, 128), BF),
            V((NX, 8, 128), F32), V((NZ, 8, 128), F32), V((8, 8, 128), F32),
            D((3,)), D((6, NZ)), D((6, NZ)), D((2, NZ)), D((2, NZ)), D((2, NZ)), D((2, NZ)),
            D((2, NZ)), D((2, NZ)), D((NX,)), D((NX,)), D((3, NX)), D((3, NX)), D((8,)), D((8,)),
            D((2, NZ)), D((2, NZ))],
        compiler_params=pltpu.CompilerParams(
            collective_id=0, has_side_effects=True, vmem_limit_bytes=60 << 20),
    )(q, k, v, docs, fm)


def body(queries, keys, values, documents, feature_map):
    norm = 1.0 / (TOKENS * 64)
    ta, ya, wa, la = whole(norm, queries, keys, values, documents.reshape(1, BLK), feature_map)
    return (ta, ya, la.reshape(()), wa.reshape(NZ, 128, 128))


def solution(mesh):
    split = Mesh(
        mesh.devices.reshape(mesh.shape["grp"], 8, 4, mesh.shape["head"]),
        ("grp", "seq_0", "seq_1", "head"),
    )
    return jax.shard_map(
        body,
        mesh=split,
        in_specs=(
            P(SEQ, ("grp", "head"), None),
            P(SEQ, ("grp", "head"), None),
            P(SEQ, ("grp", "head"), None),
            P(SEQ),
            P(("grp", "head"), None, None),
        ),
        out_specs=(
            P(SEQ, ("grp", "head"), None),
            P(SEQ, ("grp", "head"), None),
            P(),
            P(("grp", "head"), None, None),
        ),
        check_vma=False,
    )
```

```python
import functools
import math

import jax
import jax.numpy as jnp
from jax import lax
from jax.experimental import pallas as pl
from jax.experimental.pallas import tpu as pltpu
from jax.sharding import Mesh
from jax.sharding import PartitionSpec as P

SEQ = ("seq_0", "seq_1")
MESH = pl.DeviceIdType.MESH

TOKENS, BLK, WINDOW, LOC, GRP, HALF = 6144, 192, 64, 384, 768, 64
NZ, NX = 8, 4
FRONT = 896
ROWS = FRONT + TOKENS + 128
F32, BF = jnp.float32, jnp.bfloat16
NEG = -1e30
SCALE = 128**-0.5
C2 = SCALE * math.log2(math.e)


def mm(a, b, ca=1, cb=0):
    return lax.dot_general(a, b, (((ca,), (cb,)), ((), ())), preferred_element_type=F32)


def hilo(a):
    hi = a.astype(BF)
    return hi, (a - hi.astype(F32)).astype(BF)


def rcopy(src, dst, ssem, rsem, **where):
    return pltpu.make_async_remote_copy(
        src_ref=src, dst_ref=dst, send_sem=ssem, recv_sem=rsem,
        device_id=where, device_id_type=MESH)


def nth(j):
    odd = lax.rem(j, 2)
    return lax.rem(odd * ((j + 1) // 2) + (1 - odd) * (NZ - j // 2), NZ)


def with_ones(v):
    return jnp.concatenate([v, jnp.ones_like(v)], axis=1)


def iota(shape, dim):
    return lax.broadcasted_iota(jnp.int32, shape, dim).astype(F32)


def kernel(norm, q_ref, k_ref, v_ref, doc_ref, fm_ref, ta, ya, wout, lout,
           flat, out3, tr, qa, ka, va, ca, qe, kT, vT, wq2, wk2, pkT, dpT, ms, accs, tb, yb, sts, dss, run, dwq, pls,
           dwb, wx, wg, lx, lz, lc,
           own, zs, zr, rs, rr, ls_, lr, ys, yr, cs, cr, xs, xr, gs, gr, os, orr):
    z, x = lax.axis_index("seq_0"), lax.axis_index("seq_1")
    h, g = lax.axis_index("head"), lax.axis_index("grp")
    right, left, far = lax.rem(x + 1, NX), lax.rem(x + 3, NX), lax.rem(x + 2, NX)
    cols = [{"grp": lax.rem(g + (d // NX), 2), "head": lax.rem(h + d % NX, NX)} for d in range(1, 8)]

    everyone = ([{"seq_0": lax.rem(z + d, NZ)} for d in range(1, NZ)]
                + [{"seq_1": lax.rem(x + d, NX)} for d in range(1, NX)] + cols)
    barrier = pltpu.get_barrier_semaphore()
    for peer in everyone:
        pl.semaphore_signal(barrier, inc=1, device_id=peer, device_id_type=MESH)

    for i, ref in enumerate((k_ref, v_ref, q_ref)):
        flat[...] = ref[...].astype(F32).reshape(BLK * NZ, 128)
        for d in range(NZ):
            out3[i, d] = flat[pl.ds(d, BLK, stride=NZ), :].astype(BF)

    docs = doc_ref[...]
    row = lax.broadcasted_iota(jnp.int32, (8, 128), 0)
    tile = jnp.zeros((8, 128), F32)
    for d in (1, 2, 3):
        n = jnp.sum((docs < d).astype(F32), axis=1, keepdims=True)
        tile = tile + jnp.where(row == d, jnp.broadcast_to(n, (8, 128)), 0.0)
    ca[x, z] = tile
    zero = jnp.zeros((FRONT, 128), BF)
    for ref in (ka, va):
        ref[:FRONT] = zero
        ref[FRONT + TOKENS:] = zero[:128]
    vT[:, :FRONT] = jnp.zeros((128, FRONT), BF)
    vT[:, FRONT + TOKENS:] = jnp.zeros((128, 128), BF)
    dpT[...] = jnp.zeros_like(dpT)
    pkT[:, :FRONT] = jnp.zeros((128, FRONT), F32)
    pkT[:, FRONT + TOKENS:] = jnp.zeros((128, 128), F32)
    w = fm_ref[z]
    wqh, wql = hilo(jnp.concatenate([w[:, :HALF], -w[:, :HALF]], axis=1))
    wq2[...] = jnp.concatenate([wqh, wql], axis=1)
    wkh, wkl = hilo(jnp.concatenate([w[:, HALF:], -w[:, HALF:]], axis=1).T)
    wk2[0] = wkh
    wk2[1] = wkl

    pl.semaphore_wait(barrier, len(everyone))

    def krows(arr, s, col):
        return arr.at[pl.ds(pl.multiple_of(FRONT + GRP * s + BLK * col, 64), BLK)]

    def zcopy(i, t):
        src = out3.at[i, t]
        dst = qa.at[z] if i == 2 else krows((ka, va)[i], z, x)
        return rcopy(src, dst, zs.at[i, t], zr.at[i, z], seq_0=t)

    def zarrive(i, s):
        dst = qa.at[s] if i == 2 else krows((ka, va)[i], s, x)
        rcopy(dst, dst, zs.at[i, s], zr.at[i, s], seq_0=s).wait_recv()

    def count_copy(t):
        return rcopy(ca.at[x, z], ca.at[x, z], zs.at[3, t], zr.at[3, z], seq_0=t)

    def xcopy(i, s, col, to, sems, semr):
        ref = krows((ka, va)[i], s, col)
        return rcopy(ref, ref, sems.at[i, s], semr.at[i, s], seq_1=to)

    local = [pltpu.make_async_copy(out3.at[0, z], krows(ka, z, x), own.at[0]),
             pltpu.make_async_copy(out3.at[1, z], krows(va, z, x), own.at[1]),
             pltpu.make_async_copy(out3.at[2, z], qa.at[z], own.at[2])]
    for c in local:
        c.start()
    for j in range(1, NZ):
        count_copy(lax.rem(z + nth(j), NZ)).start()

    def target(j):
        return lax.rem(z + NZ - nth(j), NZ)

    def send_all(j, _):
        zcopy(0, target(j)).start()
        zcopy(1, target(j)).start()

        @pl.when(j > 1)
        def _():
            zcopy(2, target(j - 1)).start()
        return 0
    lax.fori_loop(1, NZ, send_all, 0)
    zcopy(2, target(NZ - 1)).start()
    for c in local:
        c.wait()

    def forward(s):
        for i in range(2):
            xcopy(i, s, x, right, rs, rr).start()
            xcopy(i, s, x, left, ls_, lr).start()

    def relay(s):
        xcopy(0, s, left, right, rs, rr).wait_recv()
        xcopy(0, s, left, right, ys, yr).start()
        xcopy(1, s, right, left, ls_, lr).wait_recv()
        xcopy(1, s, right, left, ys, yr).start()

    def complete(s):
        xcopy(1, s, left, right, rs, rr).wait_recv()
        xcopy(0, s, right, left, ls_, lr).wait_recv()
        xcopy(0, s, far, right, ys, yr).wait_recv()
        xcopy(1, s, far, left, ys, yr).wait_recv()

    def nearby(n):
        return lax.rem(z + nth(n), NZ)

    forward(z)
    for n in (1, 2):
        zarrive(0, nearby(n))
        zarrive(1, nearby(n))
        forward(nearby(n))
        relay(nearby(n - 1))
        if n == 1:
            for j in range(1, NZ):
                s = lax.rem(z + j, NZ)
                rcopy(ca.at[x, s], ca.at[x, s], zs.at[3, s], zr.at[3, s], seq_0=s).wait_recv()
            for d in range(1, NX):
                t = lax.rem(x + d, NX)
                rcopy(ca.at[x], ca.at[x], cs.at[t], cr.at[x], seq_1=t).start()
    for d in range(1, NX):
        s = lax.rem(x + d, NX)
        rcopy(ca.at[s], ca.at[s], cs.at[s], cr.at[s], seq_1=s).wait_recv()
    for d in range(1, NX):
        t = lax.rem(x + d, NX)
        rcopy(ca.at[x], ca.at[x], cs.at[t], cr.at[x], seq_1=t).wait_send()
    tally = jnp.zeros((8, 128), F32)
    for i in range(NX):
        for j in range(NZ):
            tally = tally + ca[i, j]
    st1, st2, st3 = tally[1:2, :1], tally[2:3, :1], tally[3:4, :1]
    lane = lax.broadcasted_iota(jnp.int32, (1, 128), 1)
    full = lambda d: tally[d:d + 1, :]
    low = jnp.where(lane == 0, 0.0, jnp.where(lane == 1, full(1), jnp.where(
        lane == 2, full(2), jnp.where(lane == 3, full(3), 1e9))))
    high = jnp.where(lane == 0, full(1), jnp.where(lane == 1, full(2), jnp.where(
        lane == 2, full(3), 1e9)))

    sub = lax.broadcasted_iota(jnp.int32, (128, 1), 0)
    low_col = jnp.where(sub == 0, 0.0, jnp.where(sub == 1, st1, jnp.where(
        sub == 2, st2, jnp.where(sub == 3, st3, 1e9))))
    high_col = jnp.where(sub == 0, st1, jnp.where(sub == 1, st2, jnp.where(sub == 2, st3, 1e9)))

    def dstart(i):
        return jnp.where(i >= st3, st3, jnp.where(i >= st2, st2, jnp.where(i >= st1, st1, 0.0)))

    def qpos(s):
        return (GRP * s + BLK * x).astype(F32) + iota((BLK, 1), 0)

    def absorb(n):
        a = nearby(n)
        o = pl.multiple_of(FRONT + GRP * a, 128)
        kk = ka[pl.ds(o, GRP), :].T
        kT[:128, pl.ds(o, GRP)] = kk
        vT[:, pl.ds(o, GRP)] = va[pl.ds(o, GRP), :].T
        l = mm(wk2[0], kk) + mm(wk2[1], kk)
        for f in (0, HALF):
            lh = l[f:f + HALF]
            e = jnp.exp(lh - jnp.max(lh, axis=0, keepdims=True))
            pkT[f:f + HALF, pl.ds(o, GRP)] = e * (1.0 / jnp.sum(e, axis=0, keepdims=True))
        kpos = (GRP * a).astype(F32) + iota((1, GRP), 1)
        kT[128:, pl.ds(o, GRP)] = jnp.where((kpos >= low_col) & (kpos < high_col), 1.0, 0.0).astype(BF)
        icol = qpos(a)
        miss = jnp.logical_not((icol >= low) & (icol < high)) & (lane < 4)
        qe[a] = jnp.where(miss, NEG, 0.0).astype(BF)
        jrow = (GRP * a).astype(F32) + iota((1, GRP), 1)
        s = mm(qa[a], kk)
        s = jnp.where((jrow <= icol) & (jrow >= dstart(icol)), s, NEG)
        m = jnp.max(s, axis=1, keepdims=True)
        p = jnp.exp2((s - m) * C2)
        ms[a] = m
        accs[a] = mm(p.astype(BF), with_ones(va[pl.ds(o, GRP), :]))

        def place(j):
            b = nearby(j)
            ge = (a - b + NZ) // NZ
            zq, zk = ge * a + (1 - ge) * b, ge * b + (1 - ge) * a
            return zq, pl.ds(pl.multiple_of(FRONT + GRP * zk, 128), GRP)

        def pairs(spots):
            scs = [mm(jnp.concatenate([qa[zq], qe[zq]], axis=1),
                      kT[:, r]) for zq, r in spots]
            tops = [jnp.max(sc, axis=1, keepdims=True) for sc in scs]
            olds, news = [], []
            for (zq, _), top in zip(spots, tops):
                olds.append(ms[zq])
                news.append(jnp.maximum(olds[-1], top))
                ms[zq] = news[-1]
            sums = [mm(jnp.exp2((sc - mn) * C2).astype(BF), with_ones(va[r, :]))
                    for sc, mn, (_, r) in zip(scs, news, spots)]
            for (zq, _), mo, mn, add in zip(spots, olds, news, sums):
                accs[zq] = accs[zq] * jnp.exp2((mo - mn) * C2) + add

        @pl.when(lax.rem(n, 2) == 1)
        def _():
            pairs([place(n - 1)])

        def two(j, _):
            pairs([place(2 * j), place(2 * j + 1)])
            return 0
        lax.fori_loop(0, n // 2, two, 0)

    def step(n, _):
        complete(nearby(n - 2))
        absorb(n - 2)
        s = nearby(n + 1)
        zarrive(0, s)
        zarrive(1, s)
        forward(s)
        relay(nearby(n))
        zarrive(2, nearby(n - 1))
        return 0
    lax.fori_loop(2, NZ - 1, step, 0)

    def late(n, _):
        @pl.when(n > NZ - 3)
        def _():
            zarrive(2, nearby(n))
        complete(nearby(n))
        absorb(n)

        @pl.when(n == NZ - 3)
        def _():
            relay(nearby(NZ - 1))
        return 0
    lax.fori_loop(NZ - 3, NZ, late, 0)

    off = BLK * x + 64 * lax.rem(x, 2)
    run[...] = jnp.zeros_like(run)

    def local_row(s):
        return pl.multiple_of(GRP * s + off + GRP, 128)

    def group_mask(s):
        end = (GRP * s + off + GRP - FRONT).astype(F32)
        jg = end - GRP + iota((1, GRP), 1)
        tag = dstart(jnp.zeros((1, 1), F32) + (end - 1.0))
        return (jg >= tag) & (jg < end) & (jg >= 0.0), tag, end

    def states(s, _):
        r = local_row(s)
        mask, tag, end = group_mask(s)
        o = pl.multiple_of(r - GRP, 128)
        pg = jnp.where(mask, pkT[:, pl.ds(o, GRP)], 0.0).astype(BF)
        keep = jnp.where(tag < end - GRP, 1.0, 0.0)
        st = run[...] * keep + mm(pg, with_ones(va[pl.ds(o, GRP), :]))
        run[...] = st
        hi, lo = hilo(st)
        sts[s, 0] = hi
        sts[s, 1] = lo
        tb[s] = (accs[s][:, :128] / accs[s][:, 128:]).astype(BF)
        return 0
    lax.fori_loop(0, NZ, states, 0)

    dwq[...] = jnp.zeros_like(dwq)
    pls[...] = jnp.zeros_like(pls)

    def send_out(i, t):
        return rcopy((tb, yb)[i].at[t], tr.at[i, z], os.at[i, t], orr.at[i, z], seq_0=t)

    def block(n, _):
        s = lax.rem(z + nth(NZ - 1 - n), NZ)

        @pl.when(n < NZ - 1)
        def _():
            send_out(0, s).start()

        @pl.when(n > 0)
        def _():
            send_out(1, lax.rem(z + nth(NZ - n), NZ)).start()
        r = local_row(s)
        q = qa[s]
        kl = ka[pl.ds(r, LOC), :]
        vl = with_ones(va[pl.ds(r, LOC), :])
        icol = qpos(s)
        dcol = dstart(icol)
        jrow = (GRP * s + off + GRP - FRONT).astype(F32) + iota((1, LOC), 1)
        same = jrow >= dcol
        sc = mm(q, kl, 1, 1)
        lq = mm(q, wq2[...])
        lq = lq[:, :128] + lq[:, 128:]
        ph = []
        for f in (0, HALF):
            lh = lq[:, f:f + HALF]
            e = jnp.exp(lh - jnp.max(lh, axis=1, keepdims=True))
            ph.append(e * (1.0 / jnp.sum(e, axis=1, keepdims=True)))
        pq = jnp.concatenate(ph, axis=1)
        pq_h, pq_l = hilo(pq)
        _, tag, end = group_mask(s)
        uses = jnp.where((dcol == tag) & (end > 0.0), 1.0, 0.0)
        sh, sl = sts[s, 0], sts[s, 1]
        sth = mm(pq_h, sh) + mm(pq_l, sh) + mm(pq_h, sl)
        swm = jnp.where(same & (jrow <= icol) & (jrow > icol - WINDOW), sc, NEG)
        a = jnp.exp2((swm - jnp.max(swm, axis=1, keepdims=True)) * C2)
        bey = same & (jrow <= icol - WINDOW)
        pl_T = pkT[:, pl.ds(r, LOC)].astype(BF)
        bb = jnp.where(bey, mm(pq_h, pl_T), 0.0)
        nd = mm((a + bb).astype(BF), vl) + uses * sth
        rden = 1.0 / nd[:, 128:]
        y = nd[:, :128] * rden
        yb[s] = y.astype(BF)
        e = y - tb[s].astype(F32)
        pls[...] += jnp.sum((e * e).reshape(BLK // 8, 8, 128), axis=0)
        gr_ = e * rden * (2.0 * norm)
        gx = jnp.concatenate([gr_, -gr_ * y], axis=1)
        gh, _ = hilo(gx)
        db = jnp.where(bey, mm(gh, vl, 1, 1), 0.0).astype(BF)
        guh, gul = hilo(gx * uses)
        dpq = mm(db, pl_T, 1, 1) + mm(guh, sh, 1, 1) + mm(gul, sh, 1, 1) + mm(guh, sl, 1, 1)
        dpT[:, pl.ds(r, LOC)] += mm(pq_h, db, 0, 0)
        dss[s] = mm(pq_h, guh, 0, 0)
        out = []
        for f in (0, HALF):
            pp, dd = pq[:, f:f + HALF], dpq[:, f:f + HALF]
            out.append(pp * (dd - jnp.sum(pp * dd, axis=1, keepdims=True)))
        dh, dlo = hilo(jnp.concatenate(out, axis=1))
        dwq[...] += mm(q, jnp.concatenate([dh, dlo], axis=1), 0, 0)
        return 0
    lax.fori_loop(0, NZ, block, 0)

    def lscatter(t):
        return rcopy(lx.at[x], lx.at[x], xs.at[1, t], xr.at[1, x], seq_1=t)

    def lspread(s, t):
        return rcopy(lz.at[s], lz.at[s], zs.at[5, t], zr.at[5, s], seq_0=t)
    lx[x] = pls[...] * norm
    for d in range(1, NX):
        lscatter(lax.rem(x + d, NX)).start()

    run[...] = jnp.zeros_like(run)

    def back(n, _):
        s = NZ - 1 - n
        o = pl.multiple_of(local_row(s) - GRP, 128)
        mask, tag, end = group_mask(s)
        keep = jnp.where(dstart(jnp.zeros((1, 1), F32) + (end + GRP - 1.0)) == tag, 1.0, 0.0)
        rr_ = run[...] * keep + dss[s]
        run[...] = rr_
        d = mm(rr_.astype(BF), jnp.concatenate([vT[:, pl.ds(o, GRP)], jnp.ones((128, GRP), BF)], axis=0))
        dpT[:, pl.ds(o, GRP)] += jnp.where(mask, d, 0.0)
        return 0
    lax.fori_loop(0, NZ, back, 0)
    for d in range(1, NX):
        s = lax.rem(x + d, NX)
        rcopy(lx.at[s], lx.at[s], xs.at[1, s], xr.at[1, s], seq_1=s).wait_recv()
    lz[z] = (lx[0] + lx[1]) + (lx[2] + lx[3])
    for j in range(1, NZ):
        lspread(z, lax.rem(z + nth(j), NZ)).start()

    def fin(s, acc):
        o = pl.multiple_of(FRONT + GRP * s, 128)
        out = []
        for f in (0, HALF):
            pp, dd = pkT[f:f + HALF, pl.ds(o, GRP)], dpT[f:f + HALF, pl.ds(o, GRP)]
            out.append(pp * (dd - jnp.sum(pp * dd, axis=0, keepdims=True)))
        dh, dlo = hilo(jnp.concatenate(out, axis=0))
        kk = ka[pl.ds(o, GRP), :]
        return acc + mm(dh, kk) + mm(dlo, kk)
    dk = lax.fori_loop(0, NZ, fin, jnp.zeros((128, 128), F32)).T
    dq = dwq[:, :128] + dwq[:, 128:]
    dw = jnp.concatenate([dq[:, :HALF] - dq[:, HALF:], dk[:, :HALF] - dk[:, HALF:]], axis=1)
    dwb[...] = dw.reshape(NX, 32, 128)

    def scatter(t):
        return rcopy(dwb.at[t], wx.at[x], xs.at[0, t], xr.at[0, x], seq_1=t)

    def zspread(s, t):
        return rcopy(wg.at[x, s], wg.at[x, s], zs.at[4, t], zr.at[4, s], seq_0=t)
    for d in range(1, NX):
        scatter(lax.rem(x + d, NX)).start()
    wx[x] = dwb[x]
    for d in range(1, NX):
        s = lax.rem(x + d, NX)
        rcopy(wx.at[s], wx.at[s], xs.at[0, s], xr.at[0, s], seq_1=s).wait_recv()
    wg[x, z] = ((wx[0] + wx[1]) + (wx[2] + wx[3])).astype(BF)
    for j in range(1, NZ):
        zspread(z, lax.rem(z + nth(j), NZ)).start()
    for j in range(1, NZ):
        s = lax.rem(z + j, NZ)
        lspread(s, s).wait_recv()
    part = lz[0]
    for i in range(1, NZ):
        part = part + lz[i]
    mine = NX * g + h
    lc[mine] = part
    for peer in cols:
        there = NX * peer["grp"] + peer["head"]
        rcopy(lc.at[mine], lc.at[mine], gs.at[there], gr.at[mine], **peer).start()

    def land(i, src, dst):
        for j in range(1, NZ):
            s = lax.rem(z + j, NZ)
            rcopy(tr.at[i, s], tr.at[i, s], os.at[i, s], orr.at[i, s], seq_0=s).wait_recv()
        tr[i, z] = src[z]
        for d in range(NZ):
            flat[pl.ds(d, BLK, stride=NZ), :] = tr[i, d].astype(F32)
        dst[...] = flat[...].reshape(BLK, NZ, 128).astype(BF)
    land(0, tb, ta)
    for j in range(1, NZ):
        s = lax.rem(z + j, NZ)
        zspread(s, s).wait_recv()
    for d in range(1, NX):
        t = lax.rem(x + d, NX)
        rcopy(wg.at[x], wg.at[x], xs.at[2, t], xr.at[2, x], seq_1=t).start()
    land(1, yb, ya)
    for peer in cols:
        there = NX * peer["grp"] + peer["head"]
        rcopy(lc.at[there], lc.at[there], gs.at[there], gr.at[there], **peer).wait_recv()
    part = lc[0]
    for i in range(1, 8):
        part = part + lc[i]
    lout[...] = jnp.sum(jnp.sum(part, axis=0, keepdims=True), axis=1, keepdims=True)
    for d in range(1, NX):
        s = lax.rem(x + d, NX)
        rcopy(wg.at[s], wg.at[s], xs.at[2, s], xr.at[2, s], seq_1=s).wait_recv()
    for i in range(NX):
        wout[:, i] = wg[i].astype(F32)

    def drain(j, _):
        s = lax.rem(z + j, NZ)
        for i in range(2):
            send_out(i, s).wait_send()
        for i in range(3):
            zcopy(i, s).wait_send()
        count_copy(s).wait_send()
        zspread(z, s).wait_send()
        lspread(z, s).wait_send()
        return 0
    lax.fori_loop(1, NZ, drain, 0)

    def drain_x(s, _):
        for i in range(2):
            xcopy(i, s, x, right, rs, rr).wait_send()
            xcopy(i, s, x, left, ls_, lr).wait_send()
        xcopy(0, s, left, right, ys, yr).wait_send()
        xcopy(1, s, right, left, ys, yr).wait_send()
        return 0
    lax.fori_loop(0, NZ, drain_x, 0)
    for d in range(1, NX):
        t = lax.rem(x + d, NX)
        scatter(t).wait_send()
        lscatter(t).wait_send()
        rcopy(wg.at[x], wg.at[x], xs.at[2, t], xr.at[2, x], seq_1=t).wait_send()
    for peer in cols:
        there = NX * peer["grp"] + peer["head"]
        rcopy(lc.at[mine], lc.at[mine], gs.at[there], gr.at[mine], **peer).wait_send()


def whole(norm, q, k, v, docs, fm):
    M = pl.BlockSpec(memory_space=pltpu.VMEM)
    D, V = pltpu.SemaphoreType.DMA, pltpu.VMEM
    return pl.pallas_call(
        functools.partial(kernel, norm),
        out_shape=(V((BLK, NZ, 128), BF), V((BLK, NZ, 128), BF), V((NZ, NX, 32, 128), F32),
                   jax.ShapeDtypeStruct((1, 1), F32)),
        in_specs=[M] * 5, out_specs=(M,) * 4,
        scratch_shapes=[
            V((BLK * NZ, 128), F32), V((3, NZ, BLK, 128), BF), V((2, NZ, BLK, 128), BF),
            V((NZ, BLK, 128), BF), V((ROWS, 128), BF), V((ROWS, 128), BF), V((NX, NZ, 8, 128), F32),
            V((NZ, BLK, 128), BF), V((256, ROWS), BF), V((128, ROWS), BF), V((128, 256), BF), V((2, 128, 128), BF),
            V((128, ROWS), F32), V((128, ROWS), F32),
            V((NZ, BLK, 1), F32), V((NZ, BLK, 256), F32), V((NZ, BLK, 128), BF), V((NZ, BLK, 128), BF),
            V((NZ, 2, 128, 256), BF), V((NZ, 128, 256), F32), V((128, 256), F32), V((128, 256), F32),
            V((8, 128), F32),
            V((NX, 32, 128), F32), V((NX, 32, 128), F32), V((NX, NZ, 32, 128), BF),
            V((NX, 8, 128), F32), V((NZ, 8, 128), F32), V((8, 8, 128), F32),
            D((3,)), D((6, NZ)), D((6, NZ)), D((2, NZ)), D((2, NZ)), D((2, NZ)), D((2, NZ)),
            D((2, NZ)), D((2, NZ)), D((NX,)), D((NX,)), D((3, NX)), D((3, NX)), D((8,)), D((8,)),
            D((2, NZ)), D((2, NZ))],
        compiler_params=pltpu.CompilerParams(
            collective_id=0, has_side_effects=True, vmem_limit_bytes=60 << 20),
    )(q, k, v, docs, fm)


def body(queries, keys, values, documents, feature_map):
    norm = 1.0 / (TOKENS * 64)
    ta, ya, wa, la = whole(norm, queries, keys, values, documents.reshape(1, BLK), feature_map)
    return (ta, ya, la.reshape(()), wa.reshape(NZ, 128, 128))


def solution(mesh):
    split = Mesh(
        mesh.devices.reshape(mesh.shape["grp"], 8, 4, mesh.shape["head"]),
        ("grp", "seq_0", "seq_1", "head"),
    )
    return jax.shard_map(
        body,
        mesh=split,
        in_specs=(
            P(SEQ, ("grp", "head"), None),
            P(SEQ, ("grp", "head"), None),
            P(SEQ, ("grp", "head"), None),
            P(SEQ),
            P(("grp", "head"), None, None),
        ),
        out_specs=(
            P(SEQ, ("grp", "head"), None),
            P(SEQ, ("grp", "head"), None),
            P(),
            P(("grp", "head"), None, None),
        ),
        check_vma=False,
    )
```

```python
import functools
import math

import jax
import jax.numpy as jnp
from jax import lax
from jax.experimental import pallas as pl
from jax.experimental.pallas import tpu as pltpu
from jax.sharding import Mesh
from jax.sharding import PartitionSpec as P

SEQ = ("seq_0", "seq_1")
MESH = pl.DeviceIdType.MESH

TOKENS, BLK, WINDOW, LOC, GRP, HALF = 6144, 192, 64, 384, 768, 64
NZ, NX = 8, 4
FRONT = 896
ROWS = FRONT + TOKENS + 128
F32, BF = jnp.float32, jnp.bfloat16
NEG = -1e30
SCALE = 128**-0.5
LOG2E = math.log2(math.e)
C2 = SCALE * LOG2E


def mm(a, b, ca=1, cb=0):
    return lax.dot_general(a, b, (((ca,), (cb,)), ((), ())), preferred_element_type=F32)


def hilo(a):
    hi = a.astype(BF)
    return hi, (a - hi.astype(F32)).astype(BF)


def rcopy(src, dst, ssem, rsem, **where):
    return pltpu.make_async_remote_copy(
        src_ref=src, dst_ref=dst, send_sem=ssem, recv_sem=rsem,
        device_id=where, device_id_type=MESH)


def nth(j):
    odd = lax.rem(j, 2)
    return lax.rem(odd * ((j + 1) // 2) + (1 - odd) * (NZ - j // 2), NZ)


def with_ones(v):
    return jnp.concatenate([v, jnp.ones_like(v)], axis=1)


def iota(shape, dim):
    return lax.broadcasted_iota(jnp.int32, shape, dim).astype(F32)


def kernel(norm, q_ref, k_ref, v_ref, doc_ref, fm_ref, ta, ya, wout, lout,
           flat, out3, tr, qa, ka, va, ca, qe, pqs, kT, vT, wq2, wk2, pkT, dpT, ms, accs, tb, yb, sts, dss, run, dwq, pls,
           dwb, wx, wg, lx, lz, lc,
           own, zs, zr, rs, rr, ls_, lr, ys, yr, cs, cr, xs, xr, gs, gr, os, orr):
    z, x = lax.axis_index("seq_0"), lax.axis_index("seq_1")
    h, g = lax.axis_index("head"), lax.axis_index("grp")
    right, left, far = lax.rem(x + 1, NX), lax.rem(x + 3, NX), lax.rem(x + 2, NX)
    cols = [{"grp": lax.rem(g + (d // NX), 2), "head": lax.rem(h + d % NX, NX)} for d in range(1, 8)]

    everyone = ([{"seq_0": lax.rem(z + d, NZ)} for d in range(1, NZ)]
                + [{"seq_1": lax.rem(x + d, NX)} for d in range(1, NX)] + cols)
    barrier = pltpu.get_barrier_semaphore()
    for peer in everyone:
        pl.semaphore_signal(barrier, inc=1, device_id=peer, device_id_type=MESH)

    for i, ref in enumerate((k_ref, v_ref, q_ref)):
        flat[...] = ref[...].astype(F32).reshape(BLK * NZ, 128)
        for d in range(NZ):
            out3[i, d] = flat[pl.ds(d, BLK, stride=NZ), :].astype(BF)

    docs = doc_ref[...]
    row = lax.broadcasted_iota(jnp.int32, (8, 128), 0)
    tile = jnp.zeros((8, 128), F32)
    for d in (1, 2, 3):
        n = jnp.sum((docs < d).astype(F32), axis=1, keepdims=True)
        tile = tile + jnp.where(row == d, jnp.broadcast_to(n, (8, 128)), 0.0)
    ca[x, z] = tile
    zero = jnp.zeros((FRONT, 128), BF)
    for ref in (ka, va):
        ref[:FRONT] = zero
        ref[FRONT + TOKENS:] = zero[:128]
    vT[:, :FRONT] = jnp.zeros((128, FRONT), BF)
    vT[:, FRONT + TOKENS:] = jnp.zeros((128, 128), BF)
    dpT[...] = jnp.zeros_like(dpT)
    kT[144:] = jnp.zeros((112, ROWS), BF)
    pkT[:, :FRONT] = jnp.zeros((128, FRONT), F32)
    pkT[:, FRONT + TOKENS:] = jnp.zeros((128, 128), F32)
    w = fm_ref[z]
    wqh, wql = hilo(jnp.concatenate([w[:, :HALF], -w[:, :HALF]], axis=1) * LOG2E)
    wq2[...] = jnp.concatenate([wqh, wql], axis=1)
    wkh, wkl = hilo(jnp.concatenate([w[:, HALF:], -w[:, HALF:]], axis=1).T * LOG2E)
    wk2[0] = wkh
    wk2[1] = wkl

    pl.semaphore_wait(barrier, len(everyone))

    def krows(arr, s, col):
        return arr.at[pl.ds(pl.multiple_of(FRONT + GRP * s + BLK * col, 64), BLK)]

    def zcopy(i, t):
        src = out3.at[i, t]
        dst = qa.at[z] if i == 2 else krows((ka, va)[i], z, x)
        return rcopy(src, dst, zs.at[i, t], zr.at[i, z], seq_0=t)

    def zarrive(i, s):
        dst = qa.at[s] if i == 2 else krows((ka, va)[i], s, x)
        rcopy(dst, dst, zs.at[i, s], zr.at[i, s], seq_0=s).wait_recv()

    def count_copy(t):
        return rcopy(ca.at[x, z], ca.at[x, z], zs.at[3, t], zr.at[3, z], seq_0=t)

    def xcopy(i, s, col, to, sems, semr):
        ref = krows((ka, va)[i], s, col)
        return rcopy(ref, ref, sems.at[i, s], semr.at[i, s], seq_1=to)

    local = [pltpu.make_async_copy(out3.at[0, z], krows(ka, z, x), own.at[0]),
             pltpu.make_async_copy(out3.at[1, z], krows(va, z, x), own.at[1]),
             pltpu.make_async_copy(out3.at[2, z], qa.at[z], own.at[2])]
    for c in local:
        c.start()
    for j in range(1, NZ):
        count_copy(lax.rem(z + nth(j), NZ)).start()

    def target(j):
        return lax.rem(z + NZ - nth(j), NZ)

    def send_all(j, _):
        zcopy(0, target(j)).start()
        zcopy(1, target(j)).start()

        @pl.when(j > 1)
        def _():
            zcopy(2, target(j - 1)).start()
        return 0
    lax.fori_loop(1, NZ, send_all, 0)
    zcopy(2, target(NZ - 1)).start()
    for c in local:
        c.wait()

    def forward(s):
        for i in range(2):
            xcopy(i, s, x, right, rs, rr).start()
            xcopy(i, s, x, left, ls_, lr).start()

    def relay(s):
        xcopy(0, s, left, right, rs, rr).wait_recv()
        xcopy(0, s, left, right, ys, yr).start()
        xcopy(1, s, right, left, ls_, lr).wait_recv()
        xcopy(1, s, right, left, ys, yr).start()

    def complete(s):
        xcopy(1, s, left, right, rs, rr).wait_recv()
        xcopy(0, s, right, left, ls_, lr).wait_recv()
        xcopy(0, s, far, right, ys, yr).wait_recv()
        xcopy(1, s, far, left, ys, yr).wait_recv()

    def nearby(n):
        return lax.rem(z + nth(n), NZ)

    forward(z)
    for n in (1, 2):
        zarrive(0, nearby(n))
        zarrive(1, nearby(n))
        forward(nearby(n))
        relay(nearby(n - 1))
        if n == 1:
            for j in range(1, NZ):
                s = lax.rem(z + j, NZ)
                rcopy(ca.at[x, s], ca.at[x, s], zs.at[3, s], zr.at[3, s], seq_0=s).wait_recv()
            for d in range(1, NX):
                t = lax.rem(x + d, NX)
                rcopy(ca.at[x], ca.at[x], cs.at[t], cr.at[x], seq_1=t).start()
    for d in range(1, NX):
        s = lax.rem(x + d, NX)
        rcopy(ca.at[s], ca.at[s], cs.at[s], cr.at[s], seq_1=s).wait_recv()
    for d in range(1, NX):
        t = lax.rem(x + d, NX)
        rcopy(ca.at[x], ca.at[x], cs.at[t], cr.at[x], seq_1=t).wait_send()
    tally = jnp.zeros((8, 128), F32)
    for i in range(NX):
        for j in range(NZ):
            tally = tally + ca[i, j]
    st1, st2, st3 = tally[1:2, :1], tally[2:3, :1], tally[3:4, :1]
    lane = lax.broadcasted_iota(jnp.int32, (1, 128), 1)
    full = lambda d: tally[d:d + 1, :]
    low = jnp.where(lane == 0, 0.0, jnp.where(lane == 1, full(1), jnp.where(
        lane == 2, full(2), jnp.where(lane == 3, full(3), 1e9))))
    high = jnp.where(lane == 0, full(1), jnp.where(lane == 1, full(2), jnp.where(
        lane == 2, full(3), 1e9)))

    sub = lax.broadcasted_iota(jnp.int32, (16, 1), 0)
    low_col = jnp.where(sub == 0, 0.0, jnp.where(sub == 1, st1, jnp.where(
        sub == 2, st2, jnp.where(sub == 3, st3, 1e9))))
    high_col = jnp.where(sub == 0, st1, jnp.where(sub == 1, st2, jnp.where(sub == 2, st3, 1e9)))

    def dstart(i):
        return jnp.where(i >= st3, st3, jnp.where(i >= st2, st2, jnp.where(i >= st1, st1, 0.0)))

    def qpos(s):
        return (GRP * s + BLK * x).astype(F32) + iota((BLK, 1), 0)

    def absorb(n):
        a = nearby(n)
        o = pl.multiple_of(FRONT + GRP * a, 128)
        kk = ka[pl.ds(o, GRP), :].T
        kT[:128, pl.ds(o, GRP)] = kk
        vT[:, pl.ds(o, GRP)] = va[pl.ds(o, GRP), :].T
        l = mm(wk2[0], kk) + mm(wk2[1], kk)
        for f in (0, HALF):
            lh = l[f:f + HALF]
            e = jnp.exp2(lh - jnp.max(lh, axis=0, keepdims=True))
            pkT[f:f + HALF, pl.ds(o, GRP)] = e * (1.0 / jnp.sum(e, axis=0, keepdims=True))
        kpos = (GRP * a).astype(F32) + iota((1, GRP), 1)
        kT[128:144, pl.ds(o, GRP)] = jnp.where((kpos >= low_col) & (kpos < high_col), 1.0, 0.0).astype(BF)
        icol = qpos(a)
        miss = jnp.logical_not((icol >= low) & (icol < high)) & (lane < 4)
        qe[a] = jnp.where(miss, NEG, 0.0).astype(BF)
        lq = mm(qa[a], wq2[...])
        lq = lq[:, :128] + lq[:, 128:]
        for f in (0, HALF):
            lh = lq[:, f:f + HALF]
            e = jnp.exp2(lh - jnp.max(lh, axis=1, keepdims=True))
            pqs[a, :, f:f + HALF] = e * (1.0 / jnp.sum(e, axis=1, keepdims=True))
        jrow = (GRP * a).astype(F32) + iota((1, GRP), 1)
        s = mm(qa[a], kk)
        s = jnp.where((jrow <= icol) & (jrow >= dstart(icol)), s, NEG)
        m = jnp.max(s, axis=1, keepdims=True)
        p = jnp.exp2((s - m) * C2)
        ms[a] = m
        accs[a] = mm(p.astype(BF), with_ones(va[pl.ds(o, GRP), :]))

        def place(j):
            b = nearby(j)
            ge = (a - b + NZ) // NZ
            zq, zk = ge * a + (1 - ge) * b, ge * b + (1 - ge) * a
            return zq, pl.ds(pl.multiple_of(FRONT + GRP * zk, 128), GRP)

        def pairs(spots):
            scs = [mm(jnp.concatenate([qa[zq], qe[zq]], axis=1),
                      kT[:, r]) for zq, r in spots]
            tops = [jnp.max(sc, axis=1, keepdims=True) for sc in scs]
            olds, news = [], []
            for (zq, _), top in zip(spots, tops):
                olds.append(ms[zq])
                news.append(jnp.maximum(olds[-1], top))
                ms[zq] = news[-1]
            sums = [mm(jnp.exp2((sc - mn) * C2).astype(BF), with_ones(va[r, :]))
                    for sc, mn, (_, r) in zip(scs, news, spots)]
            for (zq, _), mo, mn, add in zip(spots, olds, news, sums):
                accs[zq] = accs[zq] * jnp.exp2((mo - mn) * C2) + add

        @pl.when(n == NZ - 2)
        def _():
            relay(nearby(NZ - 1))

        @pl.when(lax.rem(n, 2) == 1)
        def _():
            pairs([place(n - 1)])

        def two(j, _):
            pairs([place(2 * j), place(2 * j + 1)])
            return 0
        lax.fori_loop(0, n // 2, two, 0)

    def step(n, _):
        @pl.when(n > 0)
        def _():
            zarrive(2, nearby(n))
        complete(nearby(n))
        absorb(n)

        @pl.when(n < NZ - 3)
        def _():
            relay(nearby(n + 2))

        @pl.when((n < NZ - 4) | (n == NZ - 3))
        def _():
            s = nearby(n + 3 - n // (NZ - 3))
            zarrive(0, s)
            zarrive(1, s)
            forward(s)
        return 0
    lax.fori_loop(0, NZ, step, 0)

    off = BLK * x + 64 * lax.rem(x, 2)
    run[...] = jnp.zeros_like(run)

    def local_row(s):
        return pl.multiple_of(GRP * s + off + GRP, 128)

    def group_mask(s):
        end = (GRP * s + off + GRP - FRONT).astype(F32)
        jg = end - GRP + iota((1, GRP), 1)
        tag = dstart(jnp.zeros((1, 1), F32) + (end - 1.0))
        return (jg >= tag) & (jg < end) & (jg >= 0.0), tag, end

    def states(s, _):
        r = local_row(s)
        mask, tag, end = group_mask(s)
        o = pl.multiple_of(r - GRP, 128)
        pg = jnp.where(mask, pkT[:, pl.ds(o, GRP)], 0.0).astype(BF)
        keep = jnp.where(tag < end - GRP, 1.0, 0.0)
        st = run[...] * keep + mm(pg, with_ones(va[pl.ds(o, GRP), :]))
        run[...] = st
        hi, lo = hilo(st)
        sts[s, 0] = hi
        sts[s, 1] = lo
        tb[s] = (accs[s][:, :128] / accs[s][:, 128:]).astype(BF)
        return 0
    lax.fori_loop(0, NZ, states, 0)

    dwq[...] = jnp.zeros_like(dwq)
    pls[...] = jnp.zeros_like(pls)

    def send_out(i, t):
        return rcopy((tb, yb)[i].at[t], tr.at[i, z], os.at[i, t], orr.at[i, z], seq_0=t)

    def block(n, _):
        s = lax.rem(z + nth(NZ - 1 - n), NZ)

        @pl.when(n < NZ - 1)
        def _():
            send_out(0, s).start()

        @pl.when(n > 0)
        def _():
            send_out(1, lax.rem(z + nth(NZ - n), NZ)).start()
        r = local_row(s)
        q = qa[s]
        kl = ka[pl.ds(r, LOC), :]
        vl = with_ones(va[pl.ds(r, LOC), :])
        icol = qpos(s)
        dcol = dstart(icol)
        jrow = (GRP * s + off + GRP - FRONT).astype(F32) + iota((1, LOC), 1)
        same = jrow >= dcol
        sc = mm(q, kl, 1, 1)
        pq = pqs[s]
        pq_h, pq_l = hilo(pq)
        _, tag, end = group_mask(s)
        uses = jnp.where((dcol == tag) & (end > 0.0), 1.0, 0.0)
        sh, sl = sts[s, 0], sts[s, 1]
        sth = mm(pq_h, sh) + mm(pq_l, sh) + mm(pq_h, sl)
        swm = jnp.where(same & (jrow <= icol) & (jrow > icol - WINDOW), sc, NEG)
        a = jnp.exp2((swm - jnp.max(swm, axis=1, keepdims=True)) * C2)
        bey = same & (jrow <= icol - WINDOW)
        pl_T = pkT[:, pl.ds(r, LOC)].astype(BF)
        bb = jnp.where(bey, mm(pq_h, pl_T), 0.0)
        nd = mm((a + bb).astype(BF), vl) + uses * sth
        rden = 1.0 / nd[:, 128:]
        y = nd[:, :128] * rden
        yb[s] = y.astype(BF)
        e = y - tb[s].astype(F32)
        pls[...] += jnp.sum((e * e).reshape(BLK // 8, 8, 128), axis=0)
        gr_ = e * rden * (2.0 * norm)
        gx = jnp.concatenate([gr_, -gr_ * y], axis=1)
        gh, _ = hilo(gx)
        db = jnp.where(bey, mm(gh, vl, 1, 1), 0.0).astype(BF)
        guh, gul = hilo(gx * uses)
        dpq = mm(db, pl_T, 1, 1) + mm(guh, sh, 1, 1) + mm(gul, sh, 1, 1) + mm(guh, sl, 1, 1)
        dpT[:, pl.ds(r, LOC)] += mm(pq_h, db, 0, 0)
        dss[s] = mm(pq_h, guh, 0, 0)
        out = []
        for f in (0, HALF):
            pp, dd = pq[:, f:f + HALF], dpq[:, f:f + HALF]
            out.append(pp * (dd - jnp.sum(pp * dd, axis=1, keepdims=True)))
        dh, dlo = hilo(jnp.concatenate(out, axis=1))
        dwq[...] += mm(q, jnp.concatenate([dh, dlo], axis=1), 0, 0)
        return 0
    lax.fori_loop(0, NZ, block, 0)

    def lscatter(t):
        return rcopy(lx.at[x], lx.at[x], xs.at[1, t], xr.at[1, x], seq_1=t)

    def lspread(s, t):
        return rcopy(lz.at[s], lz.at[s], zs.at[5, t], zr.at[5, s], seq_0=t)
    lx[x] = pls[...] * norm
    for d in range(1, NX):
        lscatter(lax.rem(x + d, NX)).start()

    run[...] = jnp.zeros_like(run)

    def back(n, _):
        s = NZ - 1 - n
        o = pl.multiple_of(local_row(s) - GRP, 128)
        mask, tag, end = group_mask(s)
        keep = jnp.where(dstart(jnp.zeros((1, 1), F32) + (end + GRP - 1.0)) == tag, 1.0, 0.0)
        rr_ = run[...] * keep + dss[s]
        run[...] = rr_
        d = mm(rr_.astype(BF), jnp.concatenate([vT[:, pl.ds(o, GRP)], jnp.ones((128, GRP), BF)], axis=0))
        dpT[:, pl.ds(o, GRP)] += jnp.where(mask, d, 0.0)
        return 0
    lax.fori_loop(0, NZ, back, 0)
    for d in range(1, NX):
        s = lax.rem(x + d, NX)
        rcopy(lx.at[s], lx.at[s], xs.at[1, s], xr.at[1, s], seq_1=s).wait_recv()
    lz[z] = (lx[0] + lx[1]) + (lx[2] + lx[3])
    for j in range(1, NZ):
        lspread(z, lax.rem(z + nth(j), NZ)).start()

    def fin(s, acc):
        o = pl.multiple_of(FRONT + GRP * s, 128)
        out = []
        for f in (0, HALF):
            pp, dd = pkT[f:f + HALF, pl.ds(o, GRP)], dpT[f:f + HALF, pl.ds(o, GRP)]
            out.append(pp * (dd - jnp.sum(pp * dd, axis=0, keepdims=True)))
        dh, dlo = hilo(jnp.concatenate(out, axis=0))
        kk = ka[pl.ds(o, GRP), :]
        return acc + mm(dh, kk) + mm(dlo, kk)
    dk = lax.fori_loop(0, NZ, fin, jnp.zeros((128, 128), F32)).T
    dq = dwq[:, :128] + dwq[:, 128:]
    dw = jnp.concatenate([dq[:, :HALF] - dq[:, HALF:], dk[:, :HALF] - dk[:, HALF:]], axis=1)
    dwb[...] = dw.reshape(NX, 32, 128)

    def scatter(t):
        return rcopy(dwb.at[t], wx.at[x], xs.at[0, t], xr.at[0, x], seq_1=t)

    def zspread(s, t):
        return rcopy(wg.at[x, s], wg.at[x, s], zs.at[4, t], zr.at[4, s], seq_0=t)
    for d in range(1, NX):
        scatter(lax.rem(x + d, NX)).start()
    wx[x] = dwb[x]
    for d in range(1, NX):
        s = lax.rem(x + d, NX)
        rcopy(wx.at[s], wx.at[s], xs.at[0, s], xr.at[0, s], seq_1=s).wait_recv()
    wg[x, z] = ((wx[0] + wx[1]) + (wx[2] + wx[3])).astype(BF)
    for j in range(1, NZ):
        zspread(z, lax.rem(z + nth(j), NZ)).start()
    for j in range(1, NZ):
        s = lax.rem(z + j, NZ)
        lspread(s, s).wait_recv()
    part = lz[0]
    for i in range(1, NZ):
        part = part + lz[i]
    mine = NX * g + h
    lc[mine] = part
    for peer in cols:
        there = NX * peer["grp"] + peer["head"]
        rcopy(lc.at[mine], lc.at[mine], gs.at[there], gr.at[mine], **peer).start()

    def land(i, src, dst):
        for j in range(1, NZ):
            s = lax.rem(z + j, NZ)
            rcopy(tr.at[i, s], tr.at[i, s], os.at[i, s], orr.at[i, s], seq_0=s).wait_recv()
        tr[i, z] = src[z]
        for d in range(NZ):
            flat[pl.ds(d, BLK, stride=NZ), :] = tr[i, d].astype(F32)
        dst[...] = flat[...].reshape(BLK, NZ, 128).astype(BF)
    land(0, tb, ta)
    for j in range(1, NZ):
        s = lax.rem(z + j, NZ)
        zspread(s, s).wait_recv()
    for d in range(1, NX):
        t = lax.rem(x + d, NX)
        rcopy(wg.at[x], wg.at[x], xs.at[2, t], xr.at[2, x], seq_1=t).start()
    land(1, yb, ya)
    for peer in cols:
        there = NX * peer["grp"] + peer["head"]
        rcopy(lc.at[there], lc.at[there], gs.at[there], gr.at[there], **peer).wait_recv()
    part = lc[0]
    for i in range(1, 8):
        part = part + lc[i]
    lout[...] = jnp.sum(jnp.sum(part, axis=0, keepdims=True), axis=1, keepdims=True)
    for d in range(1, NX):
        s = lax.rem(x + d, NX)
        rcopy(wg.at[s], wg.at[s], xs.at[2, s], xr.at[2, s], seq_1=s).wait_recv()
    for i in range(NX):
        wout[:, i] = wg[i].astype(F32)

    def drain(j, _):
        s = lax.rem(z + j, NZ)
        for i in range(2):
            send_out(i, s).wait_send()
        for i in range(3):
            zcopy(i, s).wait_send()
        count_copy(s).wait_send()
        zspread(z, s).wait_send()
        lspread(z, s).wait_send()
        return 0
    lax.fori_loop(1, NZ, drain, 0)

    def drain_x(s, _):
        for i in range(2):
            xcopy(i, s, x, right, rs, rr).wait_send()
            xcopy(i, s, x, left, ls_, lr).wait_send()
        xcopy(0, s, left, right, ys, yr).wait_send()
        xcopy(1, s, right, left, ys, yr).wait_send()
        return 0
    lax.fori_loop(0, NZ, drain_x, 0)
    for d in range(1, NX):
        t = lax.rem(x + d, NX)
        scatter(t).wait_send()
        lscatter(t).wait_send()
        rcopy(wg.at[x], wg.at[x], xs.at[2, t], xr.at[2, x], seq_1=t).wait_send()
    for peer in cols:
        there = NX * peer["grp"] + peer["head"]
        rcopy(lc.at[mine], lc.at[mine], gs.at[there], gr.at[mine], **peer).wait_send()


def whole(norm, q, k, v, docs, fm):
    M = pl.BlockSpec(memory_space=pltpu.VMEM)
    D, V = pltpu.SemaphoreType.DMA, pltpu.VMEM
    return pl.pallas_call(
        functools.partial(kernel, norm),
        out_shape=(V((BLK, NZ, 128), BF), V((BLK, NZ, 128), BF), V((NZ, NX, 32, 128), F32),
                   jax.ShapeDtypeStruct((1, 1), F32)),
        in_specs=[M] * 5, out_specs=(M,) * 4,
        scratch_shapes=[
            V((BLK * NZ, 128), F32), V((3, NZ, BLK, 128), BF), V((2, NZ, BLK, 128), BF),
            V((NZ, BLK, 128), BF), V((ROWS, 128), BF), V((ROWS, 128), BF), V((NX, NZ, 8, 128), F32),
            V((NZ, BLK, 128), BF), V((NZ, BLK, 128), F32), V((256, ROWS), BF), V((128, ROWS), BF), V((128, 256), BF), V((2, 128, 128), BF),
            V((128, ROWS), F32), V((128, ROWS), F32),
            V((NZ, BLK, 1), F32), V((NZ, BLK, 256), F32), V((NZ, BLK, 128), BF), V((NZ, BLK, 128), BF),
            V((NZ, 2, 128, 256), BF), V((NZ, 128, 256), F32), V((128, 256), F32), V((128, 256), F32),
            V((8, 128), F32),
            V((NX, 32, 128), F32), V((NX, 32, 128), F32), V((NX, NZ, 32, 128), BF),
            V((NX, 8, 128), F32), V((NZ, 8, 128), F32), V((8, 8, 128), F32),
            D((3,)), D((6, NZ)), D((6, NZ)), D((2, NZ)), D((2, NZ)), D((2, NZ)), D((2, NZ)),
            D((2, NZ)), D((2, NZ)), D((NX,)), D((NX,)), D((3, NX)), D((3, NX)), D((8,)), D((8,)),
            D((2, NZ)), D((2, NZ))],
        compiler_params=pltpu.CompilerParams(
            collective_id=0, has_side_effects=True, vmem_limit_bytes=60 << 20),
    )(q, k, v, docs, fm)


def body(queries, keys, values, documents, feature_map):
    norm = 1.0 / (TOKENS * 64)
    ta, ya, wa, la = whole(norm, queries, keys, values, documents.reshape(1, BLK), feature_map)
    return (ta, ya, la.reshape(()), wa.reshape(NZ, 128, 128))


def solution(mesh):
    split = Mesh(
        mesh.devices.reshape(mesh.shape["grp"], 8, 4, mesh.shape["head"]),
        ("grp", "seq_0", "seq_1", "head"),
    )
    return jax.shard_map(
        body,
        mesh=split,
        in_specs=(
            P(SEQ, ("grp", "head"), None),
            P(SEQ, ("grp", "head"), None),
            P(SEQ, ("grp", "head"), None),
            P(SEQ),
            P(("grp", "head"), None, None),
        ),
        out_specs=(
            P(SEQ, ("grp", "head"), None),
            P(SEQ, ("grp", "head"), None),
            P(),
            P(("grp", "head"), None, None),
        ),
        check_vma=False,
    )
```

```python
import functools
import math

import jax
import jax.numpy as jnp
from jax import lax
from jax.experimental import pallas as pl
from jax.experimental.pallas import tpu as pltpu
from jax.sharding import Mesh
from jax.sharding import PartitionSpec as P

SEQ = ("seq_0", "seq_1")
MESH = pl.DeviceIdType.MESH

TOKENS, BLK, WINDOW, LOC, GRP, HALF = 6144, 192, 64, 384, 768, 64
NZ, NX = 8, 4
FRONT = 896
ROWS = FRONT + TOKENS + 128
F32, BF = jnp.float32, jnp.bfloat16
NEG = -1e30
SCALE = 128**-0.5
LOG2E = math.log2(math.e)
C2 = SCALE * LOG2E


def mm(a, b, ca=1, cb=0):
    return lax.dot_general(a, b, (((ca,), (cb,)), ((), ())), preferred_element_type=F32)


def hilo(a):
    hi = a.astype(BF)
    return hi, (a - hi.astype(F32)).astype(BF)


def rcopy(src, dst, ssem, rsem, **where):
    return pltpu.make_async_remote_copy(
        src_ref=src, dst_ref=dst, send_sem=ssem, recv_sem=rsem,
        device_id=where, device_id_type=MESH)


def nth(j):
    odd = lax.rem(j, 2)
    return lax.rem(odd * ((j + 1) // 2) + (1 - odd) * (NZ - j // 2), NZ)


def with_ones(v):
    return jnp.concatenate([v, jnp.ones_like(v)], axis=1)


def iota(shape, dim):
    return lax.broadcasted_iota(jnp.int32, shape, dim).astype(F32)


def kernel(norm, q_ref, k_ref, v_ref, doc_ref, fm_ref, ta, ya, wout, lout,
           flat, out3, tr, qa, ka, va, ca, qe, kT, vT, wq2, wk2, pkT, dpT, ms, accs, tb, yb, sts, dss, run, dwq, pls,
           dwb, wx, wg, lx, lz, lc,
           own, zs, zr, rs, rr, ls_, lr, ys, yr, cs, cr, xs, xr, gs, gr, os, orr):
    z, x = lax.axis_index("seq_0"), lax.axis_index("seq_1")
    h, g = lax.axis_index("head"), lax.axis_index("grp")
    right, left, far = lax.rem(x + 1, NX), lax.rem(x + 3, NX), lax.rem(x + 2, NX)
    cols = [{"grp": lax.rem(g + (d // NX), 2), "head": lax.rem(h + d % NX, NX)} for d in range(1, 8)]

    everyone = ([{"seq_0": lax.rem(z + d, NZ)} for d in range(1, NZ)]
                + [{"seq_1": lax.rem(x + d, NX)} for d in range(1, NX)] + cols)
    barrier = pltpu.get_barrier_semaphore()
    for peer in everyone:
        pl.semaphore_signal(barrier, inc=1, device_id=peer, device_id_type=MESH)

    for i, ref in enumerate((k_ref, v_ref, q_ref)):
        flat[...] = ref[...].astype(F32).reshape(BLK * NZ, 128)
        for d in range(NZ):
            out3[i, d] = flat[pl.ds(d, BLK, stride=NZ), :].astype(BF)

    docs = doc_ref[...]
    row = lax.broadcasted_iota(jnp.int32, (8, 128), 0)
    tile = jnp.zeros((8, 128), F32)
    for d in (1, 2, 3):
        n = jnp.sum((docs < d).astype(F32), axis=1, keepdims=True)
        tile = tile + jnp.where(row == d, jnp.broadcast_to(n, (8, 128)), 0.0)
    ca[x, z] = tile
    zero = jnp.zeros((FRONT, 128), BF)
    for ref in (ka, va):
        ref[:FRONT] = zero
        ref[FRONT + TOKENS:] = zero[:128]
    vT[:, :FRONT] = jnp.zeros((128, FRONT), BF)
    vT[:, FRONT + TOKENS:] = jnp.zeros((128, 128), BF)
    dpT[...] = jnp.zeros_like(dpT)
    kT[144:] = jnp.zeros((112, ROWS), BF)
    pkT[:, :FRONT] = jnp.zeros((128, FRONT), F32)
    pkT[:, FRONT + TOKENS:] = jnp.zeros((128, 128), F32)
    w = fm_ref[z]
    wqh, wql = hilo(jnp.concatenate([w[:, :HALF], -w[:, :HALF]], axis=1) * LOG2E)
    wq2[...] = jnp.concatenate([wqh, wql], axis=1)
    wkh, wkl = hilo(jnp.concatenate([w[:, HALF:], -w[:, HALF:]], axis=1).T * LOG2E)
    wk2[0] = wkh
    wk2[1] = wkl

    pl.semaphore_wait(barrier, len(everyone))

    def krows(arr, s, col):
        return arr.at[pl.ds(pl.multiple_of(FRONT + GRP * s + BLK * col, 64), BLK)]

    def zcopy(i, t):
        src = out3.at[i, t]
        dst = qa.at[z] if i == 2 else krows((ka, va)[i], z, x)
        return rcopy(src, dst, zs.at[i, t], zr.at[i, z], seq_0=t)

    def zarrive(i, s):
        dst = qa.at[s] if i == 2 else krows((ka, va)[i], s, x)
        rcopy(dst, dst, zs.at[i, s], zr.at[i, s], seq_0=s).wait_recv()

    def count_copy(t):
        return rcopy(ca.at[x, z], ca.at[x, z], zs.at[3, t], zr.at[3, z], seq_0=t)

    def xcopy(i, s, col, to, sems, semr):
        ref = krows((ka, va)[i], s, col)
        return rcopy(ref, ref, sems.at[i, s], semr.at[i, s], seq_1=to)

    local = [pltpu.make_async_copy(out3.at[0, z], krows(ka, z, x), own.at[0]),
             pltpu.make_async_copy(out3.at[1, z], krows(va, z, x), own.at[1]),
             pltpu.make_async_copy(out3.at[2, z], qa.at[z], own.at[2])]
    for c in local:
        c.start()
    for j in range(1, NZ):
        count_copy(lax.rem(z + nth(j), NZ)).start()

    def target(j):
        return lax.rem(z + NZ - nth(j), NZ)

    def send_all(j, _):
        zcopy(0, target(j)).start()
        zcopy(1, target(j)).start()

        @pl.when(j > 1)
        def _():
            zcopy(2, target(j - 1)).start()
        return 0
    lax.fori_loop(1, NZ, send_all, 0)
    zcopy(2, target(NZ - 1)).start()
    for c in local:
        c.wait()

    def forward(s):
        for i in range(2):
            xcopy(i, s, x, right, rs, rr).start()
            xcopy(i, s, x, left, ls_, lr).start()

    def relay(s):
        xcopy(0, s, left, right, rs, rr).wait_recv()
        xcopy(0, s, left, right, ys, yr).start()
        xcopy(1, s, right, left, ls_, lr).wait_recv()
        xcopy(1, s, right, left, ys, yr).start()

    def complete(s):
        xcopy(1, s, left, right, rs, rr).wait_recv()
        xcopy(0, s, right, left, ls_, lr).wait_recv()
        xcopy(0, s, far, right, ys, yr).wait_recv()
        xcopy(1, s, far, left, ys, yr).wait_recv()

    def nearby(n):
        return lax.rem(z + nth(n), NZ)

    forward(z)
    for n in (1, 2):
        zarrive(0, nearby(n))
        zarrive(1, nearby(n))
        forward(nearby(n))
        relay(nearby(n - 1))
        if n == 1:
            for j in range(1, NZ):
                s = lax.rem(z + j, NZ)
                rcopy(ca.at[x, s], ca.at[x, s], zs.at[3, s], zr.at[3, s], seq_0=s).wait_recv()
            for d in range(1, NX):
                t = lax.rem(x + d, NX)
                rcopy(ca.at[x], ca.at[x], cs.at[t], cr.at[x], seq_1=t).start()
    for d in range(1, NX):
        s = lax.rem(x + d, NX)
        rcopy(ca.at[s], ca.at[s], cs.at[s], cr.at[s], seq_1=s).wait_recv()
    for d in range(1, NX):
        t = lax.rem(x + d, NX)
        rcopy(ca.at[x], ca.at[x], cs.at[t], cr.at[x], seq_1=t).wait_send()
    tally = jnp.zeros((8, 128), F32)
    for i in range(NX):
        for j in range(NZ):
            tally = tally + ca[i, j]
    st1, st2, st3 = tally[1:2, :1], tally[2:3, :1], tally[3:4, :1]
    lane = lax.broadcasted_iota(jnp.int32, (1, 128), 1)
    full = lambda d: tally[d:d + 1, :]
    low = jnp.where(lane == 0, 0.0, jnp.where(lane == 1, full(1), jnp.where(
        lane == 2, full(2), jnp.where(lane == 3, full(3), 1e9))))
    high = jnp.where(lane == 0, full(1), jnp.where(lane == 1, full(2), jnp.where(
        lane == 2, full(3), 1e9)))

    sub = lax.broadcasted_iota(jnp.int32, (16, 1), 0)
    low_col = jnp.where(sub == 0, 0.0, jnp.where(sub == 1, st1, jnp.where(
        sub == 2, st2, jnp.where(sub == 3, st3, 1e9))))
    high_col = jnp.where(sub == 0, st1, jnp.where(sub == 1, st2, jnp.where(sub == 2, st3, 1e9)))

    def dstart(i):
        return jnp.where(i >= st3, st3, jnp.where(i >= st2, st2, jnp.where(i >= st1, st1, 0.0)))

    def qpos(s):
        return (GRP * s + BLK * x).astype(F32) + iota((BLK, 1), 0)

    def absorb(n):
        a = nearby(n)
        o = pl.multiple_of(FRONT + GRP * a, 128)
        kk = ka[pl.ds(o, GRP), :].T
        kT[:128, pl.ds(o, GRP)] = kk
        vT[:, pl.ds(o, GRP)] = va[pl.ds(o, GRP), :].T
        l = mm(wk2[0], kk) + mm(wk2[1], kk)
        for f in (0, HALF):
            lh = l[f:f + HALF]
            e = jnp.exp2(lh - jnp.max(lh, axis=0, keepdims=True))
            pkT[f:f + HALF, pl.ds(o, GRP)] = e * (1.0 / jnp.sum(e, axis=0, keepdims=True))
        kpos = (GRP * a).astype(F32) + iota((1, GRP), 1)
        kT[128:144, pl.ds(o, GRP)] = jnp.where((kpos >= low_col) & (kpos < high_col), 1.0, 0.0).astype(BF)
        icol = qpos(a)
        miss = jnp.logical_not((icol >= low) & (icol < high)) & (lane < 4)
        qe[a] = jnp.where(miss, NEG, 0.0).astype(BF)
        jrow = (GRP * a).astype(F32) + iota((1, GRP), 1)
        s = mm(qa[a], kk)
        s = jnp.where((jrow <= icol) & (jrow >= dstart(icol)), s, NEG)
        m = jnp.max(s, axis=1, keepdims=True)
        p = jnp.exp2((s - m) * C2)
        ms[a] = m
        accs[a] = mm(p.astype(BF), with_ones(va[pl.ds(o, GRP), :]))

        def place(j):
            b = nearby(j)
            ge = (a - b + NZ) // NZ
            zq, zk = ge * a + (1 - ge) * b, ge * b + (1 - ge) * a
            return zq, pl.ds(pl.multiple_of(FRONT + GRP * zk, 128), GRP)

        def pairs(spots):
            scs = [mm(jnp.concatenate([qa[zq], qe[zq]], axis=1),
                      kT[:, r]) for zq, r in spots]
            tops = [jnp.max(sc, axis=1, keepdims=True) for sc in scs]
            olds, news = [], []
            for (zq, _), top in zip(spots, tops):
                olds.append(ms[zq])
                news.append(jnp.maximum(olds[-1], top))
                ms[zq] = news[-1]
            sums = [mm(jnp.exp2((sc - mn) * C2).astype(BF), with_ones(va[r, :]))
                    for sc, mn, (_, r) in zip(scs, news, spots)]
            for (zq, _), mo, mn, add in zip(spots, olds, news, sums):
                accs[zq] = accs[zq] * jnp.exp2((mo - mn) * C2) + add

        @pl.when(lax.rem(n, 2) == 1)
        def _():
            pairs([place(n - 1)])

        @pl.when(lax.rem(n, 4) > 1)
        def _():
            pairs([place(n // 4 * 4), place(n // 4 * 4 + 1)])

        def four(j, _):
            pairs([place(4 * j + i) for i in range(4)])
            return 0
        lax.fori_loop(0, n // 4, four, 0)

    def step(n, _):
        complete(nearby(n - 2))
        absorb(n - 2)
        s = nearby(n + 1)
        zarrive(0, s)
        zarrive(1, s)
        forward(s)
        relay(nearby(n))
        zarrive(2, nearby(n - 1))
        return 0
    lax.fori_loop(2, NZ - 1, step, 0)

    def late(n, _):
        @pl.when(n > NZ - 3)
        def _():
            zarrive(2, nearby(n))
        complete(nearby(n))
        absorb(n)

        @pl.when(n == NZ - 3)
        def _():
            relay(nearby(NZ - 1))
        return 0
    lax.fori_loop(NZ - 3, NZ, late, 0)

    off = BLK * x + 64 * lax.rem(x, 2)
    run[...] = jnp.zeros_like(run)

    def local_row(s):
        return pl.multiple_of(GRP * s + off + GRP, 128)

    def group_mask(s):
        end = (GRP * s + off + GRP - FRONT).astype(F32)
        jg = end - GRP + iota((1, GRP), 1)
        tag = dstart(jnp.zeros((1, 1), F32) + (end - 1.0))
        return (jg >= tag) & (jg < end) & (jg >= 0.0), tag, end

    def states(s, _):
        r = local_row(s)
        mask, tag, end = group_mask(s)
        o = pl.multiple_of(r - GRP, 128)
        pg = jnp.where(mask, pkT[:, pl.ds(o, GRP)], 0.0).astype(BF)
        keep = jnp.where(tag < end - GRP, 1.0, 0.0)
        st = run[...] * keep + mm(pg, with_ones(va[pl.ds(o, GRP), :]))
        run[...] = st
        hi, lo = hilo(st)
        sts[s, 0] = hi
        sts[s, 1] = lo
        tb[s] = (accs[s][:, :128] / accs[s][:, 128:]).astype(BF)
        return 0
    lax.fori_loop(0, NZ, states, 0)

    dwq[...] = jnp.zeros_like(dwq)
    pls[...] = jnp.zeros_like(pls)

    def send_out(i, t):
        return rcopy((tb, yb)[i].at[t], tr.at[i, z], os.at[i, t], orr.at[i, z], seq_0=t)

    def block(n, _):
        s = lax.rem(z + nth(NZ - 1 - n), NZ)

        @pl.when(n < NZ - 1)
        def _():
            send_out(0, s).start()

        @pl.when(n > 0)
        def _():
            send_out(1, lax.rem(z + nth(NZ - n), NZ)).start()
        r = local_row(s)
        q = qa[s]
        kl = ka[pl.ds(r, LOC), :]
        vl = with_ones(va[pl.ds(r, LOC), :])
        icol = qpos(s)
        dcol = dstart(icol)
        jrow = (GRP * s + off + GRP - FRONT).astype(F32) + iota((1, LOC), 1)
        same = jrow >= dcol
        sc = mm(q, kl, 1, 1)
        lq = mm(q, wq2[...])
        lq = lq[:, :128] + lq[:, 128:]
        ph = []
        for f in (0, HALF):
            lh = lq[:, f:f + HALF]
            e = jnp.exp2(lh - jnp.max(lh, axis=1, keepdims=True))
            ph.append(e * (1.0 / jnp.sum(e, axis=1, keepdims=True)))
        pq = jnp.concatenate(ph, axis=1)
        pq_h, pq_l = hilo(pq)
        _, tag, end = group_mask(s)
        uses = jnp.where((dcol == tag) & (end > 0.0), 1.0, 0.0)
        sh, sl = sts[s, 0], sts[s, 1]
        sth = mm(pq_h, sh) + mm(pq_l, sh) + mm(pq_h, sl)
        swm = jnp.where(same & (jrow <= icol) & (jrow > icol - WINDOW), sc, NEG)
        a = jnp.exp2((swm - jnp.max(swm, axis=1, keepdims=True)) * C2)
        bey = same & (jrow <= icol - WINDOW)
        pl_T = pkT[:, pl.ds(r, LOC)].astype(BF)
        bb = jnp.where(bey, mm(pq_h, pl_T), 0.0)
        nd = mm((a + bb).astype(BF), vl) + uses * sth
        rden = 1.0 / nd[:, 128:]
        y = nd[:, :128] * rden
        yb[s] = y.astype(BF)
        e = y - tb[s].astype(F32)
        pls[...] += jnp.sum((e * e).reshape(BLK // 8, 8, 128), axis=0)
        gr_ = e * rden * (2.0 * norm)
        gx = jnp.concatenate([gr_, -gr_ * y], axis=1)
        gh, _ = hilo(gx)
        db = jnp.where(bey, mm(gh, vl, 1, 1), 0.0).astype(BF)
        guh, gul = hilo(gx * uses)
        dpq = mm(db, pl_T, 1, 1) + mm(guh, sh, 1, 1) + mm(gul, sh, 1, 1) + mm(guh, sl, 1, 1)
        dpT[:, pl.ds(r, LOC)] += mm(pq_h, db, 0, 0)
        dss[s] = mm(pq_h, guh, 0, 0)
        out = []
        for f in (0, HALF):
            pp, dd = pq[:, f:f + HALF], dpq[:, f:f + HALF]
            out.append(pp * (dd - jnp.sum(pp * dd, axis=1, keepdims=True)))
        dh, dlo = hilo(jnp.concatenate(out, axis=1))
        dwq[...] += mm(q, jnp.concatenate([dh, dlo], axis=1), 0, 0)
        return 0
    lax.fori_loop(0, NZ, block, 0)

    def lscatter(t):
        return rcopy(lx.at[x], lx.at[x], xs.at[1, t], xr.at[1, x], seq_1=t)

    def lspread(s, t):
        return rcopy(lz.at[s], lz.at[s], zs.at[5, t], zr.at[5, s], seq_0=t)
    lx[x] = pls[...] * norm
    for d in range(1, NX):
        lscatter(lax.rem(x + d, NX)).start()

    run[...] = jnp.zeros_like(run)

    def back(n, _):
        s = NZ - 1 - n
        o = pl.multiple_of(local_row(s) - GRP, 128)
        mask, tag, end = group_mask(s)
        keep = jnp.where(dstart(jnp.zeros((1, 1), F32) + (end + GRP - 1.0)) == tag, 1.0, 0.0)
        rr_ = run[...] * keep + dss[s]
        run[...] = rr_
        d = mm(rr_.astype(BF), jnp.concatenate([vT[:, pl.ds(o, GRP)], jnp.ones((128, GRP), BF)], axis=0))
        dpT[:, pl.ds(o, GRP)] += jnp.where(mask, d, 0.0)
        return 0
    lax.fori_loop(0, NZ, back, 0)
    for d in range(1, NX):
        s = lax.rem(x + d, NX)
        rcopy(lx.at[s], lx.at[s], xs.at[1, s], xr.at[1, s], seq_1=s).wait_recv()
    lz[z] = (lx[0] + lx[1]) + (lx[2] + lx[3])
    for j in range(1, NZ):
        lspread(z, lax.rem(z + nth(j), NZ)).start()

    def fin(s, acc):
        o = pl.multiple_of(FRONT + GRP * s, 128)
        out = []
        for f in (0, HALF):
            pp, dd = pkT[f:f + HALF, pl.ds(o, GRP)], dpT[f:f + HALF, pl.ds(o, GRP)]
            out.append(pp * (dd - jnp.sum(pp * dd, axis=0, keepdims=True)))
        dh, dlo = hilo(jnp.concatenate(out, axis=0))
        kk = ka[pl.ds(o, GRP), :]
        return acc + mm(dh, kk) + mm(dlo, kk)
    dk = lax.fori_loop(0, NZ, fin, jnp.zeros((128, 128), F32)).T
    dq = dwq[:, :128] + dwq[:, 128:]
    dw = jnp.concatenate([dq[:, :HALF] - dq[:, HALF:], dk[:, :HALF] - dk[:, HALF:]], axis=1)
    dwb[...] = dw.reshape(NX, 32, 128)

    def scatter(t):
        return rcopy(dwb.at[t], wx.at[x], xs.at[0, t], xr.at[0, x], seq_1=t)

    def zspread(s, t):
        return rcopy(wg.at[x, s], wg.at[x, s], zs.at[4, t], zr.at[4, s], seq_0=t)
    for d in range(1, NX):
        scatter(lax.rem(x + d, NX)).start()
    wx[x] = dwb[x]
    for d in range(1, NX):
        s = lax.rem(x + d, NX)
        rcopy(wx.at[s], wx.at[s], xs.at[0, s], xr.at[0, s], seq_1=s).wait_recv()
    wg[x, z] = ((wx[0] + wx[1]) + (wx[2] + wx[3])).astype(BF)
    for j in range(1, NZ):
        zspread(z, lax.rem(z + nth(j), NZ)).start()
    for j in range(1, NZ):
        s = lax.rem(z + j, NZ)
        lspread(s, s).wait_recv()
    part = lz[0]
    for i in range(1, NZ):
        part = part + lz[i]
    mine = NX * g + h
    lc[mine] = part
    for peer in cols:
        there = NX * peer["grp"] + peer["head"]
        rcopy(lc.at[mine], lc.at[mine], gs.at[there], gr.at[mine], **peer).start()

    def land(i, src, dst):
        for j in range(1, NZ):
            s = lax.rem(z + j, NZ)
            rcopy(tr.at[i, s], tr.at[i, s], os.at[i, s], orr.at[i, s], seq_0=s).wait_recv()
        tr[i, z] = src[z]
        for d in range(NZ):
            flat[pl.ds(d, BLK, stride=NZ), :] = tr[i, d].astype(F32)
        dst[...] = flat[...].reshape(BLK, NZ, 128).astype(BF)
    land(0, tb, ta)
    for j in range(1, NZ):
        s = lax.rem(z + j, NZ)
        zspread(s, s).wait_recv()
    for d in range(1, NX):
        t = lax.rem(x + d, NX)
        rcopy(wg.at[x], wg.at[x], xs.at[2, t], xr.at[2, x], seq_1=t).start()
    land(1, yb, ya)
    for peer in cols:
        there = NX * peer["grp"] + peer["head"]
        rcopy(lc.at[there], lc.at[there], gs.at[there], gr.at[there], **peer).wait_recv()
    part = lc[0]
    for i in range(1, 8):
        part = part + lc[i]
    lout[...] = jnp.sum(jnp.sum(part, axis=0, keepdims=True), axis=1, keepdims=True)
    for d in range(1, NX):
        s = lax.rem(x + d, NX)
        rcopy(wg.at[s], wg.at[s], xs.at[2, s], xr.at[2, s], seq_1=s).wait_recv()
    for i in range(NX):
        wout[:, i] = wg[i].astype(F32)

    def drain(j, _):
        s = lax.rem(z + j, NZ)
        for i in range(2):
            send_out(i, s).wait_send()
        for i in range(3):
            zcopy(i, s).wait_send()
        count_copy(s).wait_send()
        zspread(z, s).wait_send()
        lspread(z, s).wait_send()
        return 0
    lax.fori_loop(1, NZ, drain, 0)

    def drain_x(s, _):
        for i in range(2):
            xcopy(i, s, x, right, rs, rr).wait_send()
            xcopy(i, s, x, left, ls_, lr).wait_send()
        xcopy(0, s, left, right, ys, yr).wait_send()
        xcopy(1, s, right, left, ys, yr).wait_send()
        return 0
    lax.fori_loop(0, NZ, drain_x, 0)
    for d in range(1, NX):
        t = lax.rem(x + d, NX)
        scatter(t).wait_send()
        lscatter(t).wait_send()
        rcopy(wg.at[x], wg.at[x], xs.at[2, t], xr.at[2, x], seq_1=t).wait_send()
    for peer in cols:
        there = NX * peer["grp"] + peer["head"]
        rcopy(lc.at[mine], lc.at[mine], gs.at[there], gr.at[mine], **peer).wait_send()


def whole(norm, q, k, v, docs, fm):
    M = pl.BlockSpec(memory_space=pltpu.VMEM)
    D, V = pltpu.SemaphoreType.DMA, pltpu.VMEM
    return pl.pallas_call(
        functools.partial(kernel, norm),
        out_shape=(V((BLK, NZ, 128), BF), V((BLK, NZ, 128), BF), V((NZ, NX, 32, 128), F32),
                   jax.ShapeDtypeStruct((1, 1), F32)),
        in_specs=[M] * 5, out_specs=(M,) * 4,
        scratch_shapes=[
            V((BLK * NZ, 128), F32), V((3, NZ, BLK, 128), BF), V((2, NZ, BLK, 128), BF),
            V((NZ, BLK, 128), BF), V((ROWS, 128), BF), V((ROWS, 128), BF), V((NX, NZ, 8, 128), F32),
            V((NZ, BLK, 128), BF), V((256, ROWS), BF), V((128, ROWS), BF), V((128, 256), BF), V((2, 128, 128), BF),
            V((128, ROWS), F32), V((128, ROWS), F32),
            V((NZ, BLK, 1), F32), V((NZ, BLK, 256), F32), V((NZ, BLK, 128), BF), V((NZ, BLK, 128), BF),
            V((NZ, 2, 128, 256), BF), V((NZ, 128, 256), F32), V((128, 256), F32), V((128, 256), F32),
            V((8, 128), F32),
            V((NX, 32, 128), F32), V((NX, 32, 128), F32), V((NX, NZ, 32, 128), BF),
            V((NX, 8, 128), F32), V((NZ, 8, 128), F32), V((8, 8, 128), F32),
            D((3,)), D((6, NZ)), D((6, NZ)), D((2, NZ)), D((2, NZ)), D((2, NZ)), D((2, NZ)),
            D((2, NZ)), D((2, NZ)), D((NX,)), D((NX,)), D((3, NX)), D((3, NX)), D((8,)), D((8,)),
            D((2, NZ)), D((2, NZ))],
        compiler_params=pltpu.CompilerParams(
            collective_id=0, has_side_effects=True, vmem_limit_bytes=60 << 20),
    )(q, k, v, docs, fm)


def body(queries, keys, values, documents, feature_map):
    norm = 1.0 / (TOKENS * 64)
    ta, ya, wa, la = whole(norm, queries, keys, values, documents.reshape(1, BLK), feature_map)
    return (ta, ya, la.reshape(()), wa.reshape(NZ, 128, 128))


def solution(mesh):
    split = Mesh(
        mesh.devices.reshape(mesh.shape["grp"], 8, 4, mesh.shape["head"]),
        ("grp", "seq_0", "seq_1", "head"),
    )
    return jax.shard_map(
        body,
        mesh=split,
        in_specs=(
            P(SEQ, ("grp", "head"), None),
            P(SEQ, ("grp", "head"), None),
            P(SEQ, ("grp", "head"), None),
            P(SEQ),
            P(("grp", "head"), None, None),
        ),
        out_specs=(
            P(SEQ, ("grp", "head"), None),
            P(SEQ, ("grp", "head"), None),
            P(),
            P(("grp", "head"), None, None),
        ),
        check_vma=False,
    )
```

```python
import functools
import math

import jax
import jax.numpy as jnp
from jax import lax
from jax.experimental import pallas as pl
from jax.experimental.pallas import tpu as pltpu
from jax.sharding import Mesh
from jax.sharding import PartitionSpec as P

SEQ = ("seq_0", "seq_1")
MESH = pl.DeviceIdType.MESH

TOKENS, BLK, WINDOW, LOC, GRP, HALF = 6144, 192, 64, 384, 768, 64
NZ, NX = 8, 4
FRONT = 896
ROWS = FRONT + TOKENS + 128
F32, BF = jnp.float32, jnp.bfloat16
NEG = -1e30
SCALE = 128**-0.5
LOG2E = math.log2(math.e)
C2 = SCALE * LOG2E


def mm(a, b, ca=1, cb=0):
    return lax.dot_general(a, b, (((ca,), (cb,)), ((), ())), preferred_element_type=F32)


def hilo(a):
    hi = a.astype(BF)
    return hi, (a - hi.astype(F32)).astype(BF)


def rcopy(src, dst, ssem, rsem, **where):
    return pltpu.make_async_remote_copy(
        src_ref=src, dst_ref=dst, send_sem=ssem, recv_sem=rsem,
        device_id=where, device_id_type=MESH)


def nth(j):
    odd = lax.rem(j, 2)
    return lax.rem(odd * ((j + 1) // 2) + (1 - odd) * (NZ - j // 2), NZ)


def with_ones(v):
    return jnp.concatenate([v, jnp.ones_like(v)], axis=1)


def iota(shape, dim):
    return lax.broadcasted_iota(jnp.int32, shape, dim).astype(F32)


def kernel(norm, q_ref, k_ref, v_ref, doc_ref, fm_ref, ta, ya, wout, lout,
           flat, out3, tr, qa, ka, va, ca, qe, kT, vT, wq2, wk2, pkT, dpT, ms, accs, tb, yb, sts, dss, run, dwq, pls,
           dwb, wx, wg, lx, lz, lc,
           own, zs, zr, rs, rr, ls_, lr, ys, yr, cs, cr, xs, xr, gs, gr, os, orr, ws, wr):
    z, x = lax.axis_index("seq_0"), lax.axis_index("seq_1")
    h, g = lax.axis_index("head"), lax.axis_index("grp")
    right, left, far = lax.rem(x + 1, NX), lax.rem(x + 3, NX), lax.rem(x + 2, NX)
    cols = [{"grp": lax.rem(g + (d // NX), 2), "head": lax.rem(h + d % NX, NX)} for d in range(1, 8)]

    everyone = ([{"seq_0": lax.rem(z + d, NZ)} for d in range(1, NZ)]
                + [{"seq_1": lax.rem(x + d, NX)} for d in range(1, NX)] + cols)
    barrier = pltpu.get_barrier_semaphore()
    for peer in everyone:
        pl.semaphore_signal(barrier, inc=1, device_id=peer, device_id_type=MESH)

    for i, ref in enumerate((k_ref, v_ref, q_ref)):
        flat[...] = ref[...].astype(F32).reshape(BLK * NZ, 128)
        for d in range(NZ):
            out3[i, d] = flat[pl.ds(d, BLK, stride=NZ), :].astype(BF)

    docs = doc_ref[...]
    row = lax.broadcasted_iota(jnp.int32, (8, 128), 0)
    tile = jnp.zeros((8, 128), F32)
    for d in (1, 2, 3):
        n = jnp.sum((docs < d).astype(F32), axis=1, keepdims=True)
        tile = tile + jnp.where(row == d, jnp.broadcast_to(n, (8, 128)), 0.0)
    ca[x, z] = tile
    zero = jnp.zeros((FRONT, 128), BF)
    for ref in (ka, va):
        ref[:FRONT] = zero
        ref[FRONT + TOKENS:] = zero[:128]
    vT[:, :FRONT] = jnp.zeros((128, FRONT), BF)
    vT[:, FRONT + TOKENS:] = jnp.zeros((128, 128), BF)
    dpT[...] = jnp.zeros_like(dpT)
    kT[144:] = jnp.zeros((112, ROWS), BF)
    pkT[:, :FRONT] = jnp.zeros((128, FRONT), F32)
    pkT[:, FRONT + TOKENS:] = jnp.zeros((128, 128), F32)
    w = fm_ref[z]
    wqh, wql = hilo(jnp.concatenate([w[:, :HALF], -w[:, :HALF]], axis=1) * LOG2E)
    wq2[...] = jnp.concatenate([wqh, wql], axis=1)
    wkh, wkl = hilo(jnp.concatenate([w[:, HALF:], -w[:, HALF:]], axis=1).T * LOG2E)
    wk2[0] = wkh
    wk2[1] = wkl

    pl.semaphore_wait(barrier, len(everyone))

    def krows(arr, s, col):
        return arr.at[pl.ds(pl.multiple_of(FRONT + GRP * s + BLK * col, 64), BLK)]

    def zcopy(i, t):
        src = out3.at[i, t]
        dst = qa.at[z] if i == 2 else krows((ka, va)[i], z, x)
        return rcopy(src, dst, zs.at[i, t], zr.at[i, z], seq_0=t)

    def zarrive(i, s):
        dst = qa.at[s] if i == 2 else krows((ka, va)[i], s, x)
        rcopy(dst, dst, zs.at[i, s], zr.at[i, s], seq_0=s).wait_recv()

    def count_copy(t):
        return rcopy(ca.at[x, z], ca.at[x, z], zs.at[3, t], zr.at[3, z], seq_0=t)

    def xcopy(i, s, col, to, sems, semr):
        ref = krows((ka, va)[i], s, col)
        return rcopy(ref, ref, sems.at[i, s], semr.at[i, s], seq_1=to)

    local = [pltpu.make_async_copy(out3.at[0, z], krows(ka, z, x), own.at[0]),
             pltpu.make_async_copy(out3.at[1, z], krows(va, z, x), own.at[1]),
             pltpu.make_async_copy(out3.at[2, z], qa.at[z], own.at[2])]
    for c in local:
        c.start()
    for j in range(1, NZ):
        count_copy(lax.rem(z + nth(j), NZ)).start()

    def target(j):
        return lax.rem(z + NZ - nth(j), NZ)

    def send_all(j, _):
        zcopy(0, target(j)).start()
        zcopy(1, target(j)).start()

        @pl.when(j > 1)
        def _():
            zcopy(2, target(j - 1)).start()
        return 0
    lax.fori_loop(1, NZ, send_all, 0)
    zcopy(2, target(NZ - 1)).start()
    for c in local:
        c.wait()

    def forward(s):
        for i in range(2):
            xcopy(i, s, x, right, rs, rr).start()
            xcopy(i, s, x, left, ls_, lr).start()

    def relay(s):
        xcopy(0, s, left, right, rs, rr).wait_recv()
        xcopy(0, s, left, right, ys, yr).start()
        xcopy(1, s, right, left, ls_, lr).wait_recv()
        xcopy(1, s, right, left, ys, yr).start()

    def complete(s):
        xcopy(1, s, left, right, rs, rr).wait_recv()
        xcopy(0, s, right, left, ls_, lr).wait_recv()
        xcopy(0, s, far, right, ys, yr).wait_recv()
        xcopy(1, s, far, left, ys, yr).wait_recv()

    def nearby(n):
        return lax.rem(z + nth(n), NZ)

    forward(z)
    for n in (1, 2):
        zarrive(0, nearby(n))
        zarrive(1, nearby(n))
        forward(nearby(n))
        relay(nearby(n - 1))
        if n == 1:
            for j in range(1, NZ):
                s = lax.rem(z + j, NZ)
                rcopy(ca.at[x, s], ca.at[x, s], zs.at[3, s], zr.at[3, s], seq_0=s).wait_recv()
            for d in range(1, NX):
                t = lax.rem(x + d, NX)
                rcopy(ca.at[x], ca.at[x], cs.at[t], cr.at[x], seq_1=t).start()
    for d in range(1, NX):
        s = lax.rem(x + d, NX)
        rcopy(ca.at[s], ca.at[s], cs.at[s], cr.at[s], seq_1=s).wait_recv()
    for d in range(1, NX):
        t = lax.rem(x + d, NX)
        rcopy(ca.at[x], ca.at[x], cs.at[t], cr.at[x], seq_1=t).wait_send()
    tally = jnp.zeros((8, 128), F32)
    for i in range(NX):
        for j in range(NZ):
            tally = tally + ca[i, j]
    st1, st2, st3 = tally[1:2, :1], tally[2:3, :1], tally[3:4, :1]
    lane = lax.broadcasted_iota(jnp.int32, (1, 128), 1)
    full = lambda d: tally[d:d + 1, :]
    low = jnp.where(lane == 0, 0.0, jnp.where(lane == 1, full(1), jnp.where(
        lane == 2, full(2), jnp.where(lane == 3, full(3), 1e9))))
    high = jnp.where(lane == 0, full(1), jnp.where(lane == 1, full(2), jnp.where(
        lane == 2, full(3), 1e9)))

    sub = lax.broadcasted_iota(jnp.int32, (16, 1), 0)
    low_col = jnp.where(sub == 0, 0.0, jnp.where(sub == 1, st1, jnp.where(
        sub == 2, st2, jnp.where(sub == 3, st3, 1e9))))
    high_col = jnp.where(sub == 0, st1, jnp.where(sub == 1, st2, jnp.where(sub == 2, st3, 1e9)))

    def dstart(i):
        return jnp.where(i >= st3, st3, jnp.where(i >= st2, st2, jnp.where(i >= st1, st1, 0.0)))

    def qpos(s):
        return (GRP * s + BLK * x).astype(F32) + iota((BLK, 1), 0)

    def absorb(n):
        a = nearby(n)
        o = pl.multiple_of(FRONT + GRP * a, 128)
        kk = ka[pl.ds(o, GRP), :].T
        kT[:128, pl.ds(o, GRP)] = kk
        vT[:, pl.ds(o, GRP)] = va[pl.ds(o, GRP), :].T
        l = mm(wk2[0], kk) + mm(wk2[1], kk)
        for f in (0, HALF):
            lh = l[f:f + HALF]
            e = jnp.exp2(lh - jnp.max(lh, axis=0, keepdims=True))
            pkT[f:f + HALF, pl.ds(o, GRP)] = e * (1.0 / jnp.sum(e, axis=0, keepdims=True))
        kpos = (GRP * a).astype(F32) + iota((1, GRP), 1)
        kT[128:144, pl.ds(o, GRP)] = jnp.where((kpos >= low_col) & (kpos < high_col), 1.0, 0.0).astype(BF)
        icol = qpos(a)
        miss = jnp.logical_not((icol >= low) & (icol < high)) & (lane < 4)
        qe[a] = jnp.where(miss, NEG, 0.0).astype(BF)
        jrow = (GRP * a).astype(F32) + iota((1, GRP), 1)
        s = mm(qa[a], kk)
        s = jnp.where((jrow <= icol) & (jrow >= dstart(icol)), s, NEG)
        m = jnp.max(s, axis=1, keepdims=True)
        p = jnp.exp2((s - m) * C2)
        ms[a] = m
        accs[a] = mm(p.astype(BF), with_ones(va[pl.ds(o, GRP), :]))

        def place(j):
            b = nearby(j)
            ge = (a - b + NZ) // NZ
            zq, zk = ge * a + (1 - ge) * b, ge * b + (1 - ge) * a
            return zq, pl.ds(pl.multiple_of(FRONT + GRP * zk, 128), GRP)

        def pairs(spots):
            scs = [mm(jnp.concatenate([qa[zq], qe[zq]], axis=1),
                      kT[:, r]) for zq, r in spots]
            tops = [jnp.max(sc, axis=1, keepdims=True) for sc in scs]
            olds, news = [], []
            for (zq, _), top in zip(spots, tops):
                olds.append(ms[zq])
                news.append(jnp.maximum(olds[-1], top))
                ms[zq] = news[-1]
            sums = [mm(jnp.exp2((sc - mn) * C2).astype(BF), with_ones(va[r, :]))
                    for sc, mn, (_, r) in zip(scs, news, spots)]
            for (zq, _), mo, mn, add in zip(spots, olds, news, sums):
                accs[zq] = accs[zq] * jnp.exp2((mo - mn) * C2) + add

        @pl.when(lax.rem(n, 2) == 1)
        def _():
            pairs([place(n - 1)])

        @pl.when(lax.rem(n, 4) > 1)
        def _():
            pairs([place(n // 4 * 4), place(n // 4 * 4 + 1)])

        def four(j, _):
            pairs([place(4 * j + i) for i in range(4)])
            return 0
        lax.fori_loop(0, n // 4, four, 0)

    def step(n, _):
        complete(nearby(n - 2))
        absorb(n - 2)
        s = nearby(n + 1)
        zarrive(0, s)
        zarrive(1, s)
        forward(s)
        relay(nearby(n))
        zarrive(2, nearby(n - 1))
        return 0
    lax.fori_loop(2, NZ - 1, step, 0)

    def late(n, _):
        @pl.when(n > NZ - 3)
        def _():
            zarrive(2, nearby(n))
        complete(nearby(n))
        absorb(n)

        @pl.when(n == NZ - 3)
        def _():
            relay(nearby(NZ - 1))
        return 0
    lax.fori_loop(NZ - 3, NZ, late, 0)

    off = BLK * x + 64 * lax.rem(x, 2)
    run[...] = jnp.zeros_like(run)

    def local_row(s):
        return pl.multiple_of(GRP * s + off + GRP, 128)

    def group_mask(s):
        end = (GRP * s + off + GRP - FRONT).astype(F32)
        jg = end - GRP + iota((1, GRP), 1)
        tag = dstart(jnp.zeros((1, 1), F32) + (end - 1.0))
        return (jg >= tag) & (jg < end) & (jg >= 0.0), tag, end

    def states(s, _):
        r = local_row(s)
        mask, tag, end = group_mask(s)
        o = pl.multiple_of(r - GRP, 128)
        pg = jnp.where(mask, pkT[:, pl.ds(o, GRP)], 0.0).astype(BF)
        keep = jnp.where(tag < end - GRP, 1.0, 0.0)
        st = run[...] * keep + mm(pg, with_ones(va[pl.ds(o, GRP), :]))
        run[...] = st
        hi, lo = hilo(st)
        sts[s, 0] = hi
        sts[s, 1] = lo
        tb[s] = (accs[s][:, :128] / accs[s][:, 128:]).astype(BF)
        return 0
    lax.fori_loop(0, NZ, states, 0)

    dwq[...] = jnp.zeros_like(dwq)
    pls[...] = jnp.zeros_like(pls)

    def send_out(i, t):
        return rcopy((tb, yb)[i].at[t], tr.at[i, z], os.at[i, t], orr.at[i, z], seq_0=t)

    def block(n, _):
        s = lax.rem(z + nth(NZ - 1 - n), NZ)

        @pl.when(n < NZ - 1)
        def _():
            send_out(0, s).start()

        @pl.when(n > 0)
        def _():
            send_out(1, lax.rem(z + nth(NZ - n), NZ)).start()
        r = local_row(s)
        q = qa[s]
        kl = ka[pl.ds(r, LOC), :]
        vl = with_ones(va[pl.ds(r, LOC), :])
        icol = qpos(s)
        dcol = dstart(icol)
        jrow = (GRP * s + off + GRP - FRONT).astype(F32) + iota((1, LOC), 1)
        same = jrow >= dcol
        sc = mm(q, kl, 1, 1)
        lq = mm(q, wq2[...])
        lq = lq[:, :128] + lq[:, 128:]
        ph = []
        for f in (0, HALF):
            lh = lq[:, f:f + HALF]
            e = jnp.exp2(lh - jnp.max(lh, axis=1, keepdims=True))
            ph.append(e * (1.0 / jnp.sum(e, axis=1, keepdims=True)))
        pq = jnp.concatenate(ph, axis=1)
        pq_h, pq_l = hilo(pq)
        _, tag, end = group_mask(s)
        uses = jnp.where((dcol == tag) & (end > 0.0), 1.0, 0.0)
        sh, sl = sts[s, 0], sts[s, 1]
        sth = mm(pq_h, sh) + mm(pq_l, sh) + mm(pq_h, sl)
        swm = jnp.where(same & (jrow <= icol) & (jrow > icol - WINDOW), sc, NEG)
        a = jnp.exp2((swm - jnp.max(swm, axis=1, keepdims=True)) * C2)
        bey = same & (jrow <= icol - WINDOW)
        pl_T = pkT[:, pl.ds(r, LOC)].astype(BF)
        bb = jnp.where(bey, mm(pq_h, pl_T), 0.0)
        nd = mm((a + bb).astype(BF), vl) + uses * sth
        rden = 1.0 / nd[:, 128:]
        y = nd[:, :128] * rden
        yb[s] = y.astype(BF)
        e = y - tb[s].astype(F32)
        pls[...] += jnp.sum((e * e).reshape(BLK // 8, 8, 128), axis=0)
        gr_ = e * rden * (2.0 * norm)
        gx = jnp.concatenate([gr_, -gr_ * y], axis=1)
        gh, _ = hilo(gx)
        db = jnp.where(bey, mm(gh, vl, 1, 1), 0.0).astype(BF)
        guh, gul = hilo(gx * uses)
        dpq = mm(db, pl_T, 1, 1) + mm(guh, sh, 1, 1) + mm(gul, sh, 1, 1) + mm(guh, sl, 1, 1)
        dpT[:, pl.ds(r, LOC)] += mm(pq_h, db, 0, 0)
        dss[s] = mm(pq_h, guh, 0, 0)
        out = []
        for f in (0, HALF):
            pp, dd = pq[:, f:f + HALF], dpq[:, f:f + HALF]
            out.append(pp * (dd - jnp.sum(pp * dd, axis=1, keepdims=True)))
        dh, dlo = hilo(jnp.concatenate(out, axis=1))
        dwq[...] += mm(q, jnp.concatenate([dh, dlo], axis=1), 0, 0)
        return 0
    lax.fori_loop(0, NZ, block, 0)

    def lscatter(t):
        return rcopy(lx.at[x], lx.at[x], xs.at[1, t], xr.at[1, x], seq_1=t)

    def lspread(s, t):
        return rcopy(lz.at[s], lz.at[s], zs.at[5, t], zr.at[5, s], seq_0=t)
    lx[x] = pls[...] * norm
    for d in range(1, NX):
        lscatter(lax.rem(x + d, NX)).start()

    run[...] = jnp.zeros_like(run)

    def back(n, _):
        s = NZ - 1 - n
        o = pl.multiple_of(local_row(s) - GRP, 128)
        mask, tag, end = group_mask(s)
        keep = jnp.where(dstart(jnp.zeros((1, 1), F32) + (end + GRP - 1.0)) == tag, 1.0, 0.0)
        rr_ = run[...] * keep + dss[s]
        run[...] = rr_
        d = mm(rr_.astype(BF), jnp.concatenate([vT[:, pl.ds(o, GRP)], jnp.ones((128, GRP), BF)], axis=0))
        dpT[:, pl.ds(o, GRP)] += jnp.where(mask, d, 0.0)
        return 0
    lax.fori_loop(0, NZ, back, 0)
    for d in range(1, NX):
        s = lax.rem(x + d, NX)
        rcopy(lx.at[s], lx.at[s], xs.at[1, s], xr.at[1, s], seq_1=s).wait_recv()
    lz[z] = (lx[0] + lx[1]) + (lx[2] + lx[3])
    for j in range(1, NZ):
        lspread(z, lax.rem(z + nth(j), NZ)).start()

    def fin(s, acc):
        o = pl.multiple_of(FRONT + GRP * s, 128)
        out = []
        for f in (0, HALF):
            pp, dd = pkT[f:f + HALF, pl.ds(o, GRP)], dpT[f:f + HALF, pl.ds(o, GRP)]
            out.append(pp * (dd - jnp.sum(pp * dd, axis=0, keepdims=True)))
        dh, dlo = hilo(jnp.concatenate(out, axis=0))
        kk = ka[pl.ds(o, GRP), :]
        return acc + mm(dh, kk) + mm(dlo, kk)
    dk = lax.fori_loop(0, NZ, fin, jnp.zeros((128, 128), F32)).T
    dq = dwq[:, :128] + dwq[:, 128:]
    dw = jnp.concatenate([dq[:, :HALF] - dq[:, HALF:], dk[:, :HALF] - dk[:, HALF:]], axis=1)
    dwb[...] = dw.reshape(NX, 32, 128)

    def scatter(t):
        return rcopy(dwb.at[t], wx.at[x], xs.at[0, t], xr.at[0, x], seq_1=t)

    def zspread(s, t):
        return rcopy(wg.at[x, s], wg.at[x, s], zs.at[4, t], zr.at[4, s], seq_0=t)
    def onward(s, t):
        return rcopy(wg.at[x, s], wg.at[x, s], ws.at[s, t], wr.at[s, x], seq_1=t)
    for d in range(1, NX):
        scatter(lax.rem(x + d, NX)).start()
    wx[x] = dwb[x]
    for d in range(1, NX):
        s = lax.rem(x + d, NX)
        rcopy(wx.at[s], wx.at[s], xs.at[0, s], xr.at[0, s], seq_1=s).wait_recv()
    wg[x, z] = ((wx[0] + wx[1]) + (wx[2] + wx[3])).astype(BF)
    for j in range(1, NZ):
        zspread(z, lax.rem(z + nth(j), NZ)).start()
    for d in range(1, NX):
        onward(z, lax.rem(x + d, NX)).start()
    for j in range(1, NZ):
        s = lax.rem(z + j, NZ)
        lspread(s, s).wait_recv()
    part = lz[0]
    for i in range(1, NZ):
        part = part + lz[i]
    mine = NX * g + h
    lc[mine] = part
    for peer in cols:
        there = NX * peer["grp"] + peer["head"]
        rcopy(lc.at[mine], lc.at[mine], gs.at[there], gr.at[mine], **peer).start()

    def land(i, src, dst):
        for j in range(1, NZ):
            s = lax.rem(z + j, NZ)
            rcopy(tr.at[i, s], tr.at[i, s], os.at[i, s], orr.at[i, s], seq_0=s).wait_recv()
        tr[i, z] = src[z]
        for d in range(NZ):
            flat[pl.ds(d, BLK, stride=NZ), :] = tr[i, d].astype(F32)
        dst[...] = flat[...].reshape(BLK, NZ, 128).astype(BF)
    land(0, tb, ta)
    for j in range(1, NZ):
        s = lax.rem(z + nth(j), NZ)
        zspread(s, s).wait_recv()
        for d in range(1, NX):
            onward(s, lax.rem(x + d, NX)).start()
    land(1, yb, ya)
    for peer in cols:
        there = NX * peer["grp"] + peer["head"]
        rcopy(lc.at[there], lc.at[there], gs.at[there], gr.at[there], **peer).wait_recv()
    part = lc[0]
    for i in range(1, 8):
        part = part + lc[i]
    lout[...] = jnp.sum(jnp.sum(part, axis=0, keepdims=True), axis=1, keepdims=True)
    for d in range(1, NX):
        s = lax.rem(x + d, NX)
        for j in range(NZ):
            rcopy(wg.at[s, j], wg.at[s, j], ws.at[j, s], wr.at[j, s], seq_1=s).wait_recv()
    for i in range(NX):
        wout[:, i] = wg[i].astype(F32)

    def drain(j, _):
        s = lax.rem(z + j, NZ)
        for i in range(2):
            send_out(i, s).wait_send()
        for i in range(3):
            zcopy(i, s).wait_send()
        count_copy(s).wait_send()
        zspread(z, s).wait_send()
        lspread(z, s).wait_send()
        return 0
    lax.fori_loop(1, NZ, drain, 0)

    def drain_x(s, _):
        for i in range(2):
            xcopy(i, s, x, right, rs, rr).wait_send()
            xcopy(i, s, x, left, ls_, lr).wait_send()
        xcopy(0, s, left, right, ys, yr).wait_send()
        xcopy(1, s, right, left, ys, yr).wait_send()
        return 0
    lax.fori_loop(0, NZ, drain_x, 0)
    for d in range(1, NX):
        t = lax.rem(x + d, NX)
        scatter(t).wait_send()
        lscatter(t).wait_send()
        for j in range(NZ):
            onward(j, t).wait_send()
    for peer in cols:
        there = NX * peer["grp"] + peer["head"]
        rcopy(lc.at[mine], lc.at[mine], gs.at[there], gr.at[mine], **peer).wait_send()


def whole(norm, q, k, v, docs, fm):
    M = pl.BlockSpec(memory_space=pltpu.VMEM)
    D, V = pltpu.SemaphoreType.DMA, pltpu.VMEM
    return pl.pallas_call(
        functools.partial(kernel, norm),
        out_shape=(V((BLK, NZ, 128), BF), V((BLK, NZ, 128), BF), V((NZ, NX, 32, 128), F32),
                   jax.ShapeDtypeStruct((1, 1), F32)),
        in_specs=[M] * 5, out_specs=(M,) * 4,
        scratch_shapes=[
            V((BLK * NZ, 128), F32), V((3, NZ, BLK, 128), BF), V((2, NZ, BLK, 128), BF),
            V((NZ, BLK, 128), BF), V((ROWS, 128), BF), V((ROWS, 128), BF), V((NX, NZ, 8, 128), F32),
            V((NZ, BLK, 128), BF), V((256, ROWS), BF), V((128, ROWS), BF), V((128, 256), BF), V((2, 128, 128), BF),
            V((128, ROWS), F32), V((128, ROWS), F32),
            V((NZ, BLK, 1), F32), V((NZ, BLK, 256), F32), V((NZ, BLK, 128), BF), V((NZ, BLK, 128), BF),
            V((NZ, 2, 128, 256), BF), V((NZ, 128, 256), F32), V((128, 256), F32), V((128, 256), F32),
            V((8, 128), F32),
            V((NX, 32, 128), F32), V((NX, 32, 128), F32), V((NX, NZ, 32, 128), BF),
            V((NX, 8, 128), F32), V((NZ, 8, 128), F32), V((8, 8, 128), F32),
            D((3,)), D((6, NZ)), D((6, NZ)), D((2, NZ)), D((2, NZ)), D((2, NZ)), D((2, NZ)),
            D((2, NZ)), D((2, NZ)), D((NX,)), D((NX,)), D((3, NX)), D((3, NX)), D((8,)), D((8,)),
            D((2, NZ)), D((2, NZ)), D((NZ, NX)), D((NZ, NX))],
        compiler_params=pltpu.CompilerParams(
            collective_id=0, has_side_effects=True, vmem_limit_bytes=60 << 20),
    )(q, k, v, docs, fm)


def body(queries, keys, values, documents, feature_map):
    norm = 1.0 / (TOKENS * 64)
    ta, ya, wa, la = whole(norm, queries, keys, values, documents.reshape(1, BLK), feature_map)
    return (ta, ya, la.reshape(()), wa.reshape(NZ, 128, 128))


def solution(mesh):
    split = Mesh(
        mesh.devices.reshape(mesh.shape["grp"], 8, 4, mesh.shape["head"]),
        ("grp", "seq_0", "seq_1", "head"),
    )
    return jax.shard_map(
        body,
        mesh=split,
        in_specs=(
            P(SEQ, ("grp", "head"), None),
            P(SEQ, ("grp", "head"), None),
            P(SEQ, ("grp", "head"), None),
            P(SEQ),
            P(("grp", "head"), None, None),
        ),
        out_specs=(
            P(SEQ, ("grp", "head"), None),
            P(SEQ, ("grp", "head"), None),
            P(),
            P(("grp", "head"), None, None),
        ),
        check_vma=False,
    )
```
